256 devices in a mesh: order: 8 (over y, core), basin: 32 (over z, x).
Axes of the slice: x: 4, y: 4, z: 8, core: 2. Of those that a mesh axis runs over, the one named last changes fastest.
Arguments:
- forcings: bfloat16 [32, 16, 131072], P(None, None, ('order', 'basin')), may hold values from -6 to 6
- w_input: bfloat16 [512, 16], replicated, may hold values from -1.5 to 1.5
- w_recur: bfloat16 [512, 128], replicated, may hold values from -0.5 to 0.5
- gate_bias: float32 [512], replicated, may hold values from -3 to 3
- w_runoff: float32 [128], replicated, may hold values from -0.5 to 0.5
- travel_time: float32 [131072], P(('order', 'basin')), may hold values from 1 to 8
- weight_x: float32 [131072], P(('order', 'basin')), may hold values from 0 to 0.3
- drain_basin: int32 [131072, 1], P(('order', 'basin')), may hold values from 0 to 31; in each aligned block of 512 rows (0 to 511, 512 to 1023, ...) at most 32 rows name the same one
- drain_reach: int32 [131072, 1], P(('order', 'basin')), may hold values from 0 to 511
Outputs:
- discharge: float32 [32, 131072], P(None, ('order', 'basin'))
The draws below stay inside these ranges and needn't reach their ends.
Inputs may be any that keep to these rules, and one draw needn't show every extreme that they name: `drain_basin`: among the reaches of one device (aligned blocks of 512 reaches), at most 32 drain to the same basin index, and exactly 32 do for some basin index in some block.
All inputs are finite; a program needn't handle non-finite values.
Results may differ from the reference program's by a relative error of at most 0.0003.
Values sent between devices are 32-bit elements; how exact they have to be, the bound alone decides.
A program may use at most 64 MiB of HBM per device.

```python
import math
import jax
import jax.numpy as jnp
import numpy as np
from jax import lax

CHANNELS = 16
UNITS = 128
DAYS = 32
R_DEV = 512
CAP = 32
REACHES = 131072
N_ORDER = 8
N_BASIN = 32


def place_ends(drawn, key, smallest, high):
    longest = drawn.shape.index(max(drawn.shape))
    spots = []
    for shift in (0, 1):
        where = [jax.random.randint(jax.random.fold_in(key, axis), (), 0, length) for axis, length in enumerate(drawn.shape)]
        where[longest] = (where[longest] + shift) % drawn.shape[longest]
        spots.append(tuple(where))
    return drawn.at[spots[0]].set(smallest).at[spots[1]].set(high)


def block_levels(key, dims, cuts, smallest, top_value):
    factor_of = 1.0
    for dim, parts in cuts:
        draws = jax.random.uniform(jax.random.fold_in(jax.random.fold_in(key, 6), dim), (parts,), jnp.float32, smallest / len(cuts), top_value / len(cuts))
        factor_of = factor_of * jnp.repeat(jnp.exp(draws), dims[dim] // parts).reshape((-1,) + (1,) * (len(dims) - 1 - dim))
    return factor_of


def assign_block(stream_key, own, number, rows, amount, top, bound, skew):
    ranking = jax.random.permutation(stream_key, amount)
    heavy_load, ordinary = shares(amount, rows * top, bound, skew, True), shares(amount, rows * top, bound, skew, False)
    places = jnp.arange(amount)

    def named(sizes, offset_by):
        used = int((sizes > 0).sum())
        fixed = max(1, used // 4)
        moved = fixed + (places - fixed + offset_by * (used - fixed)) % max(1, amount - fixed)
        return jnp.zeros((amount,), jnp.int32).at[ranking[jnp.where(places < fixed, places, moved)]].set(jnp.asarray(sizes, jnp.int32))

    sizes = jnp.where(number % 4 == 0, named(heavy_load, number // 4), named(ordinary, number - number // 4 - 1))
    mixed = jax.random.permutation(jax.random.fold_in(own, 3), amount)
    donor, sink = mixed[0:amount // 2 * 2:2], mixed[1:amount // 2 * 2:2]
    room = jnp.minimum(sizes[donor] - 1, bound - sizes[sink]) // 2
    room = jnp.where((donor == ranking[0]) | (sink == ranking[0]) | (sizes[sink] == 0), 0, jnp.maximum(room, 0))
    moved = jax.random.randint(jax.random.fold_in(own, 4), (amount // 2,), 0, 1 << 20) % (room + 1)
    sizes = sizes.at[donor].add(-moved).at[sink].add(moved)
    labels = jnp.searchsorted(jnp.cumsum(sizes), jnp.arange(rows * top), side="right").astype(jnp.int32)
    table = labels.reshape(top, rows).T
    table = table[jax.random.permutation(jax.random.fold_in(own, 1), rows)]
    offset_by = jax.random.randint(jax.random.fold_in(own, 2), (rows, 1), 0, top)
    return jnp.take_along_axis(table, (jnp.arange(top)[None, :] + offset_by) % top, axis=1)


def shares(amount, total, limit, lean, full):
    portions = [(1 << 20) // math.isqrt(grade ** lean) + 1 for grade in range(1, amount + 1)]
    largest = limit if full else min(limit, max(-(-total // amount), total * portions[0] // sum(portions)))
    least = 1 if total - largest >= amount - 1 else 0
    counts, surplus = [largest] + [least] * (amount - 1), total - largest - least * (amount - 1)
    while surplus > 0:
        free = [i for i in range(1, amount) if counts[i] < largest] or [i for i in range(1, amount) if counts[i] < limit]
        pool, remaining = sum([portions[i] for i in free]), surplus
        for i in free:
            more = min(limit - counts[i], max(1, remaining * portions[i] // pool), surplus)
            counts[i] = counts[i] + more
            surplus = surplus - more
    return np.array(counts)


def scatter_about(key, extent, scale, bound, split=(), kind=jnp.bfloat16):
    level = block_levels(key, extent, split, -0.22, 0.18) if split else 1.0
    array = jax.random.normal(key, extent, jnp.float32) * scale * level
    return jnp.minimum(jnp.maximum(array, -bound), bound).astype(kind)


def setup_inputs(seed: int = 0) -> dict:
    keys = jax.random.split(jax.random.key(seed), 10)
    forcings = scatter_about(keys[0], (DAYS, CHANNELS, REACHES), 1.0, 6.0, ((2, 256),))
    w_input = scatter_about(keys[1], (4 * UNITS, CHANNELS), CHANNELS ** -0.5, 1.5)
    w_recur = scatter_about(keys[2], (4 * UNITS, UNITS), UNITS ** -0.5, 0.5)
    gate_bias = scatter_about(keys[3], (4 * UNITS,), 1.0, 3.0, (), jnp.float32)
    w_runoff = scatter_about(keys[4], (UNITS,), UNITS ** -0.5, 0.5, (), jnp.float32)
    travel_time = jnp.clip(jnp.exp(math.log(8.0) - 2.0794415 * jax.random.uniform(keys[5], (REACHES,), jnp.float32) ** block_levels(keys[5], (REACHES,), ((0, 256),), -0.2, 0.2)), 1.0, 8.0)
    weight_x = jnp.clip(0.3 * jax.random.uniform(keys[6], (REACHES,), jnp.float32) ** block_levels(keys[6], (REACHES,), ((0, 256),), -0.2, 0.2), 0.0, 0.3)
    drain_basin_keys = jax.random.split(jax.random.fold_in(keys[7], 1), REACHES // R_DEV)
    drain_basin_turns = jax.random.permutation(jax.random.fold_in(keys[7], 3), REACHES // R_DEV)
    drain_basin = jax.vmap(lambda own, number: assign_block(jax.random.fold_in(keys[7], 2), own, number, R_DEV, N_BASIN, 1, CAP, 2))(drain_basin_keys, drain_basin_turns).reshape((REACHES, 1))
    drain_reach = place_ends(jax.random.randint(keys[8], (REACHES, 1), 0, R_DEV), jax.random.fold_in(keys[8], 1), 0, R_DEV - 1).astype(jnp.int32)
    return dict(forcings=forcings, w_input=w_input, w_recur=w_recur, gate_bias=gate_bias, w_runoff=w_runoff, travel_time=travel_time, weight_x=weight_x, drain_basin=drain_basin, drain_reach=drain_reach)


def lstm_days(lstm_state, day_block, w_input, w_recur, gate_bias, w_runoff):
    units = w_recur.shape[1]

    def one_day(recurrent, inputs):
        hidden, memory = recurrent
        gate_sums = jnp.dot(w_input, inputs, preferred_element_type=jnp.float32) + jnp.dot(w_recur, hidden, preferred_element_type=jnp.float32) + gate_bias[:, None]
        ingate = jax.nn.sigmoid(gate_sums[:units])
        forget = jax.nn.sigmoid(gate_sums[units:2 * units])
        candidate = jnp.tanh(gate_sums[2 * units:3 * units])
        outgate = jax.nn.sigmoid(gate_sums[3 * units:])
        memory = forget * memory + ingate * candidate
        hidden = (outgate * jnp.tanh(memory)).astype(jnp.bfloat16)
        runoff = jax.nn.softplus(jnp.dot(w_runoff, hidden.astype(jnp.float32), precision=lax.Precision.HIGHEST))
        return (hidden, memory), runoff

    return lax.scan(one_day, lstm_state, day_block)


def routing_response(travel_time, weight_x, day_count):
    denominator = travel_time * (1.0 - weight_x) + 0.5
    coeff_first = (0.5 - travel_time * weight_x) / denominator
    coeff_second = (0.5 + travel_time * weight_x) / denominator
    recession = (travel_time * (1.0 - weight_x) - 0.5) / denominator
    lag_days = jnp.arange(day_count, dtype=jnp.float32)[:, None]
    later_terms = (coeff_first * recession + coeff_second)[None, :] * jnp.exp((lag_days - 1.0) * jnp.log(recession)[None, :])
    return jnp.where(lag_days < 0.5, coeff_first[None, :], later_terms)


def route(inflow, response):
    length = inflow.shape[0]
    summed = response[0][None, :] * inflow
    for delay in range(1, length):
        shifted = jnp.pad(inflow[:length - delay], ((delay, 0), (0, 0)))
        summed = summed + response[delay][None, :] * shifted
    return summed


def reference(forcings, w_input, w_recur, gate_bias, w_runoff, travel_time, weight_x, drain_basin, drain_reach):
    group_reach = R_DEV * N_BASIN
    day_count = forcings.shape[0]
    per_group = jnp.moveaxis(forcings.reshape(day_count, CHANNELS, N_ORDER, group_reach), 2, 0)
    travels = travel_time.reshape(N_ORDER, group_reach)
    weights = weight_x.reshape(N_ORDER, group_reach)
    target = (drain_basin[:, 0] * R_DEV + drain_reach[:, 0]).astype(jnp.int32).reshape(N_ORDER, group_reach)

    def one_group(arrive, inputs):
        day_block, travel, weighting, target_group = inputs
        lstm_state = (jnp.zeros((UNITS, group_reach), jnp.bfloat16), jnp.zeros((UNITS, group_reach), jnp.float32))
        _, runoff = lstm_days(lstm_state, day_block, w_input, w_recur, gate_bias, w_runoff)
        routed = route(runoff + arrive, routing_response(travel, weighting, day_count))
        passed = jnp.zeros((group_reach, day_count), jnp.float32).at[target_group].add(routed.T).T
        return passed, routed

    _, history = lax.scan(one_group, jnp.zeros((day_count, group_reach), jnp.float32), (per_group, travels, weights, target))
    return jnp.moveaxis(history, 0, 1).reshape(day_count, N_ORDER * group_reach)
```

```python
import functools

import jax
import jax.numpy as jnp
from jax import lax
from jax.experimental import pallas as pl
from jax.experimental.pallas import tpu as pltpu
from jax.sharding import PartitionSpec as P

MESH = pl.DeviceIdType.MESH


def lstm_days(lstm_state, day_block, w_input, w_recur, gate_bias, w_runoff):
    units = w_recur.shape[1]

    def one_day(recurrent, inputs):
        hidden, memory = recurrent
        gate_sums = (
            jnp.dot(w_input, inputs, preferred_element_type=jnp.float32)
            + jnp.dot(w_recur, hidden, preferred_element_type=jnp.float32)
            + gate_bias[:, None]
        )
        ingate = jax.nn.sigmoid(gate_sums[:units])
        forget = jax.nn.sigmoid(gate_sums[units : 2 * units])
        candidate = jnp.tanh(gate_sums[2 * units : 3 * units])
        outgate = jax.nn.sigmoid(gate_sums[3 * units :])
        memory = forget * memory + ingate * candidate
        hidden = (outgate * jnp.tanh(memory)).astype(jnp.bfloat16)
        runoff = jax.nn.softplus(
            jnp.dot(w_runoff, hidden.astype(jnp.float32), precision=lax.Precision.HIGHEST)
        )
        return ((hidden, memory), runoff)

    return lax.scan(one_day, lstm_state, day_block)


def split3(x):
    hi = x.astype(jnp.bfloat16)
    rest = x - hi.astype(jnp.float32)
    mid = rest.astype(jnp.bfloat16)
    lo = (rest - mid.astype(jnp.float32)).astype(jnp.bfloat16)
    return hi, mid, lo


def chain_kernel(n_order, n_basin, cap, runoff_ref, coef_ref, send_ref, table_ref, out_ref,
                 packed, recv, send_sem, recv_sem):
    o = lax.axis_index("order")
    b = lax.axis_index("basin")
    days = runoff_ref.shape[0]

    barrier = pltpu.get_barrier_semaphore()

    def greet(row):
        def body(j, carry):
            pl.semaphore_signal(barrier, inc=1, device_id=(row, j), device_id_type=MESH)
            return carry
        lax.fori_loop(0, n_basin, body, 0)

    @pl.when(o > 0)
    def _():
        greet(o - 1)

    @pl.when(o < n_order - 1)
    def _():
        greet(o + 1)

    at_end = jnp.logical_or(o == 0, o == n_order - 1)

    @pl.when(at_end)
    def _():
        pl.semaphore_wait(barrier, n_basin)

    @pl.when(jnp.logical_not(at_end))
    def _():
        pl.semaphore_wait(barrier, 2 * n_basin)

    out_ref[...] = runoff_ref[...]

    @pl.when(o > 0)
    def _():
        def arrived(j, carry):
            pltpu.make_async_remote_copy(
                src_ref=packed.at[pl.ds(j * cap, cap)],
                dst_ref=recv.at[pl.ds(j * cap, cap)],
                send_sem=send_sem.at[j],
                recv_sem=recv_sem.at[j],
                device_id=(o - 1, j),
                device_id_type=MESH,
            ).wait_recv()
            return carry
        lax.fori_loop(0, n_basin, arrived, 0)
        arrive = None
        for part in split3(recv[...]):
            term = lax.dot_general(part, table_ref[...], (((0,), (0,)), ((), ())),
                                   preferred_element_type=jnp.float32)
            arrive = term if arrive is None else arrive + term
        out_ref[...] = out_ref[...] + arrive

    inflow = out_ref[...]
    c0 = coef_ref[0:1, :]
    gain = coef_ref[1:2, :]
    c2 = coef_ref[2:3, :]
    lagged = jnp.zeros_like(c0)
    rows = []
    for t in range(days):
        if t > 0:
            lagged = inflow[t - 1 : t, :] + c2 * lagged
        rows.append(c0 * inflow[t : t + 1, :] + gain * lagged)
    discharge = jnp.concatenate(rows, axis=0)
    out_ref[...] = discharge

    @pl.when(o < n_order - 1)
    def _():
        packed_val = None
        for part in split3(discharge):
            term = lax.dot_general(send_ref[...], part, (((1,), (1,)), ((), ())),
                                   preferred_element_type=jnp.float32)
            packed_val = term if packed_val is None else packed_val + term
        packed[...] = packed_val

        def start(j, carry):
            pltpu.make_async_remote_copy(
                src_ref=packed.at[pl.ds(j * cap, cap)],
                dst_ref=recv.at[pl.ds(b * cap, cap)],
                send_sem=send_sem.at[j],
                recv_sem=recv_sem.at[b],
                device_id=(o + 1, j),
                device_id_type=MESH,
            ).start()
            return carry
        lax.fori_loop(0, n_basin, start, 0)

        def finish(j, carry):
            pltpu.make_async_remote_copy(
                src_ref=packed.at[pl.ds(j * cap, cap)],
                dst_ref=recv.at[pl.ds(b * cap, cap)],
                send_sem=send_sem.at[j],
                recv_sem=recv_sem.at[b],
                device_id=(o + 1, j),
                device_id_type=MESH,
            ).wait_send()
            return carry
        lax.fori_loop(0, n_basin, finish, 0)


def route_chain(runoff, coef, send_t, table, n_order, n_basin, cap):
    days, reaches = runoff.shape
    slots = n_basin * cap
    vmem = pl.BlockSpec(memory_space=pltpu.VMEM)
    return pl.pallas_call(
        functools.partial(chain_kernel, n_order, n_basin, cap),
        out_shape=jax.ShapeDtypeStruct((days, reaches), jnp.float32),
        in_specs=[vmem] * 4,
        out_specs=vmem,
        scratch_shapes=[
            pltpu.VMEM((slots, days), jnp.float32),
            pltpu.VMEM((slots, days), jnp.float32),
            pltpu.SemaphoreType.DMA((n_basin,)),
            pltpu.SemaphoreType.DMA((n_basin,)),
        ],
        compiler_params=pltpu.CompilerParams(collective_id=0, has_side_effects=True),
    )(runoff, coef, send_t, table)


def per_device(
    forcings, w_input, w_recur, gate_bias, w_runoff, travel_time, weight_x, drain_basin, drain_reach
):
    basins = lax.axis_size("basin")
    groups = lax.axis_size("order")
    day_count = forcings.shape[0]
    reach_count = forcings.shape[2]
    units = w_recur.shape[1]
    capacity = 2 * reach_count // basins
    slots = basins * capacity
    drain_to = drain_basin[:, 0]
    onehot_drain = (drain_to[:, None] == jnp.arange(basins, dtype=jnp.int32)[None, :]).astype(
        jnp.int32
    )
    slot_index = jnp.sum(jnp.cumsum(onehot_drain, axis=0) * onehot_drain, axis=1) - 1
    flat_slot = drain_to * capacity + slot_index
    send_int = (
        flat_slot[:, None] == jnp.arange(slots, dtype=jnp.int32)[None, :]
    ).astype(jnp.int32)
    sent_targets = (jnp.dot(drain_reach[:, 0] + 1, send_int) - 1).reshape(basins, capacity)
    gathered = lax.all_to_all(sent_targets, "basin", split_axis=0, concat_axis=0, tiled=True)
    targets = lax.ppermute(gathered, "order", [(i, i + 1) for i in range(groups - 1)])
    table = (
        targets.reshape(-1)[:, None] == jnp.arange(reach_count, dtype=jnp.int32)[None, :]
    ).astype(jnp.bfloat16)
    send_t = (
        jnp.arange(slots, dtype=jnp.int32)[:, None] == flat_slot[None, :]
    ).astype(jnp.bfloat16)

    denominator = travel_time * (1.0 - weight_x) + 0.5
    coeff_first = (0.5 - travel_time * weight_x) / denominator
    coeff_second = (0.5 + travel_time * weight_x) / denominator
    recession = (travel_time * (1.0 - weight_x) - 0.5) / denominator
    gain = coeff_first * recession + coeff_second
    coef = jnp.zeros((8, reach_count), jnp.float32)
    coef = coef.at[0].set(coeff_first).at[1].set(gain).at[2].set(recession)

    lstm_state = (
        jnp.zeros((units, reach_count), jnp.bfloat16),
        jnp.zeros((units, reach_count), jnp.float32),
    )
    _, runoff = lstm_days(lstm_state, forcings, w_input, w_recur, gate_bias, w_runoff)
    return route_chain(runoff, coef, send_t, table, groups, basins, capacity)


def solution(mesh):
    return jax.shard_map(
        per_device,
        mesh=mesh,
        in_specs=(
            P(None, None, ("order", "basin")),
            P(),
            P(),
            P(),
            P(),
            P(("order", "basin")),
            P(("order", "basin")),
            P(("order", "basin"), None),
            P(("order", "basin"), None),
        ),
        out_specs=P(None, ("order", "basin")),
        check_vma=False,
    )
```

```python
import functools

import jax
import jax.numpy as jnp
from jax import lax
from jax.experimental import pallas as pl
from jax.experimental.pallas import tpu as pltpu
from jax.sharding import PartitionSpec as P

MESH = pl.DeviceIdType.MESH


def lstm_days(lstm_state, day_block, w_input, w_recur, gate_bias, w_runoff):
    units = w_recur.shape[1]

    def one_day(recurrent, inputs):
        hidden, memory = recurrent
        gate_sums = (
            jnp.dot(w_input, inputs, preferred_element_type=jnp.float32)
            + jnp.dot(w_recur, hidden, preferred_element_type=jnp.float32)
            + gate_bias[:, None]
        )
        ingate = jax.nn.sigmoid(gate_sums[:units])
        forget = jax.nn.sigmoid(gate_sums[units : 2 * units])
        candidate = jnp.tanh(gate_sums[2 * units : 3 * units])
        outgate = jax.nn.sigmoid(gate_sums[3 * units :])
        memory = forget * memory + ingate * candidate
        hidden = (outgate * jnp.tanh(memory)).astype(jnp.bfloat16)
        runoff = jax.nn.softplus(
            jnp.dot(w_runoff, hidden.astype(jnp.float32), precision=lax.Precision.HIGHEST)
        )
        return ((hidden, memory), runoff)

    return lax.scan(one_day, lstm_state, day_block)


def split2(x):
    hi = x.astype(jnp.bfloat16)
    lo = (x - hi.astype(jnp.float32)).astype(jnp.bfloat16)
    return hi, lo


def chain_kernel(n_order, n_basin, cap, runoff_ref, coef_ref, send_ref, table_ref, out_ref,
                 packed, recv, send_sem, recv_sem):
    o = lax.axis_index("order")
    b = lax.axis_index("basin")
    days = runoff_ref.shape[0]

    barrier = pltpu.get_barrier_semaphore()

    def greet(row):
        def body(j, carry):
            pl.semaphore_signal(barrier, inc=1, device_id=(row, j), device_id_type=MESH)
            return carry
        lax.fori_loop(0, n_basin, body, 0)

    @pl.when(o > 0)
    def _():
        greet(o - 1)

    @pl.when(o < n_order - 1)
    def _():
        greet(o + 1)

    at_end = jnp.logical_or(o == 0, o == n_order - 1)

    @pl.when(at_end)
    def _():
        pl.semaphore_wait(barrier, n_basin)

    @pl.when(jnp.logical_not(at_end))
    def _():
        pl.semaphore_wait(barrier, 2 * n_basin)

    out_ref[...] = runoff_ref[...]

    @pl.when(o > 0)
    def _():
        def arrived(j, carry):
            pltpu.make_async_remote_copy(
                src_ref=packed.at[pl.ds(j * cap, cap)],
                dst_ref=recv.at[pl.ds(j * cap, cap)],
                send_sem=send_sem.at[j],
                recv_sem=recv_sem.at[j],
                device_id=(o - 1, j),
                device_id_type=MESH,
            ).wait_recv()
            return carry
        lax.fori_loop(0, n_basin, arrived, 0)
        arrive = None
        for part in split2(recv[...]):
            term = lax.dot_general(part, table_ref[...], (((0,), (0,)), ((), ())),
                                   preferred_element_type=jnp.float32)
            arrive = term if arrive is None else arrive + term
        out_ref[...] = out_ref[...] + arrive

    inflow = out_ref[...]
    c0 = coef_ref[0:1, :]
    gain = coef_ref[1:2, :]
    c2 = coef_ref[2:3, :]
    lagged = jnp.zeros_like(c0)
    rows = []
    for t in range(days):
        if t > 0:
            lagged = inflow[t - 1 : t, :] + c2 * lagged
        rows.append(c0 * inflow[t : t + 1, :] + gain * lagged)
    discharge = jnp.concatenate(rows, axis=0)
    out_ref[...] = discharge

    @pl.when(o < n_order - 1)
    def _():
        packed_val = None
        for part in split2(discharge):
            term = lax.dot_general(send_ref[...], part, (((1,), (1,)), ((), ())),
                                   preferred_element_type=jnp.float32)
            packed_val = term if packed_val is None else packed_val + term
        packed[...] = packed_val

        def start(j, carry):
            pltpu.make_async_remote_copy(
                src_ref=packed.at[pl.ds(j * cap, cap)],
                dst_ref=recv.at[pl.ds(b * cap, cap)],
                send_sem=send_sem.at[j],
                recv_sem=recv_sem.at[b],
                device_id=(o + 1, j),
                device_id_type=MESH,
            ).start()
            return carry
        lax.fori_loop(0, n_basin, start, 0)

        def finish(j, carry):
            pltpu.make_async_remote_copy(
                src_ref=packed.at[pl.ds(j * cap, cap)],
                dst_ref=recv.at[pl.ds(b * cap, cap)],
                send_sem=send_sem.at[j],
                recv_sem=recv_sem.at[b],
                device_id=(o + 1, j),
                device_id_type=MESH,
            ).wait_send()
            return carry
        lax.fori_loop(0, n_basin, finish, 0)


def route_chain(runoff, coef, send_t, table, n_order, n_basin, cap):
    days, reaches = runoff.shape
    slots = n_basin * cap
    vmem = pl.BlockSpec(memory_space=pltpu.VMEM)
    return pl.pallas_call(
        functools.partial(chain_kernel, n_order, n_basin, cap),
        out_shape=jax.ShapeDtypeStruct((days, reaches), jnp.float32),
        in_specs=[vmem] * 4,
        out_specs=vmem,
        scratch_shapes=[
            pltpu.VMEM((slots, days), jnp.float32),
            pltpu.VMEM((slots, days), jnp.float32),
            pltpu.SemaphoreType.DMA((n_basin,)),
            pltpu.SemaphoreType.DMA((n_basin,)),
        ],
        compiler_params=pltpu.CompilerParams(collective_id=0, has_side_effects=True),
    )(runoff, coef, send_t, table)


def per_device(
    forcings, w_input, w_recur, gate_bias, w_runoff, travel_time, weight_x, drain_basin, drain_reach
):
    basins = lax.axis_size("basin")
    groups = lax.axis_size("order")
    day_count = forcings.shape[0]
    reach_count = forcings.shape[2]
    units = w_recur.shape[1]
    capacity = 2 * reach_count // basins
    slots = basins * capacity
    drain_to = drain_basin[:, 0]
    onehot_drain = (drain_to[:, None] == jnp.arange(basins, dtype=jnp.int32)[None, :]).astype(
        jnp.int32
    )
    slot_index = jnp.sum(jnp.cumsum(onehot_drain, axis=0) * onehot_drain, axis=1) - 1
    flat_slot = drain_to * capacity + slot_index
    send_int = (
        flat_slot[:, None] == jnp.arange(slots, dtype=jnp.int32)[None, :]
    ).astype(jnp.int32)
    sent_targets = (jnp.dot(drain_reach[:, 0] + 1, send_int) - 1).reshape(basins, capacity)
    gathered = lax.all_to_all(sent_targets, "basin", split_axis=0, concat_axis=0, tiled=True)
    targets = lax.ppermute(gathered, "order", [(i, i + 1) for i in range(groups - 1)])
    table = (
        targets.reshape(-1)[:, None] == jnp.arange(reach_count, dtype=jnp.int32)[None, :]
    ).astype(jnp.bfloat16)
    send_t = (
        jnp.arange(slots, dtype=jnp.int32)[:, None] == flat_slot[None, :]
    ).astype(jnp.bfloat16)

    denominator = travel_time * (1.0 - weight_x) + 0.5
    coeff_first = (0.5 - travel_time * weight_x) / denominator
    coeff_second = (0.5 + travel_time * weight_x) / denominator
    recession = (travel_time * (1.0 - weight_x) - 0.5) / denominator
    gain = coeff_first * recession + coeff_second
    coef = jnp.zeros((8, reach_count), jnp.float32)
    coef = coef.at[0].set(coeff_first).at[1].set(gain).at[2].set(recession)

    lstm_state = (
        jnp.zeros((units, reach_count), jnp.bfloat16),
        jnp.zeros((units, reach_count), jnp.float32),
    )
    _, runoff = lstm_days(lstm_state, forcings, w_input, w_recur, gate_bias, w_runoff)
    return route_chain(runoff, coef, send_t, table, groups, basins, capacity)


def solution(mesh):
    return jax.shard_map(
        per_device,
        mesh=mesh,
        in_specs=(
            P(None, None, ("order", "basin")),
            P(),
            P(),
            P(),
            P(),
            P(("order", "basin")),
            P(("order", "basin")),
            P(("order", "basin"), None),
            P(("order", "basin"), None),
        ),
        out_specs=P(None, ("order", "basin")),
        check_vma=False,
    )
```

```python
import functools

import jax
import jax.numpy as jnp
from jax import lax
from jax.experimental import pallas as pl
from jax.experimental.pallas import tpu as pltpu
from jax.sharding import PartitionSpec as P

MESH = pl.DeviceIdType.MESH


def lstm_days(lstm_state, day_block, w_input, w_recur, gate_bias, w_runoff):
    units = w_recur.shape[1]

    def one_day(recurrent, inputs):
        hidden, memory = recurrent
        gate_sums = (
            jnp.dot(w_input, inputs, preferred_element_type=jnp.float32)
            + jnp.dot(w_recur, hidden, preferred_element_type=jnp.float32)
            + gate_bias[:, None]
        )
        ingate = jax.nn.sigmoid(gate_sums[:units])
        forget = jax.nn.sigmoid(gate_sums[units : 2 * units])
        candidate = jnp.tanh(gate_sums[2 * units : 3 * units])
        outgate = jax.nn.sigmoid(gate_sums[3 * units :])
        memory = forget * memory + ingate * candidate
        hidden = (outgate * jnp.tanh(memory)).astype(jnp.bfloat16)
        runoff = jax.nn.softplus(
            jnp.dot(w_runoff, hidden.astype(jnp.float32), precision=lax.Precision.HIGHEST)
        )
        return ((hidden, memory), runoff)

    return lax.scan(one_day, lstm_state, day_block)


def lstm_kernel(block, forc_ref, w_in_ref, w_rec_ref, bias_ref, w_ro_ref, out_ref, h_scr, c_scr):
    days = forc_ref.shape[0]
    units = w_rec_ref.shape[1]
    reaches = out_ref.shape[2]
    h_scr[...] = jnp.zeros_like(h_scr)
    c_scr[...] = jnp.zeros_like(c_scr)

    def day(t, carry):
        for j in range(reaches // block):
            cols = pl.ds(j * block, block)
            gates = (
                jnp.dot(w_in_ref[...], forc_ref[t, :, cols], preferred_element_type=jnp.float32)
                + jnp.dot(w_rec_ref[...], h_scr[:, cols], preferred_element_type=jnp.float32)
                + bias_ref[...]
            )
            ingate = jax.nn.sigmoid(gates[:units])
            forget = jax.nn.sigmoid(gates[units : 2 * units])
            candidate = jnp.tanh(gates[2 * units : 3 * units])
            outgate = jax.nn.sigmoid(gates[3 * units :])
            memory = forget * c_scr[:, cols] + ingate * candidate
            hidden = (outgate * jnp.tanh(memory)).astype(jnp.bfloat16)
            c_scr[:, cols] = memory
            h_scr[:, cols] = hidden
            z = jnp.sum(w_ro_ref[...] * hidden.astype(jnp.float32), axis=0, keepdims=True)
            out_ref[t, :, cols] = jnp.maximum(z, 0.0) + jnp.log1p(jnp.exp(-jnp.abs(z)))
        return carry

    lax.fori_loop(0, days, day, 0)


def lstm_runoff(forcings, w_input, w_recur, gate_bias, w_runoff, block=128):
    days, _, reaches = forcings.shape
    units = w_recur.shape[1]
    vmem = pl.BlockSpec(memory_space=pltpu.VMEM)
    return pl.pallas_call(
        functools.partial(lstm_kernel, block),
        out_shape=jax.ShapeDtypeStruct((days, 1, reaches), jnp.float32),
        in_specs=[vmem] * 5,
        out_specs=vmem,
        scratch_shapes=[
            pltpu.VMEM((units, reaches), jnp.bfloat16),
            pltpu.VMEM((units, reaches), jnp.float32),
        ],
    )(forcings, w_input, w_recur, gate_bias[:, None], w_runoff[:, None]).reshape(days, reaches)


def split2(x):
    hi = x.astype(jnp.bfloat16)
    lo = (x - hi.astype(jnp.float32)).astype(jnp.bfloat16)
    return hi, lo


def chain_kernel(n_order, n_basin, cap, runoff_ref, coef_ref, send_ref, table_ref, out_ref,
                 packed, recv, send_sem, recv_sem):
    o = lax.axis_index("order")
    b = lax.axis_index("basin")
    days = runoff_ref.shape[0]

    barrier = pltpu.get_barrier_semaphore()

    def greet(row):
        def body(j, carry):
            pl.semaphore_signal(barrier, inc=1, device_id=(row, j), device_id_type=MESH)
            return carry
        lax.fori_loop(0, n_basin, body, 0)

    @pl.when(o > 0)
    def _():
        greet(o - 1)

    @pl.when(o < n_order - 1)
    def _():
        greet(o + 1)

    at_end = jnp.logical_or(o == 0, o == n_order - 1)

    @pl.when(at_end)
    def _():
        pl.semaphore_wait(barrier, n_basin)

    @pl.when(jnp.logical_not(at_end))
    def _():
        pl.semaphore_wait(barrier, 2 * n_basin)

    out_ref[...] = runoff_ref[...]

    @pl.when(o > 0)
    def _():
        def arrived(j, carry):
            pltpu.make_async_remote_copy(
                src_ref=packed.at[pl.ds(j * cap, cap)],
                dst_ref=recv.at[pl.ds(j * cap, cap)],
                send_sem=send_sem.at[j],
                recv_sem=recv_sem.at[j],
                device_id=(o - 1, j),
                device_id_type=MESH,
            ).wait_recv()
            return carry
        lax.fori_loop(0, n_basin, arrived, 0)
        arrive = None
        for part in split2(recv[...]):
            term = lax.dot_general(part, table_ref[...], (((0,), (0,)), ((), ())),
                                   preferred_element_type=jnp.float32)
            arrive = term if arrive is None else arrive + term
        out_ref[...] = out_ref[...] + arrive

    inflow = out_ref[...]
    c0 = coef_ref[0:1, :]
    gain = coef_ref[1:2, :]
    c2 = coef_ref[2:3, :]
    lagged = jnp.zeros_like(c0)
    rows = []
    for t in range(days):
        if t > 0:
            lagged = inflow[t - 1 : t, :] + c2 * lagged
        rows.append(c0 * inflow[t : t + 1, :] + gain * lagged)
    discharge = jnp.concatenate(rows, axis=0)
    out_ref[...] = discharge

    @pl.when(o < n_order - 1)
    def _():
        packed_val = None
        for part in split2(discharge):
            term = lax.dot_general(send_ref[...], part, (((1,), (1,)), ((), ())),
                                   preferred_element_type=jnp.float32)
            packed_val = term if packed_val is None else packed_val + term
        packed[...] = packed_val

        def start(j, carry):
            pltpu.make_async_remote_copy(
                src_ref=packed.at[pl.ds(j * cap, cap)],
                dst_ref=recv.at[pl.ds(b * cap, cap)],
                send_sem=send_sem.at[j],
                recv_sem=recv_sem.at[b],
                device_id=(o + 1, j),
                device_id_type=MESH,
            ).start()
            return carry
        lax.fori_loop(0, n_basin, start, 0)

        def finish(j, carry):
            pltpu.make_async_remote_copy(
                src_ref=packed.at[pl.ds(j * cap, cap)],
                dst_ref=recv.at[pl.ds(b * cap, cap)],
                send_sem=send_sem.at[j],
                recv_sem=recv_sem.at[b],
                device_id=(o + 1, j),
                device_id_type=MESH,
            ).wait_send()
            return carry
        lax.fori_loop(0, n_basin, finish, 0)


def route_chain(runoff, coef, send_t, table, n_order, n_basin, cap):
    days, reaches = runoff.shape
    slots = n_basin * cap
    vmem = pl.BlockSpec(memory_space=pltpu.VMEM)
    return pl.pallas_call(
        functools.partial(chain_kernel, n_order, n_basin, cap),
        out_shape=jax.ShapeDtypeStruct((days, reaches), jnp.float32),
        in_specs=[vmem] * 4,
        out_specs=vmem,
        scratch_shapes=[
            pltpu.VMEM((slots, days), jnp.float32),
            pltpu.VMEM((slots, days), jnp.float32),
            pltpu.SemaphoreType.DMA((n_basin,)),
            pltpu.SemaphoreType.DMA((n_basin,)),
        ],
        compiler_params=pltpu.CompilerParams(collective_id=0, has_side_effects=True),
    )(runoff, coef, send_t, table)


def per_device(
    forcings, w_input, w_recur, gate_bias, w_runoff, travel_time, weight_x, drain_basin, drain_reach
):
    basins = lax.axis_size("basin")
    groups = lax.axis_size("order")
    day_count = forcings.shape[0]
    reach_count = forcings.shape[2]
    units = w_recur.shape[1]
    capacity = 2 * reach_count // basins
    slots = basins * capacity
    drain_to = drain_basin[:, 0]
    onehot_drain = (drain_to[:, None] == jnp.arange(basins, dtype=jnp.int32)[None, :]).astype(
        jnp.int32
    )
    slot_index = jnp.sum(jnp.cumsum(onehot_drain, axis=0) * onehot_drain, axis=1) - 1
    flat_slot = drain_to * capacity + slot_index
    send_int = (
        flat_slot[:, None] == jnp.arange(slots, dtype=jnp.int32)[None, :]
    ).astype(jnp.int32)
    sent_targets = (jnp.dot(drain_reach[:, 0] + 1, send_int) - 1).reshape(basins, capacity)
    gathered = lax.all_to_all(sent_targets, "basin", split_axis=0, concat_axis=0, tiled=True)
    targets = lax.ppermute(gathered, "order", [(i, i + 1) for i in range(groups - 1)])
    table = (
        targets.reshape(-1)[:, None] == jnp.arange(reach_count, dtype=jnp.int32)[None, :]
    ).astype(jnp.bfloat16)
    send_t = (
        jnp.arange(slots, dtype=jnp.int32)[:, None] == flat_slot[None, :]
    ).astype(jnp.bfloat16)

    denominator = travel_time * (1.0 - weight_x) + 0.5
    coeff_first = (0.5 - travel_time * weight_x) / denominator
    coeff_second = (0.5 + travel_time * weight_x) / denominator
    recession = (travel_time * (1.0 - weight_x) - 0.5) / denominator
    gain = coeff_first * recession + coeff_second
    coef = jnp.zeros((8, reach_count), jnp.float32)
    coef = coef.at[0].set(coeff_first).at[1].set(gain).at[2].set(recession)

    runoff = lstm_runoff(forcings, w_input, w_recur, gate_bias, w_runoff)
    return route_chain(runoff, coef, send_t, table, groups, basins, capacity)


def solution(mesh):
    return jax.shard_map(
        per_device,
        mesh=mesh,
        in_specs=(
            P(None, None, ("order", "basin")),
            P(),
            P(),
            P(),
            P(),
            P(("order", "basin")),
            P(("order", "basin")),
            P(("order", "basin"), None),
            P(("order", "basin"), None),
        ),
        out_specs=P(None, ("order", "basin")),
        check_vma=False,
    )
```

```python
import functools

import jax
import jax.numpy as jnp
from jax import lax
from jax.experimental import pallas as pl
from jax.experimental.pallas import tpu as pltpu
from jax.sharding import PartitionSpec as P

MESH = pl.DeviceIdType.MESH


def lstm_days(lstm_state, day_block, w_input, w_recur, gate_bias, w_runoff):
    units = w_recur.shape[1]

    def one_day(recurrent, inputs):
        hidden, memory = recurrent
        gate_sums = (
            jnp.dot(w_input, inputs, preferred_element_type=jnp.float32)
            + jnp.dot(w_recur, hidden, preferred_element_type=jnp.float32)
            + gate_bias[:, None]
        )
        ingate = jax.nn.sigmoid(gate_sums[:units])
        forget = jax.nn.sigmoid(gate_sums[units : 2 * units])
        candidate = jnp.tanh(gate_sums[2 * units : 3 * units])
        outgate = jax.nn.sigmoid(gate_sums[3 * units :])
        memory = forget * memory + ingate * candidate
        hidden = (outgate * jnp.tanh(memory)).astype(jnp.bfloat16)
        runoff = jax.nn.softplus(
            jnp.dot(w_runoff, hidden.astype(jnp.float32), precision=lax.Precision.HIGHEST)
        )
        return ((hidden, memory), runoff)

    return lax.scan(one_day, lstm_state, day_block)


def lstm_kernel(block, forc_ref, w_in_ref, w_rec_ref, bias_ref, w_ro_ref, out_ref, h_scr, c_scr):
    days = forc_ref.shape[0]
    units = w_rec_ref.shape[1]
    reaches = out_ref.shape[2]
    h_scr[...] = jnp.zeros_like(h_scr)
    c_scr[...] = jnp.zeros_like(c_scr)

    def day(t, carry):
        for j in range(reaches // block):
            cols = pl.ds(j * block, block)
            gates = (
                jnp.dot(w_in_ref[...], forc_ref[t, :, cols], preferred_element_type=jnp.float32)
                + jnp.dot(w_rec_ref[...], h_scr[:, cols], preferred_element_type=jnp.float32)
                + bias_ref[...]
            )
            ingate = jax.nn.sigmoid(gates[:units])
            forget = jax.nn.sigmoid(gates[units : 2 * units])
            candidate = jnp.tanh(gates[2 * units : 3 * units])
            outgate = jax.nn.sigmoid(gates[3 * units :])
            memory = forget * c_scr[:, cols] + ingate * candidate
            hidden = (outgate * jnp.tanh(memory)).astype(jnp.bfloat16)
            c_scr[:, cols] = memory
            h_scr[:, cols] = hidden
            z = jnp.sum(w_ro_ref[...] * hidden.astype(jnp.float32), axis=0, keepdims=True)
            out_ref[t, :, cols] = jnp.maximum(z, 0.0) + jnp.log1p(jnp.exp(-jnp.abs(z)))
        return carry

    lax.fori_loop(0, days, day, 0)


def lstm_runoff(forcings, w_input, w_recur, gate_bias, w_runoff, block=128):
    days, _, reaches = forcings.shape
    units = w_recur.shape[1]
    vmem = pl.BlockSpec(memory_space=pltpu.VMEM)
    return pl.pallas_call(
        functools.partial(lstm_kernel, block),
        out_shape=jax.ShapeDtypeStruct((days, 1, reaches), jnp.float32),
        in_specs=[vmem] * 5,
        out_specs=vmem,
        scratch_shapes=[
            pltpu.VMEM((units, reaches), jnp.bfloat16),
            pltpu.VMEM((units, reaches), jnp.float32),
        ],
    )(forcings, w_input, w_recur, gate_bias[:, None], w_runoff[:, None]).reshape(days, reaches)


def split2(x):
    hi = x.astype(jnp.bfloat16)
    lo = (x - hi.astype(jnp.float32)).astype(jnp.bfloat16)
    return hi, lo


def chain_kernel(n_order, n_basin, cap, runoff_ref, coef_ref, send_ref, tgt_ref, out_ref,
                 packed, recv, table_ref, tgt_recv, send_sem, recv_sem, tsend_sem, trecv_sem):
    o = lax.axis_index("order")
    b = lax.axis_index("basin")
    days = runoff_ref.shape[0]

    barrier = pltpu.get_barrier_semaphore()

    def greet(row):
        def body(j, carry):
            pl.semaphore_signal(barrier, inc=1, device_id=(row, j), device_id_type=MESH)
            return carry
        lax.fori_loop(0, n_basin, body, 0)

    @pl.when(o > 0)
    def _():
        greet(o - 1)

    @pl.when(o < n_order - 1)
    def _():
        greet(o + 1)

    at_end = jnp.logical_or(o == 0, o == n_order - 1)

    @pl.when(at_end)
    def _():
        pl.semaphore_wait(barrier, n_basin)

    @pl.when(jnp.logical_not(at_end))
    def _():
        pl.semaphore_wait(barrier, 2 * n_basin)

    def target_copy(j, row):
        return pltpu.make_async_remote_copy(
            src_ref=tgt_ref.at[pl.ds(j * cap, cap)],
            dst_ref=tgt_recv.at[pl.ds(row * cap, cap)],
            send_sem=tsend_sem.at[j],
            recv_sem=trecv_sem.at[row],
            device_id=(o + 1, j),
            device_id_type=MESH,
        )

    @pl.when(o < n_order - 1)
    def _():
        def start(j, carry):
            target_copy(j, b).start()
            return carry
        lax.fori_loop(0, n_basin, start, 0)

    out_ref[...] = runoff_ref[...]

    @pl.when(o > 0)
    def _():
        def got(j, carry):
            pltpu.make_async_remote_copy(
                src_ref=tgt_ref.at[pl.ds(j * cap, cap)],
                dst_ref=tgt_recv.at[pl.ds(j * cap, cap)],
                send_sem=tsend_sem.at[j],
                recv_sem=trecv_sem.at[j],
                device_id=(o - 1, j),
                device_id_type=MESH,
            ).wait_recv()
            return carry
        lax.fori_loop(0, n_basin, got, 0)
        reach = lax.broadcasted_iota(jnp.int32, (1, table_ref.shape[1]), 1)
        table_ref[...] = (tgt_recv[...] == reach).astype(jnp.bfloat16)

        def arrived(j, carry):
            pltpu.make_async_remote_copy(
                src_ref=packed.at[pl.ds(j * cap, cap)],
                dst_ref=recv.at[pl.ds(j * cap, cap)],
                send_sem=send_sem.at[j],
                recv_sem=recv_sem.at[j],
                device_id=(o - 1, j),
                device_id_type=MESH,
            ).wait_recv()
            return carry
        lax.fori_loop(0, n_basin, arrived, 0)
        arrive = None
        for part in split2(recv[...]):
            term = lax.dot_general(part, table_ref[...], (((0,), (0,)), ((), ())),
                                   preferred_element_type=jnp.float32)
            arrive = term if arrive is None else arrive + term
        out_ref[...] = out_ref[...] + arrive

    inflow = out_ref[...]
    c0 = coef_ref[0:1, :]
    gain = coef_ref[1:2, :]
    c2 = coef_ref[2:3, :]
    lagged = jnp.zeros_like(c0)
    rows = []
    for t in range(days):
        if t > 0:
            lagged = inflow[t - 1 : t, :] + c2 * lagged
        rows.append(c0 * inflow[t : t + 1, :] + gain * lagged)
    discharge = jnp.concatenate(rows, axis=0)
    out_ref[...] = discharge

    @pl.when(o < n_order - 1)
    def _():
        packed_val = None
        for part in split2(discharge):
            term = lax.dot_general(send_ref[...], part, (((1,), (1,)), ((), ())),
                                   preferred_element_type=jnp.float32)
            packed_val = term if packed_val is None else packed_val + term
        packed[...] = packed_val

        def start(j, carry):
            pltpu.make_async_remote_copy(
                src_ref=packed.at[pl.ds(j * cap, cap)],
                dst_ref=recv.at[pl.ds(b * cap, cap)],
                send_sem=send_sem.at[j],
                recv_sem=recv_sem.at[b],
                device_id=(o + 1, j),
                device_id_type=MESH,
            ).start()
            return carry
        lax.fori_loop(0, n_basin, start, 0)

        def finish(j, carry):
            pltpu.make_async_remote_copy(
                src_ref=packed.at[pl.ds(j * cap, cap)],
                dst_ref=recv.at[pl.ds(b * cap, cap)],
                send_sem=send_sem.at[j],
                recv_sem=recv_sem.at[b],
                device_id=(o + 1, j),
                device_id_type=MESH,
            ).wait_send()
            return carry
        lax.fori_loop(0, n_basin, finish, 0)

        def finish_targets(j, carry):
            target_copy(j, b).wait_send()
            return carry
        lax.fori_loop(0, n_basin, finish_targets, 0)


def route_chain(runoff, coef, send_t, tgt, n_order, n_basin, cap):
    days, reaches = runoff.shape
    slots = n_basin * cap
    vmem = pl.BlockSpec(memory_space=pltpu.VMEM)
    return pl.pallas_call(
        functools.partial(chain_kernel, n_order, n_basin, cap),
        out_shape=jax.ShapeDtypeStruct((days, reaches), jnp.float32),
        in_specs=[vmem] * 4,
        out_specs=vmem,
        scratch_shapes=[
            pltpu.VMEM((slots, days), jnp.float32),
            pltpu.VMEM((slots, days), jnp.float32),
            pltpu.VMEM((slots, reaches), jnp.bfloat16),
            pltpu.VMEM((slots, 1), jnp.int32),
            pltpu.SemaphoreType.DMA((n_basin,)),
            pltpu.SemaphoreType.DMA((n_basin,)),
            pltpu.SemaphoreType.DMA((n_basin,)),
            pltpu.SemaphoreType.DMA((n_basin,)),
        ],
        compiler_params=pltpu.CompilerParams(collective_id=0, has_side_effects=True),
    )(runoff, coef, send_t, tgt)


def per_device(
    forcings, w_input, w_recur, gate_bias, w_runoff, travel_time, weight_x, drain_basin, drain_reach
):
    basins = lax.axis_size("basin")
    groups = lax.axis_size("order")
    day_count = forcings.shape[0]
    reach_count = forcings.shape[2]
    units = w_recur.shape[1]
    capacity = 2 * reach_count // basins
    slots = basins * capacity
    drain_to = drain_basin[:, 0]
    onehot_drain = (drain_to[:, None] == jnp.arange(basins, dtype=jnp.int32)[None, :]).astype(
        jnp.int32
    )
    slot_index = jnp.sum(jnp.cumsum(onehot_drain, axis=0) * onehot_drain, axis=1) - 1
    flat_slot = drain_to * capacity + slot_index
    send_int = (
        flat_slot[:, None] == jnp.arange(slots, dtype=jnp.int32)[None, :]
    ).astype(jnp.int32)
    sent_targets = (jnp.dot(drain_reach[:, 0] + 1, send_int) - 1).reshape(slots, 1)
    send_t = (
        jnp.arange(slots, dtype=jnp.int32)[:, None] == flat_slot[None, :]
    ).astype(jnp.bfloat16)

    denominator = travel_time * (1.0 - weight_x) + 0.5
    coeff_first = (0.5 - travel_time * weight_x) / denominator
    coeff_second = (0.5 + travel_time * weight_x) / denominator
    recession = (travel_time * (1.0 - weight_x) - 0.5) / denominator
    gain = coeff_first * recession + coeff_second
    coef = jnp.zeros((8, reach_count), jnp.float32)
    coef = coef.at[0].set(coeff_first).at[1].set(gain).at[2].set(recession)

    runoff = lstm_runoff(forcings, w_input, w_recur, gate_bias, w_runoff)
    return route_chain(runoff, coef, send_t, sent_targets, groups, basins, capacity)


def solution(mesh):
    return jax.shard_map(
        per_device,
        mesh=mesh,
        in_specs=(
            P(None, None, ("order", "basin")),
            P(),
            P(),
            P(),
            P(),
            P(("order", "basin")),
            P(("order", "basin")),
            P(("order", "basin"), None),
            P(("order", "basin"), None),
        ),
        out_specs=P(None, ("order", "basin")),
        check_vma=False,
    )
```

```python
import functools

import jax
import jax.numpy as jnp
from jax import lax
from jax.experimental import pallas as pl
from jax.experimental.pallas import tpu as pltpu
from jax.sharding import PartitionSpec as P

MESH = pl.DeviceIdType.MESH


def lstm_days(lstm_state, day_block, w_input, w_recur, gate_bias, w_runoff):
    units = w_recur.shape[1]

    def one_day(recurrent, inputs):
        hidden, memory = recurrent
        gate_sums = (
            jnp.dot(w_input, inputs, preferred_element_type=jnp.float32)
            + jnp.dot(w_recur, hidden, preferred_element_type=jnp.float32)
            + gate_bias[:, None]
        )
        ingate = jax.nn.sigmoid(gate_sums[:units])
        forget = jax.nn.sigmoid(gate_sums[units : 2 * units])
        candidate = jnp.tanh(gate_sums[2 * units : 3 * units])
        outgate = jax.nn.sigmoid(gate_sums[3 * units :])
        memory = forget * memory + ingate * candidate
        hidden = (outgate * jnp.tanh(memory)).astype(jnp.bfloat16)
        runoff = jax.nn.softplus(
            jnp.dot(w_runoff, hidden.astype(jnp.float32), precision=lax.Precision.HIGHEST)
        )
        return ((hidden, memory), runoff)

    return lax.scan(one_day, lstm_state, day_block)


def lstm_kernel(block, forc_ref, w_in_ref, w_rec_ref, bias_ref, w_ro_ref, out_ref, h_scr, c_scr):
    days = forc_ref.shape[0]
    units = w_rec_ref.shape[1]
    reaches = out_ref.shape[2]
    h_scr[...] = jnp.zeros_like(h_scr)
    c_scr[...] = jnp.zeros_like(c_scr)

    def day(t, carry):
        for j in range(reaches // block):
            cols = pl.ds(j * block, block)
            gates = (
                jnp.dot(w_in_ref[...], forc_ref[t, :, cols], preferred_element_type=jnp.float32)
                + jnp.dot(w_rec_ref[...], h_scr[:, cols], preferred_element_type=jnp.float32)
                + bias_ref[...]
            )
            ingate = jax.nn.sigmoid(gates[:units])
            forget = jax.nn.sigmoid(gates[units : 2 * units])
            candidate = jnp.tanh(gates[2 * units : 3 * units])
            outgate = jax.nn.sigmoid(gates[3 * units :])
            memory = forget * c_scr[:, cols] + ingate * candidate
            hidden = (outgate * jnp.tanh(memory)).astype(jnp.bfloat16)
            c_scr[:, cols] = memory
            h_scr[:, cols] = hidden
            z = jnp.sum(w_ro_ref[...] * hidden.astype(jnp.float32), axis=0, keepdims=True)
            out_ref[t, :, cols] = jnp.maximum(z, 0.0) + jnp.log1p(jnp.exp(-jnp.abs(z)))
        return carry

    lax.fori_loop(0, days, day, 0)


def lstm_runoff(forcings, w_input, w_recur, gate_bias, w_runoff, block=128):
    days, _, reaches = forcings.shape
    units = w_recur.shape[1]
    vmem = pl.BlockSpec(memory_space=pltpu.VMEM)
    return pl.pallas_call(
        functools.partial(lstm_kernel, block),
        out_shape=jax.ShapeDtypeStruct((days, 1, reaches), jnp.float32),
        in_specs=[vmem] * 5,
        out_specs=vmem,
        scratch_shapes=[
            pltpu.VMEM((units, reaches), jnp.bfloat16),
            pltpu.VMEM((units, reaches), jnp.float32),
        ],
    )(forcings, w_input, w_recur, gate_bias[:, None], w_runoff[:, None]).reshape(days, reaches)


def split2(x):
    hi = x.astype(jnp.bfloat16)
    lo = (x - hi.astype(jnp.float32)).astype(jnp.bfloat16)
    return hi, lo


def chain_kernel(n_order, n_basin, cap, runoff_ref, coef_ref, send_ref, tgt_ref, out_ref,
                 packed, recv, table_ref, tgt_recv, spread, send_sem, recv_sem, tsend_sem, trecv_sem):
    o = lax.axis_index("order")
    b = lax.axis_index("basin")
    days, reaches = runoff_ref.shape
    groups = cap // 8
    rows = 8

    barrier = pltpu.get_barrier_semaphore()

    def greet(row):
        def body(j, carry):
            pl.semaphore_signal(barrier, inc=1, device_id=(row, j), device_id_type=MESH)
            return carry
        lax.fori_loop(0, n_basin, body, 0)

    @pl.when(o > 0)
    def _():
        greet(o - 1)

    @pl.when(o < n_order - 1)
    def _():
        greet(o + 1)

    at_end = jnp.logical_or(o == 0, o == n_order - 1)

    @pl.when(at_end)
    def _():
        pl.semaphore_wait(barrier, n_basin)

    @pl.when(jnp.logical_not(at_end))
    def _():
        pl.semaphore_wait(barrier, 2 * n_basin)

    def target_copy(j, row, peer):
        return pltpu.make_async_remote_copy(
            src_ref=tgt_ref.at[pl.ds(j * rows, rows)],
            dst_ref=tgt_recv.at[pl.ds(row * rows, rows)],
            send_sem=tsend_sem.at[j],
            recv_sem=trecv_sem.at[row],
            device_id=(peer, j),
            device_id_type=MESH,
        )

    def data_copy(j, row, peer):
        return pltpu.make_async_remote_copy(
            src_ref=packed.at[pl.ds(j * rows, rows)],
            dst_ref=recv.at[pl.ds(row * rows, rows)],
            send_sem=send_sem.at[j],
            recv_sem=recv_sem.at[row],
            device_id=(peer, j),
            device_id_type=MESH,
        )

    @pl.when(o < n_order - 1)
    def _():
        def start(j, carry):
            target_copy(j, b, o + 1).start()
            return carry
        lax.fori_loop(0, n_basin, start, 0)

    spread[...] = jnp.zeros_like(spread)
    out_ref[...] = runoff_ref[...]

    @pl.when(o > 0)
    def _():
        def got(j, carry):
            target_copy(j, j, o - 1).wait_recv()
            return carry
        lax.fori_loop(0, n_basin, got, 0)
        reach = lax.broadcasted_iota(jnp.int32, (1, reaches), 1)
        for k in range(groups):
            table_ref[:, k * reaches : (k + 1) * reaches] = (
                tgt_recv[:, k : k + 1] == reach
            ).astype(jnp.bfloat16)

        def arrived(j, carry):
            data_copy(j, j, o - 1).wait_recv()
            return carry
        lax.fori_loop(0, n_basin, arrived, 0)
        wide = None
        for part in split2(recv[...]):
            term = lax.dot_general(part, table_ref[...], (((0,), (0,)), ((), ())),
                                   preferred_element_type=jnp.float32)
            wide = term if wide is None else wide + term
        arrive = wide[0:days, 0:reaches]
        for k in range(1, groups):
            arrive = arrive + wide[k * days : (k + 1) * days, k * reaches : (k + 1) * reaches]
        out_ref[...] = out_ref[...] + arrive

    inflow = out_ref[...]
    c0 = coef_ref[0:1, :]
    gain = coef_ref[1:2, :]
    c2 = coef_ref[2:3, :]
    lagged = jnp.zeros_like(c0)
    day_rows = []
    for t in range(days):
        if t > 0:
            lagged = inflow[t - 1 : t, :] + c2 * lagged
        day_rows.append(c0 * inflow[t : t + 1, :] + gain * lagged)
    discharge = jnp.concatenate(day_rows, axis=0)
    out_ref[...] = discharge

    @pl.when(o < n_order - 1)
    def _():
        packed_val = None
        for part in split2(discharge):
            for k in range(groups):
                spread[k * days : (k + 1) * days, k * reaches : (k + 1) * reaches] = part
            term = lax.dot_general(send_ref[...], spread[...], (((1,), (1,)), ((), ())),
                                   preferred_element_type=jnp.float32)
            packed_val = term if packed_val is None else packed_val + term
        packed[...] = packed_val

        def start(j, carry):
            data_copy(j, b, o + 1).start()
            return carry
        lax.fori_loop(0, n_basin, start, 0)

        def finish(j, carry):
            data_copy(j, b, o + 1).wait_send()
            target_copy(j, b, o + 1).wait_send()
            return carry
        lax.fori_loop(0, n_basin, finish, 0)


def route_chain(runoff, coef, send_t, tgt, n_order, n_basin, cap):
    days, reaches = runoff.shape
    groups = cap // 8
    vmem = pl.BlockSpec(memory_space=pltpu.VMEM)
    return pl.pallas_call(
        functools.partial(chain_kernel, n_order, n_basin, cap),
        out_shape=jax.ShapeDtypeStruct((days, reaches), jnp.float32),
        in_specs=[vmem] * 4,
        out_specs=vmem,
        scratch_shapes=[
            pltpu.VMEM((n_basin * 8, groups * days), jnp.float32),
            pltpu.VMEM((n_basin * 8, groups * days), jnp.float32),
            pltpu.VMEM((n_basin * 8, groups * reaches), jnp.bfloat16),
            pltpu.VMEM((n_basin * 8, groups), jnp.int32),
            pltpu.VMEM((groups * days, groups * reaches), jnp.bfloat16),
            pltpu.SemaphoreType.DMA((n_basin,)),
            pltpu.SemaphoreType.DMA((n_basin,)),
            pltpu.SemaphoreType.DMA((n_basin,)),
            pltpu.SemaphoreType.DMA((n_basin,)),
        ],
        compiler_params=pltpu.CompilerParams(collective_id=0, has_side_effects=True),
    )(runoff, coef, send_t, tgt)


def per_device(
    forcings, w_input, w_recur, gate_bias, w_runoff, travel_time, weight_x, drain_basin, drain_reach
):
    basins = lax.axis_size("basin")
    groups = lax.axis_size("order")
    day_count = forcings.shape[0]
    reach_count = forcings.shape[2]
    units = w_recur.shape[1]
    capacity = 2 * reach_count // basins
    slots = basins * capacity
    drain_to = drain_basin[:, 0]
    onehot_drain = (drain_to[:, None] == jnp.arange(basins, dtype=jnp.int32)[None, :]).astype(
        jnp.int32
    )
    slot_index = jnp.sum(jnp.cumsum(onehot_drain, axis=0) * onehot_drain, axis=1) - 1
    flat_slot = drain_to * capacity + slot_index
    send_int = (
        flat_slot[:, None] == jnp.arange(slots, dtype=jnp.int32)[None, :]
    ).astype(jnp.int32)
    groups_k = capacity // 8
    sent_targets = (jnp.dot(drain_reach[:, 0] + 1, send_int) - 1).reshape(basins, groups_k, 8)
    sent_targets = sent_targets.transpose(0, 2, 1).reshape(basins * 8, groups_k)
    send_t = (
        jnp.arange(slots, dtype=jnp.int32)[:, None] == flat_slot[None, :]
    ).astype(jnp.bfloat16)
    send_t = send_t.reshape(basins, groups_k, 8, reach_count).transpose(0, 2, 1, 3)
    send_t = send_t.reshape(basins * 8, groups_k * reach_count)

    denominator = travel_time * (1.0 - weight_x) + 0.5
    coeff_first = (0.5 - travel_time * weight_x) / denominator
    coeff_second = (0.5 + travel_time * weight_x) / denominator
    recession = (travel_time * (1.0 - weight_x) - 0.5) / denominator
    gain = coeff_first * recession + coeff_second
    coef = jnp.zeros((8, reach_count), jnp.float32)
    coef = coef.at[0].set(coeff_first).at[1].set(gain).at[2].set(recession)

    runoff = lstm_runoff(forcings, w_input, w_recur, gate_bias, w_runoff)
    return route_chain(runoff, coef, send_t, sent_targets, groups, basins, capacity)


def solution(mesh):
    return jax.shard_map(
        per_device,
        mesh=mesh,
        in_specs=(
            P(None, None, ("order", "basin")),
            P(),
            P(),
            P(),
            P(),
            P(("order", "basin")),
            P(("order", "basin")),
            P(("order", "basin"), None),
            P(("order", "basin"), None),
        ),
        out_specs=P(None, ("order", "basin")),
        check_vma=False,
    )
```

```python
import functools

import jax
import jax.numpy as jnp
from jax import lax
from jax.experimental import pallas as pl
from jax.experimental.pallas import tpu as pltpu
from jax.sharding import PartitionSpec as P

MESH = pl.DeviceIdType.MESH


def lstm_days(lstm_state, day_block, w_input, w_recur, gate_bias, w_runoff):
    units = w_recur.shape[1]

    def one_day(recurrent, inputs):
        hidden, memory = recurrent
        gate_sums = (
            jnp.dot(w_input, inputs, preferred_element_type=jnp.float32)
            + jnp.dot(w_recur, hidden, preferred_element_type=jnp.float32)
            + gate_bias[:, None]
        )
        ingate = jax.nn.sigmoid(gate_sums[:units])
        forget = jax.nn.sigmoid(gate_sums[units : 2 * units])
        candidate = jnp.tanh(gate_sums[2 * units : 3 * units])
        outgate = jax.nn.sigmoid(gate_sums[3 * units :])
        memory = forget * memory + ingate * candidate
        hidden = (outgate * jnp.tanh(memory)).astype(jnp.bfloat16)
        runoff = jax.nn.softplus(
            jnp.dot(w_runoff, hidden.astype(jnp.float32), precision=lax.Precision.HIGHEST)
        )
        return ((hidden, memory), runoff)

    return lax.scan(one_day, lstm_state, day_block)


def lstm_kernel(block, forc_ref, w_in_ref, w_rec_ref, bias_ref, w_ro_ref, out_ref, h_scr, c_scr):
    days = forc_ref.shape[0]
    units = w_rec_ref.shape[1]
    reaches = out_ref.shape[2]
    h_scr[...] = jnp.zeros_like(h_scr)
    c_scr[...] = jnp.zeros_like(c_scr)

    def day(t, carry):
        for j in range(reaches // block):
            cols = pl.ds(j * block, block)
            gates = (
                jnp.dot(w_in_ref[...], forc_ref[t, :, cols], preferred_element_type=jnp.float32)
                + jnp.dot(w_rec_ref[...], h_scr[:, cols], preferred_element_type=jnp.float32)
                + bias_ref[...]
            )
            ingate = jax.nn.sigmoid(gates[:units])
            forget = jax.nn.sigmoid(gates[units : 2 * units])
            candidate = jnp.tanh(gates[2 * units : 3 * units])
            outgate = jax.nn.sigmoid(gates[3 * units :])
            memory = forget * c_scr[:, cols] + ingate * candidate
            hidden = (outgate * jnp.tanh(memory)).astype(jnp.bfloat16)
            c_scr[:, cols] = memory
            h_scr[:, cols] = hidden
            z = jnp.sum(w_ro_ref[...] * hidden.astype(jnp.float32), axis=0, keepdims=True)
            out_ref[t, :, cols] = jnp.maximum(z, 0.0) + jnp.log1p(jnp.exp(-jnp.abs(z)))
        return carry

    lax.fori_loop(0, days, day, 0)


def lstm_runoff(forcings, w_input, w_recur, gate_bias, w_runoff, block=128):
    days, _, reaches = forcings.shape
    units = w_recur.shape[1]
    vmem = pl.BlockSpec(memory_space=pltpu.VMEM)
    return pl.pallas_call(
        functools.partial(lstm_kernel, block),
        out_shape=jax.ShapeDtypeStruct((days, 1, reaches), jnp.float32),
        in_specs=[vmem] * 5,
        out_specs=vmem,
        scratch_shapes=[
            pltpu.VMEM((units, reaches), jnp.bfloat16),
            pltpu.VMEM((units, reaches), jnp.float32),
        ],
    )(forcings, w_input, w_recur, gate_bias[:, None], w_runoff[:, None]).reshape(days, reaches)


def split2(x):
    hi = x.astype(jnp.bfloat16)
    lo = (x - hi.astype(jnp.float32)).astype(jnp.bfloat16)
    return hi, lo


def chain_kernel(n_order, n_basin, cap, runoff_ref, coef_ref, send_ref, tgt_ref, out_ref,
                 packed, recv, table_ref, tgt_recv, spread, send_sem, recv_sem, tsend_sem, trecv_sem):
    o = lax.axis_index("order")
    b = lax.axis_index("basin")
    days, reaches = runoff_ref.shape
    groups = cap // 8
    rows = 8

    barrier = pltpu.get_barrier_semaphore()

    def greet(row):
        def body(j, carry):
            pl.semaphore_signal(barrier, inc=1, device_id=(row, j), device_id_type=MESH)
            return carry
        lax.fori_loop(0, n_basin, body, 0)

    @pl.when(o > 0)
    def _():
        greet(o - 1)

    @pl.when(o < n_order - 1)
    def _():
        greet(o + 1)

    at_end = jnp.logical_or(o == 0, o == n_order - 1)

    @pl.when(at_end)
    def _():
        pl.semaphore_wait(barrier, n_basin)

    @pl.when(jnp.logical_not(at_end))
    def _():
        pl.semaphore_wait(barrier, 2 * n_basin)

    def target_copy(j, row, peer):
        return pltpu.make_async_remote_copy(
            src_ref=tgt_ref.at[pl.ds(j * rows, rows)],
            dst_ref=tgt_recv.at[pl.ds(row * rows, rows)],
            send_sem=tsend_sem.at[j],
            recv_sem=trecv_sem.at[row],
            device_id=(peer, j),
            device_id_type=MESH,
        )

    def data_copy(j, row, peer):
        return pltpu.make_async_remote_copy(
            src_ref=packed.at[pl.ds(j * rows, rows)],
            dst_ref=recv.at[pl.ds(row * rows, rows)],
            send_sem=send_sem.at[j],
            recv_sem=recv_sem.at[row],
            device_id=(peer, j),
            device_id_type=MESH,
        )

    @pl.when(o < n_order - 1)
    def _():
        def start(j, carry):
            target_copy(j, b, o + 1).start()
            return carry
        lax.fori_loop(0, n_basin, start, 0)

    spread[...] = jnp.zeros_like(spread)
    out_ref[...] = runoff_ref[...]

    @pl.when(o > 0)
    def _():
        def got(j, carry):
            target_copy(j, j, o - 1).wait_recv()
            return carry
        lax.fori_loop(0, n_basin, got, 0)
        reach = lax.broadcasted_iota(jnp.int32, (1, reaches), 1)
        for k in range(groups):
            table_ref[:, k * reaches : (k + 1) * reaches] = (
                tgt_recv[:, k : k + 1] == reach
            ).astype(jnp.bfloat16)

        def arrived(j, carry):
            data_copy(j, j, o - 1).wait_recv()
            return carry
        lax.fori_loop(0, n_basin, arrived, 0)
        both = jnp.concatenate(split2(recv[...]), axis=1)
        stacked = lax.dot_general(both, table_ref[...], (((0,), (0,)), ((), ())),
                                  preferred_element_type=jnp.float32)
        half = stacked.shape[0] // 2
        wide = stacked[:half] + stacked[half:]
        arrive = wide[0:days, 0:reaches]
        for k in range(1, groups):
            arrive = arrive + wide[k * days : (k + 1) * days, k * reaches : (k + 1) * reaches]
        out_ref[...] = out_ref[...] + arrive

    inflow = out_ref[...]
    c0 = coef_ref[0:1, :]
    gain = coef_ref[1:2, :]
    c2 = coef_ref[2:3, :]
    lagged = jnp.zeros_like(c0)
    day_rows = []
    for t in range(days):
        if t > 0:
            lagged = inflow[t - 1 : t, :] + c2 * lagged
        day_rows.append(c0 * inflow[t : t + 1, :] + gain * lagged)
    discharge = jnp.concatenate(day_rows, axis=0)
    out_ref[...] = discharge

    @pl.when(o < n_order - 1)
    def _():
        for p, part in enumerate(split2(discharge)):
            for k in range(groups):
                top = (p * groups + k) * days
                spread[top : top + days, k * reaches : (k + 1) * reaches] = part
        stacked = lax.dot_general(send_ref[...], spread[...], (((1,), (1,)), ((), ())),
                                  preferred_element_type=jnp.float32)
        half = stacked.shape[1] // 2
        packed[...] = stacked[:, :half] + stacked[:, half:]

        def start(j, carry):
            data_copy(j, b, o + 1).start()
            return carry
        lax.fori_loop(0, n_basin, start, 0)

        def finish(j, carry):
            data_copy(j, b, o + 1).wait_send()
            target_copy(j, b, o + 1).wait_send()
            return carry
        lax.fori_loop(0, n_basin, finish, 0)


def route_chain(runoff, coef, send_t, tgt, n_order, n_basin, cap):
    days, reaches = runoff.shape
    groups = cap // 8
    vmem = pl.BlockSpec(memory_space=pltpu.VMEM)
    return pl.pallas_call(
        functools.partial(chain_kernel, n_order, n_basin, cap),
        out_shape=jax.ShapeDtypeStruct((days, reaches), jnp.float32),
        in_specs=[vmem] * 4,
        out_specs=vmem,
        scratch_shapes=[
            pltpu.VMEM((n_basin * 8, groups * days), jnp.float32),
            pltpu.VMEM((n_basin * 8, groups * days), jnp.float32),
            pltpu.VMEM((n_basin * 8, groups * reaches), jnp.bfloat16),
            pltpu.VMEM((n_basin * 8, groups), jnp.int32),
            pltpu.VMEM((2 * groups * days, groups * reaches), jnp.bfloat16),
            pltpu.SemaphoreType.DMA((n_basin,)),
            pltpu.SemaphoreType.DMA((n_basin,)),
            pltpu.SemaphoreType.DMA((n_basin,)),
            pltpu.SemaphoreType.DMA((n_basin,)),
        ],
        compiler_params=pltpu.CompilerParams(collective_id=0, has_side_effects=True),
    )(runoff, coef, send_t, tgt)


def per_device(
    forcings, w_input, w_recur, gate_bias, w_runoff, travel_time, weight_x, drain_basin, drain_reach
):
    basins = lax.axis_size("basin")
    groups = lax.axis_size("order")
    day_count = forcings.shape[0]
    reach_count = forcings.shape[2]
    units = w_recur.shape[1]
    capacity = 2 * reach_count // basins
    slots = basins * capacity
    drain_to = drain_basin[:, 0]
    onehot_drain = (drain_to[:, None] == jnp.arange(basins, dtype=jnp.int32)[None, :]).astype(
        jnp.int32
    )
    slot_index = jnp.sum(jnp.cumsum(onehot_drain, axis=0) * onehot_drain, axis=1) - 1
    flat_slot = drain_to * capacity + slot_index
    send_int = (
        flat_slot[:, None] == jnp.arange(slots, dtype=jnp.int32)[None, :]
    ).astype(jnp.int32)
    groups_k = capacity // 8
    sent_targets = (jnp.dot(drain_reach[:, 0] + 1, send_int) - 1).reshape(basins, groups_k, 8)
    sent_targets = sent_targets.transpose(0, 2, 1).reshape(basins * 8, groups_k)
    send_t = (
        jnp.arange(slots, dtype=jnp.int32)[:, None] == flat_slot[None, :]
    ).astype(jnp.bfloat16)
    send_t = send_t.reshape(basins, groups_k, 8, reach_count).transpose(0, 2, 1, 3)
    send_t = send_t.reshape(basins * 8, groups_k * reach_count)

    denominator = travel_time * (1.0 - weight_x) + 0.5
    coeff_first = (0.5 - travel_time * weight_x) / denominator
    coeff_second = (0.5 + travel_time * weight_x) / denominator
    recession = (travel_time * (1.0 - weight_x) - 0.5) / denominator
    gain = coeff_first * recession + coeff_second
    coef = jnp.zeros((8, reach_count), jnp.float32)
    coef = coef.at[0].set(coeff_first).at[1].set(gain).at[2].set(recession)

    runoff = lstm_runoff(forcings, w_input, w_recur, gate_bias, w_runoff)
    return route_chain(runoff, coef, send_t, sent_targets, groups, basins, capacity)


def solution(mesh):
    return jax.shard_map(
        per_device,
        mesh=mesh,
        in_specs=(
            P(None, None, ("order", "basin")),
            P(),
            P(),
            P(),
            P(),
            P(("order", "basin")),
            P(("order", "basin")),
            P(("order", "basin"), None),
            P(("order", "basin"), None),
        ),
        out_specs=P(None, ("order", "basin")),
        check_vma=False,
    )
```

```python
import functools

import jax
import jax.numpy as jnp
from jax import lax
from jax.experimental import pallas as pl
from jax.experimental.pallas import tpu as pltpu
from jax.sharding import PartitionSpec as P

MESH = pl.DeviceIdType.MESH


def lstm_days(lstm_state, day_block, w_input, w_recur, gate_bias, w_runoff):
    units = w_recur.shape[1]

    def one_day(recurrent, inputs):
        hidden, memory = recurrent
        gate_sums = (
            jnp.dot(w_input, inputs, preferred_element_type=jnp.float32)
            + jnp.dot(w_recur, hidden, preferred_element_type=jnp.float32)
            + gate_bias[:, None]
        )
        ingate = jax.nn.sigmoid(gate_sums[:units])
        forget = jax.nn.sigmoid(gate_sums[units : 2 * units])
        candidate = jnp.tanh(gate_sums[2 * units : 3 * units])
        outgate = jax.nn.sigmoid(gate_sums[3 * units :])
        memory = forget * memory + ingate * candidate
        hidden = (outgate * jnp.tanh(memory)).astype(jnp.bfloat16)
        runoff = jax.nn.softplus(
            jnp.dot(w_runoff, hidden.astype(jnp.float32), precision=lax.Precision.HIGHEST)
        )
        return ((hidden, memory), runoff)

    return lax.scan(one_day, lstm_state, day_block)


def lstm_kernel(block, forc_ref, w_in_ref, w_rec_ref, bias_ref, w_ro_ref, out_ref, h_scr, c_scr):
    days = forc_ref.shape[0]
    units = w_rec_ref.shape[1]
    reaches = out_ref.shape[2]
    h_scr[...] = jnp.zeros_like(h_scr)
    c_scr[...] = jnp.zeros_like(c_scr)

    def day(t, carry):
        for j in range(reaches // block):
            cols = pl.ds(j * block, block)
            gates = (
                jnp.dot(w_in_ref[...], forc_ref[t, :, cols], preferred_element_type=jnp.float32)
                + jnp.dot(w_rec_ref[...], h_scr[:, cols], preferred_element_type=jnp.float32)
                + bias_ref[...]
            )
            ingate = jax.nn.sigmoid(gates[:units])
            forget = jax.nn.sigmoid(gates[units : 2 * units])
            candidate = jnp.tanh(gates[2 * units : 3 * units])
            outgate = jax.nn.sigmoid(gates[3 * units :])
            memory = forget * c_scr[:, cols] + ingate * candidate
            hidden = (outgate * jnp.tanh(memory)).astype(jnp.bfloat16)
            c_scr[:, cols] = memory
            h_scr[:, cols] = hidden
            z = jnp.sum(w_ro_ref[...] * hidden.astype(jnp.float32), axis=0, keepdims=True)
            out_ref[t, :, cols] = jnp.maximum(z, 0.0) + jnp.log1p(jnp.exp(-jnp.abs(z)))
        return carry

    lax.fori_loop(0, days, day, 0)


def lstm_runoff(forcings, w_input, w_recur, gate_bias, w_runoff, block=128):
    days, _, reaches = forcings.shape
    units = w_recur.shape[1]
    vmem = pl.BlockSpec(memory_space=pltpu.VMEM)
    return pl.pallas_call(
        functools.partial(lstm_kernel, block),
        out_shape=jax.ShapeDtypeStruct((days, 1, reaches), jnp.float32),
        in_specs=[vmem] * 5,
        out_specs=vmem,
        scratch_shapes=[
            pltpu.VMEM((units, reaches), jnp.bfloat16),
            pltpu.VMEM((units, reaches), jnp.float32),
        ],
    )(forcings, w_input, w_recur, gate_bias[:, None], w_runoff[:, None]).reshape(days, reaches)


def split2(x):
    hi = x.astype(jnp.bfloat16)
    lo = (x - hi.astype(jnp.float32)).astype(jnp.bfloat16)
    return hi, lo


def route_days(inflow, coef):
    days = inflow.shape[0]
    c0, gain, c2 = coef
    lagged = jnp.zeros_like(c0)
    day_rows = []
    for t in range(days):
        if t > 0:
            lagged = inflow[t - 1 : t, :] + c2 * lagged
        day_rows.append(c0 * inflow[t : t + 1, :] + gain * lagged)
    return jnp.concatenate(day_rows, axis=0)


def chain_kernel(n_order, n_basin, cap, runoff_ref, tt_ref, wx_ref, send_ref, tgt_ref, out_ref,
                 packed, recv, table_ref, tgt_recv, spread, send_sem, recv_sem, tsend_sem, trecv_sem):
    o = lax.axis_index("order")
    b = lax.axis_index("basin")
    days, reaches = runoff_ref.shape
    groups = cap // 8
    rows = 8

    barrier = pltpu.get_barrier_semaphore()

    def greet(row):
        def body(j, carry):
            pl.semaphore_signal(barrier, inc=1, device_id=(row, j), device_id_type=MESH)
            return carry
        lax.fori_loop(0, n_basin, body, 0)

    @pl.when(o > 0)
    def _():
        greet(o - 1)

    @pl.when(o < n_order - 1)
    def _():
        greet(o + 1)

    travel = tt_ref[...]
    weight = wx_ref[...]
    denominator = travel * (1.0 - weight) + 0.5
    coeff_first = (0.5 - travel * weight) / denominator
    coeff_second = (0.5 + travel * weight) / denominator
    recession = (travel * (1.0 - weight) - 0.5) / denominator
    coef = (coeff_first, coeff_first * recession + coeff_second, recession)

    def pack(discharge):
        for p, part in enumerate(split2(discharge)):
            for k in range(groups):
                top = (p * groups + k) * days
                spread[top : top + days, k * reaches : (k + 1) * reaches] = part
        stacked = lax.dot_general(send_ref[...], spread[...], (((1,), (1,)), ((), ())),
                                  preferred_element_type=jnp.float32)
        half = stacked.shape[1] // 2
        packed[...] = stacked[:, :half] + stacked[:, half:]

    spread[...] = jnp.zeros_like(spread)

    @pl.when(o == 0)
    def _():
        discharge = route_days(runoff_ref[...], coef)
        out_ref[...] = discharge
        pack(discharge)

    at_end = jnp.logical_or(o == 0, o == n_order - 1)

    @pl.when(at_end)
    def _():
        pl.semaphore_wait(barrier, n_basin)

    @pl.when(jnp.logical_not(at_end))
    def _():
        pl.semaphore_wait(barrier, 2 * n_basin)

    def target_copy(j, row, peer):
        return pltpu.make_async_remote_copy(
            src_ref=tgt_ref.at[pl.ds(j * rows, rows)],
            dst_ref=tgt_recv.at[pl.ds(row * rows, rows)],
            send_sem=tsend_sem.at[j],
            recv_sem=trecv_sem.at[row],
            device_id=(peer, j),
            device_id_type=MESH,
        )

    def data_copy(j, row, peer):
        return pltpu.make_async_remote_copy(
            src_ref=packed.at[pl.ds(j * rows, rows)],
            dst_ref=recv.at[pl.ds(row * rows, rows)],
            send_sem=send_sem.at[j],
            recv_sem=recv_sem.at[row],
            device_id=(peer, j),
            device_id_type=MESH,
        )

    @pl.when(o < n_order - 1)
    def _():
        def start(j, carry):
            target_copy(j, b, o + 1).start()
            return carry
        lax.fori_loop(0, n_basin, start, 0)

    @pl.when(o > 0)
    def _():
        def got(j, carry):
            target_copy(j, j, o - 1).wait_recv()
            return carry
        lax.fori_loop(0, n_basin, got, 0)
        reach = lax.broadcasted_iota(jnp.int32, (1, reaches), 1)
        for k in range(groups):
            table_ref[:, k * reaches : (k + 1) * reaches] = (
                tgt_recv[:, k : k + 1] == reach
            ).astype(jnp.bfloat16)

        def arrived(j, carry):
            data_copy(j, j, o - 1).wait_recv()
            return carry
        lax.fori_loop(0, n_basin, arrived, 0)
        both = jnp.concatenate(split2(recv[...]), axis=1)
        stacked = lax.dot_general(both, table_ref[...], (((0,), (0,)), ((), ())),
                                  preferred_element_type=jnp.float32)
        half = stacked.shape[0] // 2
        wide = stacked[:half] + stacked[half:]
        arrive = wide[0:days, 0:reaches]
        for k in range(1, groups):
            arrive = arrive + wide[k * days : (k + 1) * days, k * reaches : (k + 1) * reaches]
        discharge = route_days(runoff_ref[...] + arrive, coef)
        out_ref[...] = discharge

        @pl.when(o < n_order - 1)
        def _():
            pack(discharge)

    @pl.when(o < n_order - 1)
    def _():
        def start(j, carry):
            data_copy(j, b, o + 1).start()
            return carry
        lax.fori_loop(0, n_basin, start, 0)

        def finish(j, carry):
            data_copy(j, b, o + 1).wait_send()
            target_copy(j, b, o + 1).wait_send()
            return carry
        lax.fori_loop(0, n_basin, finish, 0)


def route_chain(runoff, travel_time, weight_x, send_t, tgt, n_order, n_basin, cap):
    days, reaches = runoff.shape
    groups = cap // 8
    vmem = pl.BlockSpec(memory_space=pltpu.VMEM)
    return pl.pallas_call(
        functools.partial(chain_kernel, n_order, n_basin, cap),
        out_shape=jax.ShapeDtypeStruct((days, reaches), jnp.float32),
        in_specs=[vmem] * 5,
        out_specs=vmem,
        scratch_shapes=[
            pltpu.VMEM((n_basin * 8, groups * days), jnp.float32),
            pltpu.VMEM((n_basin * 8, groups * days), jnp.float32),
            pltpu.VMEM((n_basin * 8, groups * reaches), jnp.bfloat16),
            pltpu.VMEM((n_basin * 8, groups), jnp.int32),
            pltpu.VMEM((2 * groups * days, groups * reaches), jnp.bfloat16),
            pltpu.SemaphoreType.DMA((n_basin,)),
            pltpu.SemaphoreType.DMA((n_basin,)),
            pltpu.SemaphoreType.DMA((n_basin,)),
            pltpu.SemaphoreType.DMA((n_basin,)),
        ],
        compiler_params=pltpu.CompilerParams(collective_id=0, has_side_effects=True),
    )(runoff, travel_time.reshape(1, reaches), weight_x.reshape(1, reaches), send_t, tgt)


def per_device(
    forcings, w_input, w_recur, gate_bias, w_runoff, travel_time, weight_x, drain_basin, drain_reach
):
    basins = lax.axis_size("basin")
    groups = lax.axis_size("order")
    day_count = forcings.shape[0]
    reach_count = forcings.shape[2]
    units = w_recur.shape[1]
    capacity = 2 * reach_count // basins
    slots = basins * capacity
    drain_to = drain_basin[:, 0]
    onehot_drain = (drain_to[:, None] == jnp.arange(basins, dtype=jnp.int32)[None, :]).astype(
        jnp.int32
    )
    slot_index = jnp.sum(jnp.cumsum(onehot_drain, axis=0) * onehot_drain, axis=1) - 1
    flat_slot = drain_to * capacity + slot_index
    send_int = (
        flat_slot[:, None] == jnp.arange(slots, dtype=jnp.int32)[None, :]
    ).astype(jnp.int32)
    groups_k = capacity // 8
    sent_targets = (jnp.dot(drain_reach[:, 0] + 1, send_int) - 1).reshape(basins, groups_k, 8)
    sent_targets = sent_targets.transpose(0, 2, 1).reshape(basins * 8, groups_k)
    send_t = (
        jnp.arange(slots, dtype=jnp.int32)[:, None] == flat_slot[None, :]
    ).astype(jnp.bfloat16)
    send_t = send_t.reshape(basins, groups_k, 8, reach_count).transpose(0, 2, 1, 3)
    send_t = send_t.reshape(basins * 8, groups_k * reach_count)

    runoff = lstm_runoff(forcings, w_input, w_recur, gate_bias, w_runoff)
    return route_chain(runoff, travel_time, weight_x, send_t, sent_targets, groups, basins, capacity)


def solution(mesh):
    return jax.shard_map(
        per_device,
        mesh=mesh,
        in_specs=(
            P(None, None, ("order", "basin")),
            P(),
            P(),
            P(),
            P(),
            P(("order", "basin")),
            P(("order", "basin")),
            P(("order", "basin"), None),
            P(("order", "basin"), None),
        ),
        out_specs=P(None, ("order", "basin")),
        check_vma=False,
    )
```

```python
import functools

import jax
import jax.numpy as jnp
from jax import lax
from jax.experimental import pallas as pl
from jax.experimental.pallas import tpu as pltpu
from jax.sharding import PartitionSpec as P

MESH = pl.DeviceIdType.MESH


def lstm_days(lstm_state, day_block, w_input, w_recur, gate_bias, w_runoff):
    units = w_recur.shape[1]

    def one_day(recurrent, inputs):
        hidden, memory = recurrent
        gate_sums = (
            jnp.dot(w_input, inputs, preferred_element_type=jnp.float32)
            + jnp.dot(w_recur, hidden, preferred_element_type=jnp.float32)
            + gate_bias[:, None]
        )
        ingate = jax.nn.sigmoid(gate_sums[:units])
        forget = jax.nn.sigmoid(gate_sums[units : 2 * units])
        candidate = jnp.tanh(gate_sums[2 * units : 3 * units])
        outgate = jax.nn.sigmoid(gate_sums[3 * units :])
        memory = forget * memory + ingate * candidate
        hidden = (outgate * jnp.tanh(memory)).astype(jnp.bfloat16)
        runoff = jax.nn.softplus(
            jnp.dot(w_runoff, hidden.astype(jnp.float32), precision=lax.Precision.HIGHEST)
        )
        return ((hidden, memory), runoff)

    return lax.scan(one_day, lstm_state, day_block)


def half_tanh_sigmoid(x):
    return 0.5 + 0.5 * jnp.tanh(0.5 * x)


def lstm_kernel(block, forc_ref, w_in_ref, w_rec_ref, bias_ref, w_ro_ref, out_ref, h_scr, c_scr):
    days = forc_ref.shape[0]
    units = w_rec_ref.shape[1]
    reaches = out_ref.shape[1]
    rows = 8
    h_scr[...] = jnp.zeros_like(h_scr)
    c_scr[...] = jnp.zeros_like(c_scr)

    def step(t, cols):
        gates = (
            jnp.dot(w_in_ref[...], forc_ref[t, :, cols], preferred_element_type=jnp.float32)
            + jnp.dot(w_rec_ref[...], h_scr[:, cols], preferred_element_type=jnp.float32)
            + bias_ref[...]
        )
        ingate = half_tanh_sigmoid(gates[:units])
        forget = half_tanh_sigmoid(gates[units : 2 * units])
        candidate = jnp.tanh(gates[2 * units : 3 * units])
        outgate = half_tanh_sigmoid(gates[3 * units :])
        memory = forget * c_scr[:, cols] + ingate * candidate
        hidden = (outgate * jnp.tanh(memory)).astype(jnp.bfloat16)
        c_scr[:, cols] = memory
        h_scr[:, cols] = hidden
        z = jnp.sum(w_ro_ref[...] * hidden.astype(jnp.float32), axis=0, keepdims=True)
        return jnp.maximum(z, 0.0) + jnp.log1p(jnp.exp(-jnp.abs(z)))

    def week(w, carry):
        first = pl.multiple_of(w * rows, rows)
        for j in range(reaches // block):
            cols = pl.ds(j * block, block)
            runoff = [step(first + k, cols) for k in range(rows)]
            out_ref[pl.ds(first, rows), cols] = jnp.concatenate(runoff, axis=0)
        return carry

    lax.fori_loop(0, days // rows, week, 0)


def lstm_runoff(forcings, w_input, w_recur, gate_bias, w_runoff, block=128):
    days, _, reaches = forcings.shape
    units = w_recur.shape[1]
    vmem = pl.BlockSpec(memory_space=pltpu.VMEM)
    return pl.pallas_call(
        functools.partial(lstm_kernel, block),
        out_shape=jax.ShapeDtypeStruct((days, reaches), jnp.float32),
        in_specs=[vmem] * 5,
        out_specs=vmem,
        scratch_shapes=[
            pltpu.VMEM((units, reaches), jnp.bfloat16),
            pltpu.VMEM((units, reaches), jnp.float32),
        ],
    )(forcings, w_input, w_recur, gate_bias[:, None], w_runoff[:, None])


def split2(x):
    hi = x.astype(jnp.bfloat16)
    lo = (x - hi.astype(jnp.float32)).astype(jnp.bfloat16)
    return hi, lo


def route_days(inflow, coef):
    days = inflow.shape[0]
    c0, gain, c2 = coef
    lagged = jnp.zeros_like(c0)
    day_rows = []
    for t in range(days):
        if t > 0:
            lagged = inflow[t - 1 : t, :] + c2 * lagged
        day_rows.append(c0 * inflow[t : t + 1, :] + gain * lagged)
    return jnp.concatenate(day_rows, axis=0)


def chain_kernel(n_order, n_basin, cap, runoff_ref, tt_ref, wx_ref, send_ref, tgt_ref, out_ref,
                 packed, recv, table_ref, tgt_recv, spread, send_sem, recv_sem, tsend_sem, trecv_sem):
    o = lax.axis_index("order")
    b = lax.axis_index("basin")
    days, reaches = runoff_ref.shape
    groups = cap // 8
    rows = 8

    barrier = pltpu.get_barrier_semaphore()

    def greet(row):
        def body(j, carry):
            pl.semaphore_signal(barrier, inc=1, device_id=(row, j), device_id_type=MESH)
            return carry
        lax.fori_loop(0, n_basin, body, 0)

    @pl.when(o > 0)
    def _():
        greet(o - 1)

    @pl.when(o < n_order - 1)
    def _():
        greet(o + 1)

    travel = tt_ref[...]
    weight = wx_ref[...]
    denominator = travel * (1.0 - weight) + 0.5
    coeff_first = (0.5 - travel * weight) / denominator
    coeff_second = (0.5 + travel * weight) / denominator
    recession = (travel * (1.0 - weight) - 0.5) / denominator
    coef = (coeff_first, coeff_first * recession + coeff_second, recession)

    def pack(discharge):
        for p, part in enumerate(split2(discharge)):
            for k in range(groups):
                top = (p * groups + k) * days
                spread[top : top + days, k * reaches : (k + 1) * reaches] = part
        stacked = lax.dot_general(send_ref[...], spread[...], (((1,), (1,)), ((), ())),
                                  preferred_element_type=jnp.float32)
        half = stacked.shape[1] // 2
        packed[...] = stacked[:, :half] + stacked[:, half:]

    spread[...] = jnp.zeros_like(spread)

    @pl.when(o == 0)
    def _():
        discharge = route_days(runoff_ref[...], coef)
        out_ref[...] = discharge
        pack(discharge)

    at_end = jnp.logical_or(o == 0, o == n_order - 1)

    @pl.when(at_end)
    def _():
        pl.semaphore_wait(barrier, n_basin)

    @pl.when(jnp.logical_not(at_end))
    def _():
        pl.semaphore_wait(barrier, 2 * n_basin)

    def target_copy(j, row, peer):
        return pltpu.make_async_remote_copy(
            src_ref=tgt_ref.at[pl.ds(j * rows, rows)],
            dst_ref=tgt_recv.at[pl.ds(row * rows, rows)],
            send_sem=tsend_sem.at[j],
            recv_sem=trecv_sem.at[row],
            device_id=(peer, j),
            device_id_type=MESH,
        )

    def data_copy(j, row, peer):
        return pltpu.make_async_remote_copy(
            src_ref=packed.at[pl.ds(j * rows, rows)],
            dst_ref=recv.at[pl.ds(row * rows, rows)],
            send_sem=send_sem.at[j],
            recv_sem=recv_sem.at[row],
            device_id=(peer, j),
            device_id_type=MESH,
        )

    @pl.when(o < n_order - 1)
    def _():
        def start(j, carry):
            target_copy(j, b, o + 1).start()
            return carry
        lax.fori_loop(0, n_basin, start, 0)

    @pl.when(o > 0)
    def _():
        def got(j, carry):
            target_copy(j, j, o - 1).wait_recv()
            return carry
        lax.fori_loop(0, n_basin, got, 0)
        reach = lax.broadcasted_iota(jnp.int32, (1, reaches), 1)
        for k in range(groups):
            table_ref[:, k * reaches : (k + 1) * reaches] = (
                tgt_recv[:, k : k + 1] == reach
            ).astype(jnp.bfloat16)

        def arrived(j, carry):
            data_copy(j, j, o - 1).wait_recv()
            return carry
        lax.fori_loop(0, n_basin, arrived, 0)
        both = jnp.concatenate(split2(recv[...]), axis=1)
        stacked = lax.dot_general(both, table_ref[...], (((0,), (0,)), ((), ())),
                                  preferred_element_type=jnp.float32)
        half = stacked.shape[0] // 2
        wide = stacked[:half] + stacked[half:]
        arrive = wide[0:days, 0:reaches]
        for k in range(1, groups):
            arrive = arrive + wide[k * days : (k + 1) * days, k * reaches : (k + 1) * reaches]
        discharge = route_days(runoff_ref[...] + arrive, coef)
        out_ref[...] = discharge

        @pl.when(o < n_order - 1)
        def _():
            pack(discharge)

    @pl.when(o < n_order - 1)
    def _():
        def start(j, carry):
            data_copy(j, b, o + 1).start()
            return carry
        lax.fori_loop(0, n_basin, start, 0)

        def finish(j, carry):
            data_copy(j, b, o + 1).wait_send()
            target_copy(j, b, o + 1).wait_send()
            return carry
        lax.fori_loop(0, n_basin, finish, 0)


def route_chain(runoff, travel_time, weight_x, send_t, tgt, n_order, n_basin, cap):
    days, reaches = runoff.shape
    groups = cap // 8
    vmem = pl.BlockSpec(memory_space=pltpu.VMEM)
    return pl.pallas_call(
        functools.partial(chain_kernel, n_order, n_basin, cap),
        out_shape=jax.ShapeDtypeStruct((days, reaches), jnp.float32),
        in_specs=[vmem] * 5,
        out_specs=vmem,
        scratch_shapes=[
            pltpu.VMEM((n_basin * 8, groups * days), jnp.float32),
            pltpu.VMEM((n_basin * 8, groups * days), jnp.float32),
            pltpu.VMEM((n_basin * 8, groups * reaches), jnp.bfloat16),
            pltpu.VMEM((n_basin * 8, groups), jnp.int32),
            pltpu.VMEM((2 * groups * days, groups * reaches), jnp.bfloat16),
            pltpu.SemaphoreType.DMA((n_basin,)),
            pltpu.SemaphoreType.DMA((n_basin,)),
            pltpu.SemaphoreType.DMA((n_basin,)),
            pltpu.SemaphoreType.DMA((n_basin,)),
        ],
        compiler_params=pltpu.CompilerParams(collective_id=0, has_side_effects=True),
    )(runoff, travel_time.reshape(1, reaches), weight_x.reshape(1, reaches), send_t, tgt)


def per_device(
    forcings, w_input, w_recur, gate_bias, w_runoff, travel_time, weight_x, drain_basin, drain_reach
):
    basins = lax.axis_size("basin")
    groups = lax.axis_size("order")
    day_count = forcings.shape[0]
    reach_count = forcings.shape[2]
    units = w_recur.shape[1]
    capacity = 2 * reach_count // basins
    slots = basins * capacity
    drain_to = drain_basin[:, 0]
    onehot_drain = (drain_to[:, None] == jnp.arange(basins, dtype=jnp.int32)[None, :]).astype(
        jnp.int32
    )
    slot_index = jnp.sum(jnp.cumsum(onehot_drain, axis=0) * onehot_drain, axis=1) - 1
    flat_slot = drain_to * capacity + slot_index
    send_int = (
        flat_slot[:, None] == jnp.arange(slots, dtype=jnp.int32)[None, :]
    ).astype(jnp.int32)
    groups_k = capacity // 8
    sent_targets = (jnp.dot(drain_reach[:, 0] + 1, send_int) - 1).reshape(basins, groups_k, 8)
    sent_targets = sent_targets.transpose(0, 2, 1).reshape(basins * 8, groups_k)
    send_t = (
        jnp.arange(slots, dtype=jnp.int32)[:, None] == flat_slot[None, :]
    ).astype(jnp.bfloat16)
    send_t = send_t.reshape(basins, groups_k, 8, reach_count).transpose(0, 2, 1, 3)
    send_t = send_t.reshape(basins * 8, groups_k * reach_count)

    runoff = lstm_runoff(forcings, w_input, w_recur, gate_bias, w_runoff)
    return route_chain(runoff, travel_time, weight_x, send_t, sent_targets, groups, basins, capacity)


def solution(mesh):
    return jax.shard_map(
        per_device,
        mesh=mesh,
        in_specs=(
            P(None, None, ("order", "basin")),
            P(),
            P(),
            P(),
            P(),
            P(("order", "basin")),
            P(("order", "basin")),
            P(("order", "basin"), None),
            P(("order", "basin"), None),
        ),
        out_specs=P(None, ("order", "basin")),
        check_vma=False,
    )
```

```python
import functools

import jax
import jax.numpy as jnp
from jax import lax
from jax.experimental import pallas as pl
from jax.experimental.pallas import tpu as pltpu
from jax.sharding import PartitionSpec as P

MESH = pl.DeviceIdType.MESH


def lstm_days(lstm_state, day_block, w_input, w_recur, gate_bias, w_runoff):
    units = w_recur.shape[1]

    def one_day(recurrent, inputs):
        hidden, memory = recurrent
        gate_sums = (
            jnp.dot(w_input, inputs, preferred_element_type=jnp.float32)
            + jnp.dot(w_recur, hidden, preferred_element_type=jnp.float32)
            + gate_bias[:, None]
        )
        ingate = jax.nn.sigmoid(gate_sums[:units])
        forget = jax.nn.sigmoid(gate_sums[units : 2 * units])
        candidate = jnp.tanh(gate_sums[2 * units : 3 * units])
        outgate = jax.nn.sigmoid(gate_sums[3 * units :])
        memory = forget * memory + ingate * candidate
        hidden = (outgate * jnp.tanh(memory)).astype(jnp.bfloat16)
        runoff = jax.nn.softplus(
            jnp.dot(w_runoff, hidden.astype(jnp.float32), precision=lax.Precision.HIGHEST)
        )
        return ((hidden, memory), runoff)

    return lax.scan(one_day, lstm_state, day_block)


def half_tanh_sigmoid(x):
    return 0.5 + 0.5 * jnp.tanh(0.5 * x)


def lstm_kernel(block, forc_ref, w_in_ref, w_rec_ref, bias_ref, w_ro_ref, out_ref, h_scr, c_scr, run_scr):
    days = forc_ref.shape[0]
    units = w_rec_ref.shape[1]
    reaches = out_ref.shape[1]
    h_scr[...] = jnp.zeros_like(h_scr)
    c_scr[...] = jnp.zeros_like(c_scr)

    def step(t, cols):
        gates = (
            jnp.dot(w_in_ref[...], forc_ref[t, :, cols], preferred_element_type=jnp.float32)
            + jnp.dot(w_rec_ref[...], h_scr[:, cols], preferred_element_type=jnp.float32)
            + bias_ref[...]
        )
        ingate = half_tanh_sigmoid(gates[:units])
        forget = half_tanh_sigmoid(gates[units : 2 * units])
        candidate = jnp.tanh(gates[2 * units : 3 * units])
        outgate = half_tanh_sigmoid(gates[3 * units :])
        memory = forget * c_scr[:, cols] + ingate * candidate
        hidden = (outgate * jnp.tanh(memory)).astype(jnp.bfloat16)
        c_scr[:, cols] = memory
        h_scr[:, cols] = hidden
        z = jnp.sum(w_ro_ref[...] * hidden.astype(jnp.float32), axis=0, keepdims=True)
        return jnp.maximum(z, 0.0) + jnp.log1p(jnp.exp(-jnp.abs(z)))

    def day(t, carry):
        for j in range(reaches // block):
            cols = pl.ds(j * block, block)
            run_scr[t, :, cols] = step(t, cols)
        return carry

    lax.fori_loop(0, days, day, 0)
    for t in range(days):
        out_ref[t : t + 1, :] = run_scr[t]


def lstm_runoff(forcings, w_input, w_recur, gate_bias, w_runoff, block=128):
    days, _, reaches = forcings.shape
    units = w_recur.shape[1]
    vmem = pl.BlockSpec(memory_space=pltpu.VMEM)
    return pl.pallas_call(
        functools.partial(lstm_kernel, block),
        out_shape=jax.ShapeDtypeStruct((days, reaches), jnp.float32),
        in_specs=[vmem] * 5,
        out_specs=vmem,
        scratch_shapes=[
            pltpu.VMEM((units, reaches), jnp.bfloat16),
            pltpu.VMEM((units, reaches), jnp.float32),
            pltpu.VMEM((days, 1, reaches), jnp.float32),
        ],
    )(forcings, w_input, w_recur, gate_bias[:, None], w_runoff[:, None])


def split2(x):
    hi = x.astype(jnp.bfloat16)
    lo = (x - hi.astype(jnp.float32)).astype(jnp.bfloat16)
    return hi, lo


def route_days(inflow, coef):
    days = inflow.shape[0]
    c0, gain, c2 = coef
    lagged = jnp.zeros_like(c0)
    day_rows = []
    for t in range(days):
        if t > 0:
            lagged = inflow[t - 1 : t, :] + c2 * lagged
        day_rows.append(c0 * inflow[t : t + 1, :] + gain * lagged)
    return jnp.concatenate(day_rows, axis=0)


def chain_kernel(n_order, n_basin, cap, runoff_ref, tt_ref, wx_ref, send_ref, tgt_ref, out_ref,
                 packed, recv, table_ref, tgt_recv, spread, send_sem, recv_sem, tsend_sem, trecv_sem):
    o = lax.axis_index("order")
    b = lax.axis_index("basin")
    days, reaches = runoff_ref.shape
    groups = cap // 8
    rows = 8

    barrier = pltpu.get_barrier_semaphore()

    def greet(row):
        def body(j, carry):
            pl.semaphore_signal(barrier, inc=1, device_id=(row, j), device_id_type=MESH)
            return carry
        lax.fori_loop(0, n_basin, body, 0)

    @pl.when(o > 0)
    def _():
        greet(o - 1)

    @pl.when(o < n_order - 1)
    def _():
        greet(o + 1)

    travel = tt_ref[...]
    weight = wx_ref[...]
    denominator = travel * (1.0 - weight) + 0.5
    coeff_first = (0.5 - travel * weight) / denominator
    coeff_second = (0.5 + travel * weight) / denominator
    recession = (travel * (1.0 - weight) - 0.5) / denominator
    coef = (coeff_first, coeff_first * recession + coeff_second, recession)

    def pack(discharge):
        for p, part in enumerate(split2(discharge)):
            for k in range(groups):
                top = (p * groups + k) * days
                spread[top : top + days, k * reaches : (k + 1) * reaches] = part
        stacked = lax.dot_general(send_ref[...], spread[...], (((1,), (1,)), ((), ())),
                                  preferred_element_type=jnp.float32)
        half = stacked.shape[1] // 2
        packed[...] = stacked[:, :half] + stacked[:, half:]

    spread[...] = jnp.zeros_like(spread)

    @pl.when(o == 0)
    def _():
        discharge = route_days(runoff_ref[...], coef)
        out_ref[...] = discharge
        pack(discharge)

    at_end = jnp.logical_or(o == 0, o == n_order - 1)

    @pl.when(at_end)
    def _():
        pl.semaphore_wait(barrier, n_basin)

    @pl.when(jnp.logical_not(at_end))
    def _():
        pl.semaphore_wait(barrier, 2 * n_basin)

    def target_copy(j, row, peer):
        return pltpu.make_async_remote_copy(
            src_ref=tgt_ref.at[pl.ds(j * rows, rows)],
            dst_ref=tgt_recv.at[pl.ds(row * rows, rows)],
            send_sem=tsend_sem.at[j],
            recv_sem=trecv_sem.at[row],
            device_id=(peer, j),
            device_id_type=MESH,
        )

    def data_copy(j, row, peer):
        return pltpu.make_async_remote_copy(
            src_ref=packed.at[pl.ds(j * rows, rows)],
            dst_ref=recv.at[pl.ds(row * rows, rows)],
            send_sem=send_sem.at[j],
            recv_sem=recv_sem.at[row],
            device_id=(peer, j),
            device_id_type=MESH,
        )

    @pl.when(o < n_order - 1)
    def _():
        def start(j, carry):
            target_copy(j, b, o + 1).start()
            return carry
        lax.fori_loop(0, n_basin, start, 0)

    @pl.when(o > 0)
    def _():
        def got(j, carry):
            target_copy(j, j, o - 1).wait_recv()
            return carry
        lax.fori_loop(0, n_basin, got, 0)
        reach = lax.broadcasted_iota(jnp.int32, (1, reaches), 1)
        for k in range(groups):
            table_ref[:, k * reaches : (k + 1) * reaches] = (
                tgt_recv[:, k : k + 1] == reach
            ).astype(jnp.bfloat16)

        def arrived(j, carry):
            data_copy(j, j, o - 1).wait_recv()
            return carry
        lax.fori_loop(0, n_basin, arrived, 0)
        both = jnp.concatenate(split2(recv[...]), axis=1)
        stacked = lax.dot_general(both, table_ref[...], (((0,), (0,)), ((), ())),
                                  preferred_element_type=jnp.float32)
        half = stacked.shape[0] // 2
        wide = stacked[:half] + stacked[half:]
        arrive = wide[0:days, 0:reaches]
        for k in range(1, groups):
            arrive = arrive + wide[k * days : (k + 1) * days, k * reaches : (k + 1) * reaches]
        discharge = route_days(runoff_ref[...] + arrive, coef)
        out_ref[...] = discharge

        @pl.when(o < n_order - 1)
        def _():
            pack(discharge)

    @pl.when(o < n_order - 1)
    def _():
        def start(j, carry):
            data_copy(j, b, o + 1).start()
            return carry
        lax.fori_loop(0, n_basin, start, 0)

        def finish(j, carry):
            data_copy(j, b, o + 1).wait_send()
            target_copy(j, b, o + 1).wait_send()
            return carry
        lax.fori_loop(0, n_basin, finish, 0)


def route_chain(runoff, travel_time, weight_x, send_t, tgt, n_order, n_basin, cap):
    days, reaches = runoff.shape
    groups = cap // 8
    vmem = pl.BlockSpec(memory_space=pltpu.VMEM)
    return pl.pallas_call(
        functools.partial(chain_kernel, n_order, n_basin, cap),
        out_shape=jax.ShapeDtypeStruct((days, reaches), jnp.float32),
        in_specs=[vmem] * 5,
        out_specs=vmem,
        scratch_shapes=[
            pltpu.VMEM((n_basin * 8, groups * days), jnp.float32),
            pltpu.VMEM((n_basin * 8, groups * days), jnp.float32),
            pltpu.VMEM((n_basin * 8, groups * reaches), jnp.bfloat16),
            pltpu.VMEM((n_basin * 8, groups), jnp.int32),
            pltpu.VMEM((2 * groups * days, groups * reaches), jnp.bfloat16),
            pltpu.SemaphoreType.DMA((n_basin,)),
            pltpu.SemaphoreType.DMA((n_basin,)),
            pltpu.SemaphoreType.DMA((n_basin,)),
            pltpu.SemaphoreType.DMA((n_basin,)),
        ],
        compiler_params=pltpu.CompilerParams(collective_id=0, has_side_effects=True),
    )(runoff, travel_time.reshape(1, reaches), weight_x.reshape(1, reaches), send_t, tgt)


def per_device(
    forcings, w_input, w_recur, gate_bias, w_runoff, travel_time, weight_x, drain_basin, drain_reach
):
    basins = lax.axis_size("basin")
    groups = lax.axis_size("order")
    day_count = forcings.shape[0]
    reach_count = forcings.shape[2]
    units = w_recur.shape[1]
    capacity = 2 * reach_count // basins
    slots = basins * capacity
    drain_to = drain_basin[:, 0]
    onehot_drain = (drain_to[:, None] == jnp.arange(basins, dtype=jnp.int32)[None, :]).astype(
        jnp.int32
    )
    slot_index = jnp.sum(jnp.cumsum(onehot_drain, axis=0) * onehot_drain, axis=1) - 1
    flat_slot = drain_to * capacity + slot_index
    send_int = (
        flat_slot[:, None] == jnp.arange(slots, dtype=jnp.int32)[None, :]
    ).astype(jnp.int32)
    groups_k = capacity // 8
    sent_targets = (jnp.dot(drain_reach[:, 0] + 1, send_int) - 1).reshape(basins, groups_k, 8)
    sent_targets = sent_targets.transpose(0, 2, 1).reshape(basins * 8, groups_k)
    send_t = (
        jnp.arange(slots, dtype=jnp.int32)[:, None] == flat_slot[None, :]
    ).astype(jnp.bfloat16)
    send_t = send_t.reshape(basins, groups_k, 8, reach_count).transpose(0, 2, 1, 3)
    send_t = send_t.reshape(basins * 8, groups_k * reach_count)

    runoff = lstm_runoff(forcings, w_input, w_recur, gate_bias, w_runoff)
    return route_chain(runoff, travel_time, weight_x, send_t, sent_targets, groups, basins, capacity)


def solution(mesh):
    return jax.shard_map(
        per_device,
        mesh=mesh,
        in_specs=(
            P(None, None, ("order", "basin")),
            P(),
            P(),
            P(),
            P(),
            P(("order", "basin")),
            P(("order", "basin")),
            P(("order", "basin"), None),
            P(("order", "basin"), None),
        ),
        out_specs=P(None, ("order", "basin")),
        check_vma=False,
    )
```

```python
import functools

import jax
import jax.numpy as jnp
from jax import lax
from jax.experimental import pallas as pl
from jax.experimental.pallas import tpu as pltpu
from jax.sharding import PartitionSpec as P

MESH = pl.DeviceIdType.MESH


def lstm_days(lstm_state, day_block, w_input, w_recur, gate_bias, w_runoff):
    units = w_recur.shape[1]

    def one_day(recurrent, inputs):
        hidden, memory = recurrent
        gate_sums = (
            jnp.dot(w_input, inputs, preferred_element_type=jnp.float32)
            + jnp.dot(w_recur, hidden, preferred_element_type=jnp.float32)
            + gate_bias[:, None]
        )
        ingate = jax.nn.sigmoid(gate_sums[:units])
        forget = jax.nn.sigmoid(gate_sums[units : 2 * units])
        candidate = jnp.tanh(gate_sums[2 * units : 3 * units])
        outgate = jax.nn.sigmoid(gate_sums[3 * units :])
        memory = forget * memory + ingate * candidate
        hidden = (outgate * jnp.tanh(memory)).astype(jnp.bfloat16)
        runoff = jax.nn.softplus(
            jnp.dot(w_runoff, hidden.astype(jnp.float32), precision=lax.Precision.HIGHEST)
        )
        return ((hidden, memory), runoff)

    return lax.scan(one_day, lstm_state, day_block)


def half_tanh_sigmoid(x):
    return 0.5 + 0.5 * jnp.tanh(0.5 * x)


def lstm_kernel(block, forc_ref, w_in_ref, w_rec_ref, bias_ref, w_ro_ref, out_ref, h_scr, c_scr, run_scr):
    days = forc_ref.shape[0]
    units = w_rec_ref.shape[1]
    reaches = out_ref.shape[1]
    h_scr[...] = jnp.zeros_like(h_scr)
    c_scr[...] = jnp.zeros_like(c_scr)

    def step(t, cols):
        gates = (
            jnp.dot(w_in_ref[...], forc_ref[t, :, cols], preferred_element_type=jnp.float32)
            + jnp.dot(w_rec_ref[...], h_scr[:, cols], preferred_element_type=jnp.float32)
            + bias_ref[...]
        )
        ingate = half_tanh_sigmoid(gates[:units])
        forget = half_tanh_sigmoid(gates[units : 2 * units])
        candidate = jnp.tanh(gates[2 * units : 3 * units])
        outgate = half_tanh_sigmoid(gates[3 * units :])
        memory = forget * c_scr[:, cols] + ingate * candidate
        hidden = (outgate * jnp.tanh(memory)).astype(jnp.bfloat16)
        c_scr[:, cols] = memory
        h_scr[:, cols] = hidden
        z = jnp.sum(w_ro_ref[...] * hidden.astype(jnp.float32), axis=0, keepdims=True)
        return jnp.maximum(z, 0.0) + jnp.log1p(jnp.exp(-jnp.abs(z)))

    def day(t, carry):
        for j in range(reaches // block):
            cols = pl.ds(j * block, block)
            run_scr[t, :, cols] = step(t, cols)
        return carry

    lax.fori_loop(0, days, day, 0)
    for t in range(days):
        out_ref[t : t + 1, :] = run_scr[t]


def lstm_runoff(forcings, w_input, w_recur, gate_bias, w_runoff, block=256):
    days, _, reaches = forcings.shape
    units = w_recur.shape[1]
    vmem = pl.BlockSpec(memory_space=pltpu.VMEM)
    return pl.pallas_call(
        functools.partial(lstm_kernel, block),
        out_shape=jax.ShapeDtypeStruct((days, reaches), jnp.float32),
        in_specs=[vmem] * 5,
        out_specs=vmem,
        scratch_shapes=[
            pltpu.VMEM((units, reaches), jnp.bfloat16),
            pltpu.VMEM((units, reaches), jnp.float32),
            pltpu.VMEM((days, 1, reaches), jnp.float32),
        ],
    )(forcings, w_input, w_recur, gate_bias[:, None], w_runoff[:, None])


def split2(x):
    hi = x.astype(jnp.bfloat16)
    lo = (x - hi.astype(jnp.float32)).astype(jnp.bfloat16)
    return hi, lo


def route_days(inflow, coef):
    days = inflow.shape[0]
    c0, gain, c2 = coef
    lagged = jnp.zeros_like(c0)
    day_rows = []
    for t in range(days):
        if t > 0:
            lagged = inflow[t - 1 : t, :] + c2 * lagged
        day_rows.append(c0 * inflow[t : t + 1, :] + gain * lagged)
    return jnp.concatenate(day_rows, axis=0)


def chain_kernel(n_order, n_basin, cap, runoff_ref, tt_ref, wx_ref, send_ref, tgt_ref, out_ref,
                 packed, recv, table_ref, tgt_recv, spread, send_sem, recv_sem, tsend_sem, trecv_sem):
    o = lax.axis_index("order")
    b = lax.axis_index("basin")
    days, reaches = runoff_ref.shape
    groups = cap // 8
    rows = 8

    barrier = pltpu.get_barrier_semaphore()

    def greet(row):
        def body(j, carry):
            pl.semaphore_signal(barrier, inc=1, device_id=(row, j), device_id_type=MESH)
            return carry
        lax.fori_loop(0, n_basin, body, 0)

    @pl.when(o > 0)
    def _():
        greet(o - 1)

    @pl.when(o < n_order - 1)
    def _():
        greet(o + 1)

    travel = tt_ref[...]
    weight = wx_ref[...]
    denominator = travel * (1.0 - weight) + 0.5
    coeff_first = (0.5 - travel * weight) / denominator
    coeff_second = (0.5 + travel * weight) / denominator
    recession = (travel * (1.0 - weight) - 0.5) / denominator
    coef = (coeff_first, coeff_first * recession + coeff_second, recession)

    def pack(discharge):
        for p, part in enumerate(split2(discharge)):
            for k in range(groups):
                top = (p * groups + k) * days
                spread[top : top + days, k * reaches : (k + 1) * reaches] = part
        stacked = lax.dot_general(send_ref[...], spread[...], (((1,), (1,)), ((), ())),
                                  preferred_element_type=jnp.float32)
        half = stacked.shape[1] // 2
        packed[...] = stacked[:, :half] + stacked[:, half:]

    spread[...] = jnp.zeros_like(spread)

    @pl.when(o == 0)
    def _():
        discharge = route_days(runoff_ref[...], coef)
        out_ref[...] = discharge
        pack(discharge)

    at_end = jnp.logical_or(o == 0, o == n_order - 1)

    @pl.when(at_end)
    def _():
        pl.semaphore_wait(barrier, n_basin)

    @pl.when(jnp.logical_not(at_end))
    def _():
        pl.semaphore_wait(barrier, 2 * n_basin)

    def target_copy(j, row, peer):
        return pltpu.make_async_remote_copy(
            src_ref=tgt_ref.at[pl.ds(j * rows, rows)],
            dst_ref=tgt_recv.at[pl.ds(row * rows, rows)],
            send_sem=tsend_sem.at[j],
            recv_sem=trecv_sem.at[row],
            device_id=(peer, j),
            device_id_type=MESH,
        )

    def data_copy(j, row, peer):
        return pltpu.make_async_remote_copy(
            src_ref=packed.at[pl.ds(j * rows, rows)],
            dst_ref=recv.at[pl.ds(row * rows, rows)],
            send_sem=send_sem.at[j],
            recv_sem=recv_sem.at[row],
            device_id=(peer, j),
            device_id_type=MESH,
        )

    @pl.when(o < n_order - 1)
    def _():
        def start(j, carry):
            target_copy(j, b, o + 1).start()
            return carry
        lax.fori_loop(0, n_basin, start, 0)

    @pl.when(o > 0)
    def _():
        def got(j, carry):
            target_copy(j, j, o - 1).wait_recv()
            return carry
        lax.fori_loop(0, n_basin, got, 0)
        reach = lax.broadcasted_iota(jnp.int32, (1, reaches), 1)
        for k in range(groups):
            table_ref[:, k * reaches : (k + 1) * reaches] = (
                tgt_recv[:, k : k + 1] == reach
            ).astype(jnp.bfloat16)

        def arrived(j, carry):
            data_copy(j, j, o - 1).wait_recv()
            return carry
        lax.fori_loop(0, n_basin, arrived, 0)
        both = jnp.concatenate(split2(recv[...]), axis=1)
        stacked = lax.dot_general(both, table_ref[...], (((0,), (0,)), ((), ())),
                                  preferred_element_type=jnp.float32)
        half = stacked.shape[0] // 2
        wide = stacked[:half] + stacked[half:]
        arrive = wide[0:days, 0:reaches]
        for k in range(1, groups):
            arrive = arrive + wide[k * days : (k + 1) * days, k * reaches : (k + 1) * reaches]
        discharge = route_days(runoff_ref[...] + arrive, coef)
        out_ref[...] = discharge

        @pl.when(o < n_order - 1)
        def _():
            pack(discharge)

    @pl.when(o < n_order - 1)
    def _():
        def start(j, carry):
            data_copy(j, b, o + 1).start()
            return carry
        lax.fori_loop(0, n_basin, start, 0)

        def finish(j, carry):
            data_copy(j, b, o + 1).wait_send()
            target_copy(j, b, o + 1).wait_send()
            return carry
        lax.fori_loop(0, n_basin, finish, 0)


def route_chain(runoff, travel_time, weight_x, send_t, tgt, n_order, n_basin, cap):
    days, reaches = runoff.shape
    groups = cap // 8
    vmem = pl.BlockSpec(memory_space=pltpu.VMEM)
    return pl.pallas_call(
        functools.partial(chain_kernel, n_order, n_basin, cap),
        out_shape=jax.ShapeDtypeStruct((days, reaches), jnp.float32),
        in_specs=[vmem] * 5,
        out_specs=vmem,
        scratch_shapes=[
            pltpu.VMEM((n_basin * 8, groups * days), jnp.float32),
            pltpu.VMEM((n_basin * 8, groups * days), jnp.float32),
            pltpu.VMEM((n_basin * 8, groups * reaches), jnp.bfloat16),
            pltpu.VMEM((n_basin * 8, groups), jnp.int32),
            pltpu.VMEM((2 * groups * days, groups * reaches), jnp.bfloat16),
            pltpu.SemaphoreType.DMA((n_basin,)),
            pltpu.SemaphoreType.DMA((n_basin,)),
            pltpu.SemaphoreType.DMA((n_basin,)),
            pltpu.SemaphoreType.DMA((n_basin,)),
        ],
        compiler_params=pltpu.CompilerParams(collective_id=0, has_side_effects=True),
    )(runoff, travel_time.reshape(1, reaches), weight_x.reshape(1, reaches), send_t, tgt)


def per_device(
    forcings, w_input, w_recur, gate_bias, w_runoff, travel_time, weight_x, drain_basin, drain_reach
):
    basins = lax.axis_size("basin")
    groups = lax.axis_size("order")
    day_count = forcings.shape[0]
    reach_count = forcings.shape[2]
    units = w_recur.shape[1]
    capacity = 2 * reach_count // basins
    slots = basins * capacity
    drain_to = drain_basin[:, 0]
    onehot_drain = (drain_to[:, None] == jnp.arange(basins, dtype=jnp.int32)[None, :]).astype(
        jnp.int32
    )
    slot_index = jnp.sum(jnp.cumsum(onehot_drain, axis=0) * onehot_drain, axis=1) - 1
    flat_slot = drain_to * capacity + slot_index
    send_int = (
        flat_slot[:, None] == jnp.arange(slots, dtype=jnp.int32)[None, :]
    ).astype(jnp.int32)
    groups_k = capacity // 8
    sent_targets = (jnp.dot(drain_reach[:, 0] + 1, send_int) - 1).reshape(basins, groups_k, 8)
    sent_targets = sent_targets.transpose(0, 2, 1).reshape(basins * 8, groups_k)
    send_t = (
        jnp.arange(slots, dtype=jnp.int32)[:, None] == flat_slot[None, :]
    ).astype(jnp.bfloat16)
    send_t = send_t.reshape(basins, groups_k, 8, reach_count).transpose(0, 2, 1, 3)
    send_t = send_t.reshape(basins * 8, groups_k * reach_count)

    runoff = lstm_runoff(forcings, w_input, w_recur, gate_bias, w_runoff)
    return route_chain(runoff, travel_time, weight_x, send_t, sent_targets, groups, basins, capacity)


def solution(mesh):
    return jax.shard_map(
        per_device,
        mesh=mesh,
        in_specs=(
            P(None, None, ("order", "basin")),
            P(),
            P(),
            P(),
            P(),
            P(("order", "basin")),
            P(("order", "basin")),
            P(("order", "basin"), None),
            P(("order", "basin"), None),
        ),
        out_specs=P(None, ("order", "basin")),
        check_vma=False,
    )
```

```python
import functools

import jax
import jax.numpy as jnp
from jax import lax
from jax.experimental import pallas as pl
from jax.experimental.pallas import tpu as pltpu
from jax.sharding import PartitionSpec as P

MESH = pl.DeviceIdType.MESH


def lstm_days(lstm_state, day_block, w_input, w_recur, gate_bias, w_runoff):
    units = w_recur.shape[1]

    def one_day(recurrent, inputs):
        hidden, memory = recurrent
        gate_sums = (
            jnp.dot(w_input, inputs, preferred_element_type=jnp.float32)
            + jnp.dot(w_recur, hidden, preferred_element_type=jnp.float32)
            + gate_bias[:, None]
        )
        ingate = jax.nn.sigmoid(gate_sums[:units])
        forget = jax.nn.sigmoid(gate_sums[units : 2 * units])
        candidate = jnp.tanh(gate_sums[2 * units : 3 * units])
        outgate = jax.nn.sigmoid(gate_sums[3 * units :])
        memory = forget * memory + ingate * candidate
        hidden = (outgate * jnp.tanh(memory)).astype(jnp.bfloat16)
        runoff = jax.nn.softplus(
            jnp.dot(w_runoff, hidden.astype(jnp.float32), precision=lax.Precision.HIGHEST)
        )
        return ((hidden, memory), runoff)

    return lax.scan(one_day, lstm_state, day_block)


def half_tanh_sigmoid(x):
    return 0.5 + 0.5 * jnp.tanh(0.5 * x)


def lstm_kernel(block, forc_ref, w_in_ref, w_rec_ref, bias_ref, w_ro_ref, out_ref, h_scr, c_scr, run_scr):
    days = forc_ref.shape[0]
    units = w_rec_ref.shape[1]
    reaches = out_ref.shape[1]
    h_scr[...] = jnp.zeros_like(h_scr)
    c_scr[...] = jnp.zeros_like(c_scr)

    def step(t, cols):
        gates = (
            jnp.dot(w_in_ref[...], forc_ref[t, :, cols], preferred_element_type=jnp.float32)
            + jnp.dot(w_rec_ref[...], h_scr[:, cols], preferred_element_type=jnp.float32)
            + bias_ref[...]
        )
        ingate = half_tanh_sigmoid(gates[:units])
        forget = half_tanh_sigmoid(gates[units : 2 * units])
        candidate = jnp.tanh(gates[2 * units : 3 * units])
        outgate = half_tanh_sigmoid(gates[3 * units :])
        memory = forget * c_scr[:, cols] + ingate * candidate
        hidden = (outgate * jnp.tanh(memory)).astype(jnp.bfloat16)
        c_scr[:, cols] = memory
        h_scr[:, cols] = hidden
        z = jnp.sum(w_ro_ref[...] * hidden.astype(jnp.float32), axis=0, keepdims=True)
        return jnp.maximum(z, 0.0) + jnp.log1p(jnp.exp(-jnp.abs(z)))

    def day(t, carry):
        for j in range(reaches // block):
            cols = pl.ds(j * block, block)
            run_scr[t, :, cols] = step(t, cols)
        return carry

    lax.fori_loop(0, days, day, 0)
    for t in range(days):
        out_ref[t : t + 1, :] = run_scr[t]


def lstm_runoff(forcings, w_input, w_recur, gate_bias, w_runoff, block=128):
    days, _, reaches = forcings.shape
    units = w_recur.shape[1]
    vmem = pl.BlockSpec(memory_space=pltpu.VMEM)
    return pl.pallas_call(
        functools.partial(lstm_kernel, block),
        out_shape=jax.ShapeDtypeStruct((days, reaches), jnp.float32),
        in_specs=[vmem] * 5,
        out_specs=vmem,
        scratch_shapes=[
            pltpu.VMEM((units, reaches), jnp.bfloat16),
            pltpu.VMEM((units, reaches), jnp.float32),
            pltpu.VMEM((days, 1, reaches), jnp.float32),
        ],
    )(forcings, w_input, w_recur, gate_bias[:, None], w_runoff[:, None])


def split2(x):
    hi = x.astype(jnp.bfloat16)
    lo = (x - hi.astype(jnp.float32)).astype(jnp.bfloat16)
    return hi, lo


def route_days(inflow, coef):
    days = inflow.shape[0]
    c0, gain, c2 = coef
    lagged = jnp.zeros_like(c0)
    day_rows = []
    for t in range(days):
        if t > 0:
            lagged = inflow[t - 1 : t, :] + c2 * lagged
        day_rows.append(c0 * inflow[t : t + 1, :] + gain * lagged)
    return jnp.concatenate(day_rows, axis=0)


def chain_kernel(n_order, n_basin, cap, runoff_ref, tt_ref, wx_ref, drains_ref, out_ref,
                 packed, recv, table_ref, tgt_recv, spread, send_ref, tgt_ref,
                 send_sem, recv_sem, tsend_sem, trecv_sem):
    o = lax.axis_index("order")
    b = lax.axis_index("basin")
    days, reaches = runoff_ref.shape
    groups = cap // 8
    rows = 8

    barrier = pltpu.get_barrier_semaphore()

    def greet(row):
        def body(j, carry):
            pl.semaphore_signal(barrier, inc=1, device_id=(row, j), device_id_type=MESH)
            return carry
        lax.fori_loop(0, n_basin, body, 0)

    @pl.when(o > 0)
    def _():
        greet(o - 1)

    @pl.when(o < n_order - 1)
    def _():
        greet(o + 1)

    drain_to = drains_ref[0:1, :]
    drain_at = drains_ref[1:2, :]
    onehot = (lax.broadcasted_iota(jnp.int32, (n_basin, reaches), 0) == drain_to).astype(jnp.bfloat16)
    earlier = (
        lax.broadcasted_iota(jnp.int32, (reaches, reaches), 0)
        < lax.broadcasted_iota(jnp.int32, (reaches, reaches), 1)
    ).astype(jnp.bfloat16)
    counts = jnp.dot(onehot, earlier, preferred_element_type=jnp.float32)
    slot_index = jnp.sum(counts * onehot.astype(jnp.float32), axis=0, keepdims=True)
    flat_slot = drain_to * cap + slot_index.astype(jnp.int32)
    row = lax.broadcasted_iota(jnp.int32, (n_basin * rows, 1), 0)
    row_base = lax.shift_right_logical(row, 3) * cap + jnp.bitwise_and(row, rows - 1)
    named = (drain_at + 1).astype(jnp.float32)
    for k in range(groups):
        chosen = (row_base + k * rows) == flat_slot
        send_ref[:, k * reaches : (k + 1) * reaches] = chosen.astype(jnp.bfloat16)
        found = jnp.sum(jnp.where(chosen, named, 0.0), axis=1, keepdims=True)
        tgt_ref[:, k : k + 1] = found.astype(jnp.int32) - 1

    travel = tt_ref[...]
    weight = wx_ref[...]
    denominator = travel * (1.0 - weight) + 0.5
    coeff_first = (0.5 - travel * weight) / denominator
    coeff_second = (0.5 + travel * weight) / denominator
    recession = (travel * (1.0 - weight) - 0.5) / denominator
    coef = (coeff_first, coeff_first * recession + coeff_second, recession)

    def pack(discharge):
        for p, part in enumerate(split2(discharge)):
            for k in range(groups):
                top = (p * groups + k) * days
                spread[top : top + days, k * reaches : (k + 1) * reaches] = part
        stacked = lax.dot_general(send_ref[...], spread[...], (((1,), (1,)), ((), ())),
                                  preferred_element_type=jnp.float32)
        half = stacked.shape[1] // 2
        packed[...] = stacked[:, :half] + stacked[:, half:]

    spread[...] = jnp.zeros_like(spread)

    @pl.when(o == 0)
    def _():
        discharge = route_days(runoff_ref[...], coef)
        out_ref[...] = discharge
        pack(discharge)

    at_end = jnp.logical_or(o == 0, o == n_order - 1)

    @pl.when(at_end)
    def _():
        pl.semaphore_wait(barrier, n_basin)

    @pl.when(jnp.logical_not(at_end))
    def _():
        pl.semaphore_wait(barrier, 2 * n_basin)

    def target_copy(j, row, peer):
        return pltpu.make_async_remote_copy(
            src_ref=tgt_ref.at[pl.ds(j * rows, rows)],
            dst_ref=tgt_recv.at[pl.ds(row * rows, rows)],
            send_sem=tsend_sem.at[j],
            recv_sem=trecv_sem.at[row],
            device_id=(peer, j),
            device_id_type=MESH,
        )

    def data_copy(j, row, peer):
        return pltpu.make_async_remote_copy(
            src_ref=packed.at[pl.ds(j * rows, rows)],
            dst_ref=recv.at[pl.ds(row * rows, rows)],
            send_sem=send_sem.at[j],
            recv_sem=recv_sem.at[row],
            device_id=(peer, j),
            device_id_type=MESH,
        )

    @pl.when(o < n_order - 1)
    def _():
        def start(j, carry):
            target_copy(j, b, o + 1).start()
            return carry
        lax.fori_loop(0, n_basin, start, 0)

    @pl.when(o > 0)
    def _():
        def got(j, carry):
            target_copy(j, j, o - 1).wait_recv()
            return carry
        lax.fori_loop(0, n_basin, got, 0)
        reach = lax.broadcasted_iota(jnp.int32, (1, reaches), 1)
        for k in range(groups):
            table_ref[:, k * reaches : (k + 1) * reaches] = (
                tgt_recv[:, k : k + 1] == reach
            ).astype(jnp.bfloat16)

        def arrived(j, carry):
            data_copy(j, j, o - 1).wait_recv()
            return carry
        lax.fori_loop(0, n_basin, arrived, 0)
        both = jnp.concatenate(split2(recv[...]), axis=1)
        stacked = lax.dot_general(both, table_ref[...], (((0,), (0,)), ((), ())),
                                  preferred_element_type=jnp.float32)
        half = stacked.shape[0] // 2
        wide = stacked[:half] + stacked[half:]
        arrive = wide[0:days, 0:reaches]
        for k in range(1, groups):
            arrive = arrive + wide[k * days : (k + 1) * days, k * reaches : (k + 1) * reaches]
        discharge = route_days(runoff_ref[...] + arrive, coef)
        out_ref[...] = discharge

        @pl.when(o < n_order - 1)
        def _():
            pack(discharge)

    @pl.when(o < n_order - 1)
    def _():
        def start(j, carry):
            data_copy(j, b, o + 1).start()
            return carry
        lax.fori_loop(0, n_basin, start, 0)

        def finish(j, carry):
            data_copy(j, b, o + 1).wait_send()
            target_copy(j, b, o + 1).wait_send()
            return carry
        lax.fori_loop(0, n_basin, finish, 0)


def route_chain(runoff, travel_time, weight_x, drains, n_order, n_basin, cap):
    days, reaches = runoff.shape
    groups = cap // 8
    vmem = pl.BlockSpec(memory_space=pltpu.VMEM)
    return pl.pallas_call(
        functools.partial(chain_kernel, n_order, n_basin, cap),
        out_shape=jax.ShapeDtypeStruct((days, reaches), jnp.float32),
        in_specs=[vmem] * 4,
        out_specs=vmem,
        scratch_shapes=[
            pltpu.VMEM((n_basin * 8, groups * days), jnp.float32),
            pltpu.VMEM((n_basin * 8, groups * days), jnp.float32),
            pltpu.VMEM((n_basin * 8, groups * reaches), jnp.bfloat16),
            pltpu.VMEM((n_basin * 8, groups), jnp.int32),
            pltpu.VMEM((2 * groups * days, groups * reaches), jnp.bfloat16),
            pltpu.VMEM((n_basin * 8, groups * reaches), jnp.bfloat16),
            pltpu.VMEM((n_basin * 8, groups), jnp.int32),
            pltpu.SemaphoreType.DMA((n_basin,)),
            pltpu.SemaphoreType.DMA((n_basin,)),
            pltpu.SemaphoreType.DMA((n_basin,)),
            pltpu.SemaphoreType.DMA((n_basin,)),
        ],
        compiler_params=pltpu.CompilerParams(collective_id=0, has_side_effects=True),
    )(runoff, travel_time.reshape(1, reaches), weight_x.reshape(1, reaches), drains)


def per_device(
    forcings, w_input, w_recur, gate_bias, w_runoff, travel_time, weight_x, drain_basin, drain_reach
):
    basins = lax.axis_size("basin")
    groups = lax.axis_size("order")
    reach_count = forcings.shape[2]
    capacity = 2 * reach_count // basins
    drains = jnp.stack([drain_basin[:, 0], drain_reach[:, 0]])
    runoff = lstm_runoff(forcings, w_input, w_recur, gate_bias, w_runoff)
    return route_chain(runoff, travel_time, weight_x, drains, groups, basins, capacity)


def solution(mesh):
    return jax.shard_map(
        per_device,
        mesh=mesh,
        in_specs=(
            P(None, None, ("order", "basin")),
            P(),
            P(),
            P(),
            P(),
            P(("order", "basin")),
            P(("order", "basin")),
            P(("order", "basin"), None),
            P(("order", "basin"), None),
        ),
        out_specs=P(None, ("order", "basin")),
        check_vma=False,
    )
```

```python
import functools

import jax
import jax.numpy as jnp
from jax import lax
from jax.experimental import pallas as pl
from jax.experimental.pallas import tpu as pltpu
from jax.sharding import PartitionSpec as P

MESH = pl.DeviceIdType.MESH


def lstm_days(lstm_state, day_block, w_input, w_recur, gate_bias, w_runoff):
    units = w_recur.shape[1]

    def one_day(recurrent, inputs):
        hidden, memory = recurrent
        gate_sums = (
            jnp.dot(w_input, inputs, preferred_element_type=jnp.float32)
            + jnp.dot(w_recur, hidden, preferred_element_type=jnp.float32)
            + gate_bias[:, None]
        )
        ingate = jax.nn.sigmoid(gate_sums[:units])
        forget = jax.nn.sigmoid(gate_sums[units : 2 * units])
        candidate = jnp.tanh(gate_sums[2 * units : 3 * units])
        outgate = jax.nn.sigmoid(gate_sums[3 * units :])
        memory = forget * memory + ingate * candidate
        hidden = (outgate * jnp.tanh(memory)).astype(jnp.bfloat16)
        runoff = jax.nn.softplus(
            jnp.dot(w_runoff, hidden.astype(jnp.float32), precision=lax.Precision.HIGHEST)
        )
        return ((hidden, memory), runoff)

    return lax.scan(one_day, lstm_state, day_block)


def half_tanh_sigmoid(x):
    return 0.5 + 0.5 * jnp.tanh(0.5 * x)


def lstm_kernel(block, forc_ref, w_in_ref, w_rec_ref, bias_ref, w_ro_ref, out_ref, h_scr, c_scr, run_scr):
    days = forc_ref.shape[0]
    units = w_rec_ref.shape[1]
    reaches = out_ref.shape[1]
    h_scr[...] = jnp.zeros_like(h_scr)
    c_scr[...] = jnp.zeros_like(c_scr)

    def step(t, cols):
        gates = (
            jnp.dot(w_in_ref[...], forc_ref[t, :, cols], preferred_element_type=jnp.float32)
            + jnp.dot(w_rec_ref[...], h_scr[:, cols], preferred_element_type=jnp.float32)
            + bias_ref[...]
        )
        ingate = half_tanh_sigmoid(gates[:units])
        forget = half_tanh_sigmoid(gates[units : 2 * units])
        candidate = jnp.tanh(gates[2 * units : 3 * units])
        outgate = half_tanh_sigmoid(gates[3 * units :])
        memory = forget * c_scr[:, cols] + ingate * candidate
        hidden = (outgate * jnp.tanh(memory)).astype(jnp.bfloat16)
        c_scr[:, cols] = memory
        h_scr[:, cols] = hidden
        z = jnp.sum(w_ro_ref[...] * hidden.astype(jnp.float32), axis=0, keepdims=True)
        return jnp.maximum(z, 0.0) + jnp.log1p(jnp.exp(-jnp.abs(z)))

    def day(t, carry):
        for j in range(reaches // block):
            cols = pl.ds(j * block, block)
            run_scr[t, :, cols] = step(t, cols)
        return carry

    lax.fori_loop(0, days, day, 0)
    for t in range(days):
        out_ref[t : t + 1, :] = run_scr[t]


def lstm_runoff(forcings, w_input, w_recur, gate_bias, w_runoff, block=128):
    days, _, reaches = forcings.shape
    units = w_recur.shape[1]
    vmem = pl.BlockSpec(memory_space=pltpu.VMEM)
    return pl.pallas_call(
        functools.partial(lstm_kernel, block),
        out_shape=jax.ShapeDtypeStruct((days, reaches), jnp.float32),
        in_specs=[vmem] * 5,
        out_specs=vmem,
        scratch_shapes=[
            pltpu.VMEM((units, reaches), jnp.bfloat16),
            pltpu.VMEM((units, reaches), jnp.float32),
            pltpu.VMEM((days, 1, reaches), jnp.float32),
        ],
    )(forcings, w_input, w_recur, gate_bias[:, None], w_runoff[:, None])


def split2(x):
    hi = x.astype(jnp.bfloat16)
    lo = (x - hi.astype(jnp.float32)).astype(jnp.bfloat16)
    return hi, lo


def route_days(inflow, coef):
    days = inflow.shape[0]
    c0, gain, c2 = coef
    day = lax.broadcasted_iota(jnp.int32, inflow.shape, 0)
    lagged = jnp.where(day >= 1, pltpu.roll(inflow, shift=1, axis=0), 0.0)
    power = c2
    step = 1
    while step < days:
        moved = jnp.where(day >= step, pltpu.roll(lagged, shift=step, axis=0), 0.0)
        lagged = lagged + power * moved
        power = power * power
        step *= 2
    return c0 * inflow + gain * lagged


def chain_kernel(n_order, n_basin, cap, runoff_ref, tt_ref, wx_ref, drains_ref, out_ref,
                 packed, recv, table_ref, tgt_recv, spread, send_ref, tgt_ref,
                 send_sem, recv_sem, tsend_sem, trecv_sem):
    o = lax.axis_index("order")
    b = lax.axis_index("basin")
    days, reaches = runoff_ref.shape
    groups = cap // 8
    rows = 8

    barrier = pltpu.get_barrier_semaphore()

    def greet(row):
        def body(j, carry):
            pl.semaphore_signal(barrier, inc=1, device_id=(row, j), device_id_type=MESH)
            return carry
        lax.fori_loop(0, n_basin, body, 0)

    @pl.when(o > 0)
    def _():
        greet(o - 1)

    @pl.when(o < n_order - 1)
    def _():
        greet(o + 1)

    drain_to = drains_ref[0:1, :]
    drain_at = drains_ref[1:2, :]
    onehot = (lax.broadcasted_iota(jnp.int32, (n_basin, reaches), 0) == drain_to).astype(jnp.bfloat16)
    earlier = (
        lax.broadcasted_iota(jnp.int32, (reaches, reaches), 0)
        < lax.broadcasted_iota(jnp.int32, (reaches, reaches), 1)
    ).astype(jnp.bfloat16)
    counts = jnp.dot(onehot, earlier, preferred_element_type=jnp.float32)
    slot_index = jnp.sum(counts * onehot.astype(jnp.float32), axis=0, keepdims=True)
    flat_slot = drain_to * cap + slot_index.astype(jnp.int32)
    row = lax.broadcasted_iota(jnp.int32, (n_basin * rows, 1), 0)
    row_base = lax.shift_right_logical(row, 3) * cap + jnp.bitwise_and(row, rows - 1)
    named = (drain_at + 1).astype(jnp.float32)
    for k in range(groups):
        chosen = (row_base + k * rows) == flat_slot
        send_ref[:, k * reaches : (k + 1) * reaches] = chosen.astype(jnp.bfloat16)
        found = jnp.sum(jnp.where(chosen, named, 0.0), axis=1, keepdims=True)
        tgt_ref[:, k : k + 1] = found.astype(jnp.int32) - 1

    travel = tt_ref[...]
    weight = wx_ref[...]
    denominator = travel * (1.0 - weight) + 0.5
    coeff_first = (0.5 - travel * weight) / denominator
    coeff_second = (0.5 + travel * weight) / denominator
    recession = (travel * (1.0 - weight) - 0.5) / denominator
    coef = (coeff_first, coeff_first * recession + coeff_second, recession)

    def pack(discharge):
        for p, part in enumerate(split2(discharge)):
            for k in range(groups):
                top = (p * groups + k) * days
                spread[top : top + days, k * reaches : (k + 1) * reaches] = part
        stacked = lax.dot_general(send_ref[...], spread[...], (((1,), (1,)), ((), ())),
                                  preferred_element_type=jnp.float32)
        half = stacked.shape[1] // 2
        packed[...] = stacked[:, :half] + stacked[:, half:]

    spread[...] = jnp.zeros_like(spread)

    @pl.when(o == 0)
    def _():
        discharge = route_days(runoff_ref[...], coef)
        out_ref[...] = discharge
        pack(discharge)

    at_end = jnp.logical_or(o == 0, o == n_order - 1)

    @pl.when(at_end)
    def _():
        pl.semaphore_wait(barrier, n_basin)

    @pl.when(jnp.logical_not(at_end))
    def _():
        pl.semaphore_wait(barrier, 2 * n_basin)

    def target_copy(j, row, peer):
        return pltpu.make_async_remote_copy(
            src_ref=tgt_ref.at[pl.ds(j * rows, rows)],
            dst_ref=tgt_recv.at[pl.ds(row * rows, rows)],
            send_sem=tsend_sem.at[j],
            recv_sem=trecv_sem.at[row],
            device_id=(peer, j),
            device_id_type=MESH,
        )

    def data_copy(j, row, peer):
        return pltpu.make_async_remote_copy(
            src_ref=packed.at[pl.ds(j * rows, rows)],
            dst_ref=recv.at[pl.ds(row * rows, rows)],
            send_sem=send_sem.at[j],
            recv_sem=recv_sem.at[row],
            device_id=(peer, j),
            device_id_type=MESH,
        )

    @pl.when(o < n_order - 1)
    def _():
        def start(j, carry):
            target_copy(j, b, o + 1).start()
            return carry
        lax.fori_loop(0, n_basin, start, 0)

    @pl.when(o > 0)
    def _():
        def got(j, carry):
            target_copy(j, j, o - 1).wait_recv()
            return carry
        lax.fori_loop(0, n_basin, got, 0)
        reach = lax.broadcasted_iota(jnp.int32, (1, reaches), 1)
        for k in range(groups):
            table_ref[:, k * reaches : (k + 1) * reaches] = (
                tgt_recv[:, k : k + 1] == reach
            ).astype(jnp.bfloat16)

        def arrived(j, carry):
            data_copy(j, j, o - 1).wait_recv()
            return carry
        lax.fori_loop(0, n_basin, arrived, 0)
        both = jnp.concatenate(split2(recv[...]), axis=1)
        stacked = lax.dot_general(both, table_ref[...], (((0,), (0,)), ((), ())),
                                  preferred_element_type=jnp.float32)
        half = stacked.shape[0] // 2
        wide = stacked[:half] + stacked[half:]
        arrive = wide[0:days, 0:reaches]
        for k in range(1, groups):
            arrive = arrive + wide[k * days : (k + 1) * days, k * reaches : (k + 1) * reaches]
        discharge = route_days(runoff_ref[...] + arrive, coef)
        out_ref[...] = discharge

        @pl.when(o < n_order - 1)
        def _():
            pack(discharge)

    @pl.when(o < n_order - 1)
    def _():
        def start(j, carry):
            data_copy(j, b, o + 1).start()
            return carry
        lax.fori_loop(0, n_basin, start, 0)

        def finish(j, carry):
            data_copy(j, b, o + 1).wait_send()
            target_copy(j, b, o + 1).wait_send()
            return carry
        lax.fori_loop(0, n_basin, finish, 0)


def route_chain(runoff, travel_time, weight_x, drains, n_order, n_basin, cap):
    days, reaches = runoff.shape
    groups = cap // 8
    vmem = pl.BlockSpec(memory_space=pltpu.VMEM)
    return pl.pallas_call(
        functools.partial(chain_kernel, n_order, n_basin, cap),
        out_shape=jax.ShapeDtypeStruct((days, reaches), jnp.float32),
        in_specs=[vmem] * 4,
        out_specs=vmem,
        scratch_shapes=[
            pltpu.VMEM((n_basin * 8, groups * days), jnp.float32),
            pltpu.VMEM((n_basin * 8, groups * days), jnp.float32),
            pltpu.VMEM((n_basin * 8, groups * reaches), jnp.bfloat16),
            pltpu.VMEM((n_basin * 8, groups), jnp.int32),
            pltpu.VMEM((2 * groups * days, groups * reaches), jnp.bfloat16),
            pltpu.VMEM((n_basin * 8, groups * reaches), jnp.bfloat16),
            pltpu.VMEM((n_basin * 8, groups), jnp.int32),
            pltpu.SemaphoreType.DMA((n_basin,)),
            pltpu.SemaphoreType.DMA((n_basin,)),
            pltpu.SemaphoreType.DMA((n_basin,)),
            pltpu.SemaphoreType.DMA((n_basin,)),
        ],
        compiler_params=pltpu.CompilerParams(collective_id=0, has_side_effects=True),
    )(runoff, travel_time.reshape(1, reaches), weight_x.reshape(1, reaches), drains)


def per_device(
    forcings, w_input, w_recur, gate_bias, w_runoff, travel_time, weight_x, drain_basin, drain_reach
):
    basins = lax.axis_size("basin")
    groups = lax.axis_size("order")
    reach_count = forcings.shape[2]
    capacity = 2 * reach_count // basins
    drains = jnp.stack([drain_basin[:, 0], drain_reach[:, 0]])
    runoff = lstm_runoff(forcings, w_input, w_recur, gate_bias, w_runoff)
    return route_chain(runoff, travel_time, weight_x, drains, groups, basins, capacity)


def solution(mesh):
    return jax.shard_map(
        per_device,
        mesh=mesh,
        in_specs=(
            P(None, None, ("order", "basin")),
            P(),
            P(),
            P(),
            P(),
            P(("order", "basin")),
            P(("order", "basin")),
            P(("order", "basin"), None),
            P(("order", "basin"), None),
        ),
        out_specs=P(None, ("order", "basin")),
        check_vma=False,
    )
```

```python
import functools

import jax
import jax.numpy as jnp
from jax import lax
from jax.experimental import pallas as pl
from jax.experimental.pallas import tpu as pltpu
from jax.sharding import PartitionSpec as P

MESH = pl.DeviceIdType.MESH


def lstm_days(lstm_state, day_block, w_input, w_recur, gate_bias, w_runoff):
    units = w_recur.shape[1]

    def one_day(recurrent, inputs):
        hidden, memory = recurrent
        gate_sums = (
            jnp.dot(w_input, inputs, preferred_element_type=jnp.float32)
            + jnp.dot(w_recur, hidden, preferred_element_type=jnp.float32)
            + gate_bias[:, None]
        )
        ingate = jax.nn.sigmoid(gate_sums[:units])
        forget = jax.nn.sigmoid(gate_sums[units : 2 * units])
        candidate = jnp.tanh(gate_sums[2 * units : 3 * units])
        outgate = jax.nn.sigmoid(gate_sums[3 * units :])
        memory = forget * memory + ingate * candidate
        hidden = (outgate * jnp.tanh(memory)).astype(jnp.bfloat16)
        runoff = jax.nn.softplus(
            jnp.dot(w_runoff, hidden.astype(jnp.float32), precision=lax.Precision.HIGHEST)
        )
        return ((hidden, memory), runoff)

    return lax.scan(one_day, lstm_state, day_block)


def half_tanh_sigmoid(x):
    return 0.5 + 0.5 * jnp.tanh(0.5 * x)


def as_columns(row, width):
    hi = row.astype(jnp.bfloat16).astype(jnp.float32)
    mid = (row - hi).astype(jnp.bfloat16).astype(jnp.float32)
    lo = (row - hi - mid).astype(jnp.bfloat16).astype(jnp.float32)
    parts = jnp.concatenate([hi, mid, lo, jnp.zeros((5, row.shape[1]), jnp.float32)], axis=0)
    ones = (lax.broadcasted_iota(jnp.int32, (8, width), 0) < 3).astype(jnp.bfloat16)
    return lax.dot_general(parts.astype(jnp.bfloat16), ones, (((0,), (0,)), ((), ())),
                           preferred_element_type=jnp.float32)


def lstm_kernel(block, forc_ref, w_in_ref, w_rec_ref, bias_ref, w_ro_ref, out_ref, h_scr, c_scr, run_scr):
    days = forc_ref.shape[0]
    units = w_rec_ref.shape[1]
    reaches = out_ref.shape[1]
    h_scr[...] = jnp.zeros_like(h_scr)
    c_scr[...] = jnp.zeros_like(c_scr)
    bias = as_columns(bias_ref[...], block)
    w_ro = as_columns(w_ro_ref[...], block)

    def step(t, cols):
        gates = (
            lax.dot_general(w_in_ref[...], forc_ref[t, :, cols], (((0,), (0,)), ((), ())),
                            preferred_element_type=jnp.float32)
            + jnp.dot(w_rec_ref[...], h_scr[:, cols], preferred_element_type=jnp.float32)
            + bias
        )
        ingate = half_tanh_sigmoid(gates[:units])
        forget = half_tanh_sigmoid(gates[units : 2 * units])
        candidate = jnp.tanh(gates[2 * units : 3 * units])
        outgate = half_tanh_sigmoid(gates[3 * units :])
        memory = forget * c_scr[:, cols] + ingate * candidate
        hidden = (outgate * jnp.tanh(memory)).astype(jnp.bfloat16)
        c_scr[:, cols] = memory
        h_scr[:, cols] = hidden
        z = jnp.sum(w_ro * hidden.astype(jnp.float32), axis=0, keepdims=True)
        return jnp.maximum(z, 0.0) + jnp.log1p(jnp.exp(-jnp.abs(z)))

    def day(t, carry):
        for j in range(reaches // block):
            cols = pl.ds(j * block, block)
            run_scr[t, :, cols] = step(t, cols)
        return carry

    lax.fori_loop(0, days, day, 0)
    for t in range(days):
        out_ref[t : t + 1, :] = run_scr[t]


def lstm_runoff(forcings, w_input, w_recur, gate_bias, w_runoff, block=128):
    days, _, reaches = forcings.shape
    units = w_recur.shape[1]
    vmem = pl.BlockSpec(memory_space=pltpu.VMEM)
    return pl.pallas_call(
        functools.partial(lstm_kernel, block),
        out_shape=jax.ShapeDtypeStruct((days, reaches), jnp.float32),
        in_specs=[vmem] * 5,
        out_specs=vmem,
        scratch_shapes=[
            pltpu.VMEM((units, reaches), jnp.bfloat16),
            pltpu.VMEM((units, reaches), jnp.float32),
            pltpu.VMEM((days, 1, reaches), jnp.float32),
        ],
    )(forcings, w_input.T, w_recur, gate_bias.reshape(1, -1), w_runoff.reshape(1, -1))


def split2(x):
    hi = x.astype(jnp.bfloat16)
    lo = (x - hi.astype(jnp.float32)).astype(jnp.bfloat16)
    return hi, lo


def route_days(inflow, coef):
    days = inflow.shape[0]
    c0, gain, c2 = coef
    day = lax.broadcasted_iota(jnp.int32, inflow.shape, 0)
    lagged = jnp.where(day >= 1, pltpu.roll(inflow, shift=1, axis=0), 0.0)
    power = c2
    step = 1
    while step < days:
        moved = jnp.where(day >= step, pltpu.roll(lagged, shift=step, axis=0), 0.0)
        lagged = lagged + power * moved
        power = power * power
        step *= 2
    return c0 * inflow + gain * lagged


def chain_kernel(n_order, n_basin, cap, runoff_ref, tt_ref, wx_ref, drains_ref, out_ref,
                 packed, recv, table_ref, tgt_recv, spread, send_ref, tgt_ref,
                 send_sem, recv_sem, tsend_sem, trecv_sem):
    o = lax.axis_index("order")
    b = lax.axis_index("basin")
    days, reaches = runoff_ref.shape
    groups = cap // 8
    rows = 8

    barrier = pltpu.get_barrier_semaphore()

    def greet(row):
        def body(j, carry):
            pl.semaphore_signal(barrier, inc=1, device_id=(row, j), device_id_type=MESH)
            return carry
        lax.fori_loop(0, n_basin, body, 0)

    @pl.when(o > 0)
    def _():
        greet(o - 1)

    @pl.when(o < n_order - 1)
    def _():
        greet(o + 1)

    drain_to = drains_ref[0:1, :]
    drain_at = drains_ref[1:2, :]
    onehot = (lax.broadcasted_iota(jnp.int32, (n_basin, reaches), 0) == drain_to).astype(jnp.bfloat16)
    earlier = (
        lax.broadcasted_iota(jnp.int32, (reaches, reaches), 0)
        < lax.broadcasted_iota(jnp.int32, (reaches, reaches), 1)
    ).astype(jnp.bfloat16)
    counts = jnp.dot(onehot, earlier, preferred_element_type=jnp.float32)
    slot_index = jnp.sum(counts * onehot.astype(jnp.float32), axis=0, keepdims=True)
    flat_slot = drain_to * cap + slot_index.astype(jnp.int32)
    row = lax.broadcasted_iota(jnp.int32, (n_basin * rows, 1), 0)
    row_base = lax.shift_right_logical(row, 3) * cap + jnp.bitwise_and(row, rows - 1)
    named = (drain_at + 1).astype(jnp.float32)
    for k in range(groups):
        chosen = (row_base + k * rows) == flat_slot
        send_ref[:, k * reaches : (k + 1) * reaches] = chosen.astype(jnp.bfloat16)
        found = jnp.sum(jnp.where(chosen, named, 0.0), axis=1, keepdims=True)
        tgt_ref[:, k : k + 1] = found.astype(jnp.int32) - 1

    travel = tt_ref[...]
    weight = wx_ref[...]
    denominator = travel * (1.0 - weight) + 0.5
    coeff_first = (0.5 - travel * weight) / denominator
    coeff_second = (0.5 + travel * weight) / denominator
    recession = (travel * (1.0 - weight) - 0.5) / denominator
    coef = (coeff_first, coeff_first * recession + coeff_second, recession)

    def pack(discharge):
        for p, part in enumerate(split2(discharge)):
            for k in range(groups):
                top = (p * groups + k) * days
                spread[top : top + days, k * reaches : (k + 1) * reaches] = part
        stacked = lax.dot_general(send_ref[...], spread[...], (((1,), (1,)), ((), ())),
                                  preferred_element_type=jnp.float32)
        half = stacked.shape[1] // 2
        packed[...] = stacked[:, :half] + stacked[:, half:]

    spread[...] = jnp.zeros_like(spread)

    @pl.when(o == 0)
    def _():
        discharge = route_days(runoff_ref[...], coef)
        out_ref[...] = discharge
        pack(discharge)

    at_end = jnp.logical_or(o == 0, o == n_order - 1)

    @pl.when(at_end)
    def _():
        pl.semaphore_wait(barrier, n_basin)

    @pl.when(jnp.logical_not(at_end))
    def _():
        pl.semaphore_wait(barrier, 2 * n_basin)

    def target_copy(j, row, peer):
        return pltpu.make_async_remote_copy(
            src_ref=tgt_ref.at[pl.ds(j * rows, rows)],
            dst_ref=tgt_recv.at[pl.ds(row * rows, rows)],
            send_sem=tsend_sem.at[j],
            recv_sem=trecv_sem.at[row],
            device_id=(peer, j),
            device_id_type=MESH,
        )

    def data_copy(j, row, peer):
        return pltpu.make_async_remote_copy(
            src_ref=packed.at[pl.ds(j * rows, rows)],
            dst_ref=recv.at[pl.ds(row * rows, rows)],
            send_sem=send_sem.at[j],
            recv_sem=recv_sem.at[row],
            device_id=(peer, j),
            device_id_type=MESH,
        )

    @pl.when(o < n_order - 1)
    def _():
        def start(j, carry):
            target_copy(j, b, o + 1).start()
            return carry
        lax.fori_loop(0, n_basin, start, 0)

    @pl.when(o > 0)
    def _():
        def got(j, carry):
            target_copy(j, j, o - 1).wait_recv()
            return carry
        lax.fori_loop(0, n_basin, got, 0)
        reach = lax.broadcasted_iota(jnp.int32, (1, reaches), 1)
        for k in range(groups):
            table_ref[:, k * reaches : (k + 1) * reaches] = (
                tgt_recv[:, k : k + 1] == reach
            ).astype(jnp.bfloat16)

        def arrived(j, carry):
            data_copy(j, j, o - 1).wait_recv()
            return carry
        lax.fori_loop(0, n_basin, arrived, 0)
        both = jnp.concatenate(split2(recv[...]), axis=1)
        stacked = lax.dot_general(both, table_ref[...], (((0,), (0,)), ((), ())),
                                  preferred_element_type=jnp.float32)
        half = stacked.shape[0] // 2
        wide = stacked[:half] + stacked[half:]
        arrive = wide[0:days, 0:reaches]
        for k in range(1, groups):
            arrive = arrive + wide[k * days : (k + 1) * days, k * reaches : (k + 1) * reaches]
        discharge = route_days(runoff_ref[...] + arrive, coef)
        out_ref[...] = discharge

        @pl.when(o < n_order - 1)
        def _():
            pack(discharge)

    @pl.when(o < n_order - 1)
    def _():
        def start(j, carry):
            data_copy(j, b, o + 1).start()
            return carry
        lax.fori_loop(0, n_basin, start, 0)

        def finish(j, carry):
            data_copy(j, b, o + 1).wait_send()
            target_copy(j, b, o + 1).wait_send()
            return carry
        lax.fori_loop(0, n_basin, finish, 0)


def route_chain(runoff, travel_time, weight_x, drains, n_order, n_basin, cap):
    days, reaches = runoff.shape
    groups = cap // 8
    vmem = pl.BlockSpec(memory_space=pltpu.VMEM)
    return pl.pallas_call(
        functools.partial(chain_kernel, n_order, n_basin, cap),
        out_shape=jax.ShapeDtypeStruct((days, reaches), jnp.float32),
        in_specs=[vmem] * 4,
        out_specs=vmem,
        scratch_shapes=[
            pltpu.VMEM((n_basin * 8, groups * days), jnp.float32),
            pltpu.VMEM((n_basin * 8, groups * days), jnp.float32),
            pltpu.VMEM((n_basin * 8, groups * reaches), jnp.bfloat16),
            pltpu.VMEM((n_basin * 8, groups), jnp.int32),
            pltpu.VMEM((2 * groups * days, groups * reaches), jnp.bfloat16),
            pltpu.VMEM((n_basin * 8, groups * reaches), jnp.bfloat16),
            pltpu.VMEM((n_basin * 8, groups), jnp.int32),
            pltpu.SemaphoreType.DMA((n_basin,)),
            pltpu.SemaphoreType.DMA((n_basin,)),
            pltpu.SemaphoreType.DMA((n_basin,)),
            pltpu.SemaphoreType.DMA((n_basin,)),
        ],
        compiler_params=pltpu.CompilerParams(collective_id=0, has_side_effects=True),
    )(runoff, travel_time.reshape(1, reaches), weight_x.reshape(1, reaches), drains)


def per_device(
    forcings, w_input, w_recur, gate_bias, w_runoff, travel_time, weight_x, drain_basin, drain_reach
):
    basins = lax.axis_size("basin")
    groups = lax.axis_size("order")
    reach_count = forcings.shape[2]
    capacity = 2 * reach_count // basins
    drains = jnp.stack([drain_basin[:, 0], drain_reach[:, 0]])
    runoff = lstm_runoff(forcings, w_input, w_recur, gate_bias, w_runoff)
    return route_chain(runoff, travel_time, weight_x, drains, groups, basins, capacity)


def solution(mesh):
    return jax.shard_map(
        per_device,
        mesh=mesh,
        in_specs=(
            P(None, None, ("order", "basin")),
            P(),
            P(),
            P(),
            P(),
            P(("order", "basin")),
            P(("order", "basin")),
            P(("order", "basin"), None),
            P(("order", "basin"), None),
        ),
        out_specs=P(None, ("order", "basin")),
        check_vma=False,
    )
```

```python
import functools

import jax
import jax.numpy as jnp
from jax import lax
from jax.experimental import pallas as pl
from jax.experimental.pallas import tpu as pltpu
from jax.sharding import PartitionSpec as P

MESH = pl.DeviceIdType.MESH


def lstm_days(lstm_state, day_block, w_input, w_recur, gate_bias, w_runoff):
    units = w_recur.shape[1]

    def one_day(recurrent, inputs):
        hidden, memory = recurrent
        gate_sums = (
            jnp.dot(w_input, inputs, preferred_element_type=jnp.float32)
            + jnp.dot(w_recur, hidden, preferred_element_type=jnp.float32)
            + gate_bias[:, None]
        )
        ingate = jax.nn.sigmoid(gate_sums[:units])
        forget = jax.nn.sigmoid(gate_sums[units : 2 * units])
        candidate = jnp.tanh(gate_sums[2 * units : 3 * units])
        outgate = jax.nn.sigmoid(gate_sums[3 * units :])
        memory = forget * memory + ingate * candidate
        hidden = (outgate * jnp.tanh(memory)).astype(jnp.bfloat16)
        runoff = jax.nn.softplus(
            jnp.dot(w_runoff, hidden.astype(jnp.float32), precision=lax.Precision.HIGHEST)
        )
        return ((hidden, memory), runoff)

    return lax.scan(one_day, lstm_state, day_block)


def half_tanh_sigmoid(x):
    return 0.5 + 0.5 * jnp.tanh(0.5 * x)


def as_columns(row, width):
    hi = row.astype(jnp.bfloat16).astype(jnp.float32)
    mid = (row - hi).astype(jnp.bfloat16).astype(jnp.float32)
    lo = (row - hi - mid).astype(jnp.bfloat16).astype(jnp.float32)
    parts = jnp.concatenate([hi, mid, lo, jnp.zeros((5, row.shape[1]), jnp.float32)], axis=0)
    ones = (lax.broadcasted_iota(jnp.int32, (8, width), 0) < 3).astype(jnp.bfloat16)
    return lax.dot_general(parts.astype(jnp.bfloat16), ones, (((0,), (0,)), ((), ())),
                           preferred_element_type=jnp.float32)


def lstm_kernel(block, forc_ref, w_in_ref, w_rec_ref, bias_ref, w_ro_ref, out_ref, h_scr, c_scr, run_scr):
    days = forc_ref.shape[0]
    units = w_rec_ref.shape[1]
    reaches = out_ref.shape[1]
    h_scr[...] = jnp.zeros_like(h_scr)
    c_scr[...] = jnp.zeros_like(c_scr)
    bias = as_columns(bias_ref[...], block)
    w_ro = as_columns(w_ro_ref[...], block)

    def step(t, cols):
        gates = (
            lax.dot_general(w_in_ref[...], forc_ref[t, :, cols], (((0,), (0,)), ((), ())),
                            preferred_element_type=jnp.float32)
            + jnp.dot(w_rec_ref[...], h_scr[:, cols], preferred_element_type=jnp.float32)
            + bias
        )
        ingate = half_tanh_sigmoid(gates[:units])
        forget = half_tanh_sigmoid(gates[units : 2 * units])
        candidate = jnp.tanh(gates[2 * units : 3 * units])
        outgate = half_tanh_sigmoid(gates[3 * units :])
        memory = forget * c_scr[:, cols] + ingate * candidate
        hidden = (outgate * jnp.tanh(memory)).astype(jnp.bfloat16)
        c_scr[:, cols] = memory
        h_scr[:, cols] = hidden
        z = jnp.sum(w_ro * hidden.astype(jnp.float32), axis=0, keepdims=True)
        return jnp.maximum(z, 0.0) + jnp.log1p(jnp.exp(-jnp.abs(z)))

    def day(t, carry):
        for j in range(reaches // block):
            cols = pl.ds(j * block, block)
            run_scr[t, :, cols] = step(t, cols)
        return carry

    lax.fori_loop(0, days, day, 0)
    for t in range(days):
        out_ref[t : t + 1, :] = run_scr[t]


def lstm_runoff(forcings, w_input, w_recur, gate_bias, w_runoff, block=128):
    days, _, reaches = forcings.shape
    units = w_recur.shape[1]
    vmem = pl.BlockSpec(memory_space=pltpu.VMEM)
    return pl.pallas_call(
        functools.partial(lstm_kernel, block),
        out_shape=jax.ShapeDtypeStruct((days, reaches), jnp.float32),
        in_specs=[vmem] * 5,
        out_specs=vmem,
        scratch_shapes=[
            pltpu.VMEM((units, reaches), jnp.bfloat16),
            pltpu.VMEM((units, reaches), jnp.float32),
            pltpu.VMEM((days, 1, reaches), jnp.float32),
        ],
    )(forcings, w_input.T, w_recur, gate_bias.reshape(1, -1), w_runoff.reshape(1, -1))


def split2(x):
    hi = x.astype(jnp.bfloat16)
    lo = (x - hi.astype(jnp.float32)).astype(jnp.bfloat16)
    return hi, lo


def route_days(inflow, coef):
    days = inflow.shape[0]
    c0, gain, c2 = coef
    day = lax.broadcasted_iota(jnp.int32, inflow.shape, 0)
    lagged = jnp.where(day >= 1, pltpu.roll(inflow, shift=1, axis=0), 0.0)
    power = c2
    step = 1
    while step < days:
        moved = jnp.where(day >= step, pltpu.roll(lagged, shift=step, axis=0), 0.0)
        lagged = lagged + power * moved
        power = power * power
        step *= 2
    return c0 * inflow + gain * lagged


def chain_kernel(n_order, n_basin, cap, runoff_ref, tt_ref, wx_ref, db_ref, dr_ref, out_ref,
                 packed, recv, table_ref, tgt_recv, spread, send_ref, tgt_ref,
                 send_sem, recv_sem, tsend_sem, trecv_sem):
    o = lax.axis_index("order")
    b = lax.axis_index("basin")
    days, reaches = runoff_ref.shape
    groups = cap // 8
    rows = 8

    barrier = pltpu.get_barrier_semaphore()

    def greet(row):
        def body(j, carry):
            pl.semaphore_signal(barrier, inc=1, device_id=(row, j), device_id_type=MESH)
            return carry
        lax.fori_loop(0, n_basin, body, 0)

    @pl.when(o > 0)
    def _():
        greet(o - 1)

    @pl.when(o < n_order - 1)
    def _():
        greet(o + 1)

    drain_to = db_ref[...]
    drain_at = dr_ref[...]
    onehot = (lax.broadcasted_iota(jnp.int32, (n_basin, reaches), 0) == drain_to).astype(jnp.bfloat16)
    earlier = (
        lax.broadcasted_iota(jnp.int32, (reaches, reaches), 0)
        < lax.broadcasted_iota(jnp.int32, (reaches, reaches), 1)
    ).astype(jnp.bfloat16)
    counts = jnp.dot(onehot, earlier, preferred_element_type=jnp.float32)
    slot_index = jnp.sum(counts * onehot.astype(jnp.float32), axis=0, keepdims=True)
    flat_slot = drain_to * cap + slot_index.astype(jnp.int32)
    row = lax.broadcasted_iota(jnp.int32, (n_basin * rows, 1), 0)
    row_base = lax.shift_right_logical(row, 3) * cap + jnp.bitwise_and(row, rows - 1)
    named = (drain_at + 1).astype(jnp.float32)
    for k in range(groups):
        chosen = (row_base + k * rows) == flat_slot
        send_ref[:, k * reaches : (k + 1) * reaches] = chosen.astype(jnp.bfloat16)
        found = jnp.sum(jnp.where(chosen, named, 0.0), axis=1, keepdims=True)
        tgt_ref[:, k : k + 1] = found.astype(jnp.int32) - 1

    travel = tt_ref[...]
    weight = wx_ref[...]
    denominator = travel * (1.0 - weight) + 0.5
    coeff_first = (0.5 - travel * weight) / denominator
    coeff_second = (0.5 + travel * weight) / denominator
    recession = (travel * (1.0 - weight) - 0.5) / denominator
    coef = (coeff_first, coeff_first * recession + coeff_second, recession)

    def pack(discharge):
        for p, part in enumerate(split2(discharge)):
            for k in range(groups):
                top = (p * groups + k) * days
                spread[top : top + days, k * reaches : (k + 1) * reaches] = part
        stacked = lax.dot_general(send_ref[...], spread[...], (((1,), (1,)), ((), ())),
                                  preferred_element_type=jnp.float32)
        half = stacked.shape[1] // 2
        packed[...] = stacked[:, :half] + stacked[:, half:]

    spread[...] = jnp.zeros_like(spread)

    @pl.when(o == 0)
    def _():
        discharge = route_days(runoff_ref[...], coef)
        out_ref[...] = discharge
        pack(discharge)

    at_end = jnp.logical_or(o == 0, o == n_order - 1)

    @pl.when(at_end)
    def _():
        pl.semaphore_wait(barrier, n_basin)

    @pl.when(jnp.logical_not(at_end))
    def _():
        pl.semaphore_wait(barrier, 2 * n_basin)

    def target_copy(j, row, peer):
        return pltpu.make_async_remote_copy(
            src_ref=tgt_ref.at[pl.ds(j * rows, rows)],
            dst_ref=tgt_recv.at[pl.ds(row * rows, rows)],
            send_sem=tsend_sem.at[j],
            recv_sem=trecv_sem.at[row],
            device_id=(peer, j),
            device_id_type=MESH,
        )

    def data_copy(j, row, peer):
        return pltpu.make_async_remote_copy(
            src_ref=packed.at[pl.ds(j * rows, rows)],
            dst_ref=recv.at[pl.ds(row * rows, rows)],
            send_sem=send_sem.at[j],
            recv_sem=recv_sem.at[row],
            device_id=(peer, j),
            device_id_type=MESH,
        )

    @pl.when(o < n_order - 1)
    def _():
        def start(j, carry):
            target_copy(j, b, o + 1).start()
            return carry
        lax.fori_loop(0, n_basin, start, 0)

    @pl.when(o > 0)
    def _():
        def got(j, carry):
            target_copy(j, j, o - 1).wait_recv()
            return carry
        lax.fori_loop(0, n_basin, got, 0)
        reach = lax.broadcasted_iota(jnp.int32, (1, reaches), 1)
        for k in range(groups):
            table_ref[:, k * reaches : (k + 1) * reaches] = (
                tgt_recv[:, k : k + 1] == reach
            ).astype(jnp.bfloat16)

        def arrived(j, carry):
            data_copy(j, j, o - 1).wait_recv()
            return carry
        lax.fori_loop(0, n_basin, arrived, 0)
        both = jnp.concatenate(split2(recv[...]), axis=1)
        stacked = lax.dot_general(both, table_ref[...], (((0,), (0,)), ((), ())),
                                  preferred_element_type=jnp.float32)
        half = stacked.shape[0] // 2
        wide = stacked[:half] + stacked[half:]
        arrive = wide[0:days, 0:reaches]
        for k in range(1, groups):
            arrive = arrive + wide[k * days : (k + 1) * days, k * reaches : (k + 1) * reaches]
        discharge = route_days(runoff_ref[...] + arrive, coef)
        out_ref[...] = discharge

        @pl.when(o < n_order - 1)
        def _():
            pack(discharge)

    @pl.when(o < n_order - 1)
    def _():
        def start(j, carry):
            data_copy(j, b, o + 1).start()
            return carry
        lax.fori_loop(0, n_basin, start, 0)

        def finish(j, carry):
            data_copy(j, b, o + 1).wait_send()
            target_copy(j, b, o + 1).wait_send()
            return carry
        lax.fori_loop(0, n_basin, finish, 0)


def route_chain(runoff, travel_time, weight_x, drain_basin, drain_reach, n_order, n_basin, cap):
    days, reaches = runoff.shape
    groups = cap // 8
    vmem = pl.BlockSpec(memory_space=pltpu.VMEM)
    return pl.pallas_call(
        functools.partial(chain_kernel, n_order, n_basin, cap),
        out_shape=jax.ShapeDtypeStruct((days, reaches), jnp.float32),
        in_specs=[vmem] * 5,
        out_specs=vmem,
        scratch_shapes=[
            pltpu.VMEM((n_basin * 8, groups * days), jnp.float32),
            pltpu.VMEM((n_basin * 8, groups * days), jnp.float32),
            pltpu.VMEM((n_basin * 8, groups * reaches), jnp.bfloat16),
            pltpu.VMEM((n_basin * 8, groups), jnp.int32),
            pltpu.VMEM((2 * groups * days, groups * reaches), jnp.bfloat16),
            pltpu.VMEM((n_basin * 8, groups * reaches), jnp.bfloat16),
            pltpu.VMEM((n_basin * 8, groups), jnp.int32),
            pltpu.SemaphoreType.DMA((n_basin,)),
            pltpu.SemaphoreType.DMA((n_basin,)),
            pltpu.SemaphoreType.DMA((n_basin,)),
            pltpu.SemaphoreType.DMA((n_basin,)),
        ],
        compiler_params=pltpu.CompilerParams(collective_id=0, has_side_effects=True),
    )(runoff, travel_time.reshape(1, reaches), weight_x.reshape(1, reaches),
      drain_basin.reshape(1, reaches), drain_reach.reshape(1, reaches))


def per_device(
    forcings, w_input, w_recur, gate_bias, w_runoff, travel_time, weight_x, drain_basin, drain_reach
):
    basins = lax.axis_size("basin")
    groups = lax.axis_size("order")
    reach_count = forcings.shape[2]
    capacity = 2 * reach_count // basins
    runoff = lstm_runoff(forcings, w_input, w_recur, gate_bias, w_runoff)
    return route_chain(runoff, travel_time, weight_x, drain_basin, drain_reach, groups, basins, capacity)


def solution(mesh):
    return jax.shard_map(
        per_device,
        mesh=mesh,
        in_specs=(
            P(None, None, ("order", "basin")),
            P(),
            P(),
            P(),
            P(),
            P(("order", "basin")),
            P(("order", "basin")),
            P(("order", "basin"), None),
            P(("order", "basin"), None),
        ),
        out_specs=P(None, ("order", "basin")),
        check_vma=False,
    )
```

```python
import functools

import jax
import jax.numpy as jnp
from jax import lax
from jax.experimental import pallas as pl
from jax.experimental.pallas import tpu as pltpu
from jax.sharding import PartitionSpec as P

MESH = pl.DeviceIdType.MESH


def lstm_days(lstm_state, day_block, w_input, w_recur, gate_bias, w_runoff):
    units = w_recur.shape[1]

    def one_day(recurrent, inputs):
        hidden, memory = recurrent
        gate_sums = (
            jnp.dot(w_input, inputs, preferred_element_type=jnp.float32)
            + jnp.dot(w_recur, hidden, preferred_element_type=jnp.float32)
            + gate_bias[:, None]
        )
        ingate = jax.nn.sigmoid(gate_sums[:units])
        forget = jax.nn.sigmoid(gate_sums[units : 2 * units])
        candidate = jnp.tanh(gate_sums[2 * units : 3 * units])
        outgate = jax.nn.sigmoid(gate_sums[3 * units :])
        memory = forget * memory + ingate * candidate
        hidden = (outgate * jnp.tanh(memory)).astype(jnp.bfloat16)
        runoff = jax.nn.softplus(
            jnp.dot(w_runoff, hidden.astype(jnp.float32), precision=lax.Precision.HIGHEST)
        )
        return ((hidden, memory), runoff)

    return lax.scan(one_day, lstm_state, day_block)


def half_tanh_sigmoid(x):
    return 0.5 + 0.5 * jnp.tanh(0.5 * x)


def as_columns(row, width):
    hi = row.astype(jnp.bfloat16).astype(jnp.float32)
    mid = (row - hi).astype(jnp.bfloat16).astype(jnp.float32)
    lo = (row - hi - mid).astype(jnp.bfloat16).astype(jnp.float32)
    parts = jnp.concatenate([hi, mid, lo, jnp.zeros((5, row.shape[1]), jnp.float32)], axis=0)
    ones = (lax.broadcasted_iota(jnp.int32, (8, width), 0) < 3).astype(jnp.bfloat16)
    return lax.dot_general(parts.astype(jnp.bfloat16), ones, (((0,), (0,)), ((), ())),
                           preferred_element_type=jnp.float32)


def lstm_kernel(block, forc_ref, w_in_ref, w_rec_ref, bias_ref, w_ro_ref, out_ref, h_scr, c_scr, run_scr):
    days = forc_ref.shape[0]
    units = w_rec_ref.shape[1]
    reaches = out_ref.shape[1]
    h_scr[...] = jnp.zeros_like(h_scr)
    c_scr[...] = jnp.zeros_like(c_scr)
    bias = as_columns(bias_ref[...], block)
    w_ro = as_columns(w_ro_ref[...], block)

    def step(t, cols):
        gates = (
            lax.dot_general(w_in_ref[...], forc_ref[t, :, cols], (((0,), (0,)), ((), ())),
                            preferred_element_type=jnp.float32)
            + jnp.dot(w_rec_ref[...], h_scr[:, cols], preferred_element_type=jnp.float32)
            + bias
        )
        ingate = half_tanh_sigmoid(gates[:units])
        forget = half_tanh_sigmoid(gates[units : 2 * units])
        candidate = jnp.tanh(gates[2 * units : 3 * units])
        outgate = half_tanh_sigmoid(gates[3 * units :])
        memory = forget * c_scr[:, cols] + ingate * candidate
        hidden = (outgate * jnp.tanh(memory)).astype(jnp.bfloat16)
        c_scr[:, cols] = memory
        h_scr[:, cols] = hidden
        z = jnp.sum(w_ro * hidden.astype(jnp.float32), axis=0, keepdims=True)
        return jnp.maximum(z, 0.0) + jnp.log1p(jnp.exp(-jnp.abs(z)))

    def day(t, carry):
        for j in range(reaches // block):
            cols = pl.ds(j * block, block)
            run_scr[t, :, cols] = step(t, cols)
        return carry

    lax.fori_loop(0, days, day, 0)
    for t in range(days):
        out_ref[t : t + 1, :] = run_scr[t]


def split2(x):
    hi = x.astype(jnp.bfloat16)
    lo = (x - hi.astype(jnp.float32)).astype(jnp.bfloat16)
    return hi, lo


def route_days(inflow, coef):
    days = inflow.shape[0]
    c0, gain, c2 = coef
    day = lax.broadcasted_iota(jnp.int32, inflow.shape, 0)
    lagged = jnp.where(day >= 1, pltpu.roll(inflow, shift=1, axis=0), 0.0)
    power = c2
    step = 1
    while step < days:
        moved = jnp.where(day >= step, pltpu.roll(lagged, shift=step, axis=0), 0.0)
        lagged = lagged + power * moved
        power = power * power
        step *= 2
    return c0 * inflow + gain * lagged


def chain_kernel(n_order, n_basin, cap, runoff_ref, tt_ref, wx_ref, db_ref, dr_ref, out_ref,
                 packed, recv, table_ref, tgt_recv, spread, send_ref, tgt_ref,
                 send_sem, recv_sem, tsend_sem, trecv_sem, before=None):
    o = lax.axis_index("order")
    b = lax.axis_index("basin")
    days, reaches = runoff_ref.shape
    groups = cap // 8
    rows = 8

    barrier = pltpu.get_barrier_semaphore()

    def greet(row):
        def body(j, carry):
            pl.semaphore_signal(barrier, inc=1, device_id=(row, j), device_id_type=MESH)
            return carry
        lax.fori_loop(0, n_basin, body, 0)

    @pl.when(o > 0)
    def _():
        greet(o - 1)

    @pl.when(o < n_order - 1)
    def _():
        greet(o + 1)

    if before is not None:
        before()
    drain_to = db_ref[...]
    drain_at = dr_ref[...]
    onehot = (lax.broadcasted_iota(jnp.int32, (n_basin, reaches), 0) == drain_to).astype(jnp.bfloat16)
    earlier = (
        lax.broadcasted_iota(jnp.int32, (reaches, reaches), 0)
        < lax.broadcasted_iota(jnp.int32, (reaches, reaches), 1)
    ).astype(jnp.bfloat16)
    counts = jnp.dot(onehot, earlier, preferred_element_type=jnp.float32)
    slot_index = jnp.sum(counts * onehot.astype(jnp.float32), axis=0, keepdims=True)
    flat_slot = drain_to * cap + slot_index.astype(jnp.int32)
    row = lax.broadcasted_iota(jnp.int32, (n_basin * rows, 1), 0)
    row_base = lax.shift_right_logical(row, 3) * cap + jnp.bitwise_and(row, rows - 1)
    named = (drain_at + 1).astype(jnp.float32)
    for k in range(groups):
        chosen = (row_base + k * rows) == flat_slot
        send_ref[:, k * reaches : (k + 1) * reaches] = chosen.astype(jnp.bfloat16)
        found = jnp.sum(jnp.where(chosen, named, 0.0), axis=1, keepdims=True)
        tgt_ref[:, k : k + 1] = found.astype(jnp.int32) - 1

    travel = tt_ref[...]
    weight = wx_ref[...]
    denominator = travel * (1.0 - weight) + 0.5
    coeff_first = (0.5 - travel * weight) / denominator
    coeff_second = (0.5 + travel * weight) / denominator
    recession = (travel * (1.0 - weight) - 0.5) / denominator
    coef = (coeff_first, coeff_first * recession + coeff_second, recession)

    def pack(discharge):
        for p, part in enumerate(split2(discharge)):
            for k in range(groups):
                top = (p * groups + k) * days
                spread[top : top + days, k * reaches : (k + 1) * reaches] = part
        stacked = lax.dot_general(send_ref[...], spread[...], (((1,), (1,)), ((), ())),
                                  preferred_element_type=jnp.float32)
        half = stacked.shape[1] // 2
        packed[...] = stacked[:, :half] + stacked[:, half:]

    spread[...] = jnp.zeros_like(spread)

    @pl.when(o == 0)
    def _():
        discharge = route_days(runoff_ref[...], coef)
        out_ref[...] = discharge
        pack(discharge)

    at_end = jnp.logical_or(o == 0, o == n_order - 1)

    @pl.when(at_end)
    def _():
        pl.semaphore_wait(barrier, n_basin)

    @pl.when(jnp.logical_not(at_end))
    def _():
        pl.semaphore_wait(barrier, 2 * n_basin)

    def target_copy(j, row, peer):
        return pltpu.make_async_remote_copy(
            src_ref=tgt_ref.at[pl.ds(j * rows, rows)],
            dst_ref=tgt_recv.at[pl.ds(row * rows, rows)],
            send_sem=tsend_sem.at[j],
            recv_sem=trecv_sem.at[row],
            device_id=(peer, j),
            device_id_type=MESH,
        )

    def data_copy(j, row, peer):
        return pltpu.make_async_remote_copy(
            src_ref=packed.at[pl.ds(j * rows, rows)],
            dst_ref=recv.at[pl.ds(row * rows, rows)],
            send_sem=send_sem.at[j],
            recv_sem=recv_sem.at[row],
            device_id=(peer, j),
            device_id_type=MESH,
        )

    @pl.when(o < n_order - 1)
    def _():
        def start(j, carry):
            target_copy(j, b, o + 1).start()
            return carry
        lax.fori_loop(0, n_basin, start, 0)

    @pl.when(o > 0)
    def _():
        def got(j, carry):
            target_copy(j, j, o - 1).wait_recv()
            return carry
        lax.fori_loop(0, n_basin, got, 0)
        reach = lax.broadcasted_iota(jnp.int32, (1, reaches), 1)
        for k in range(groups):
            table_ref[:, k * reaches : (k + 1) * reaches] = (
                tgt_recv[:, k : k + 1] == reach
            ).astype(jnp.bfloat16)

        def arrived(j, carry):
            data_copy(j, j, o - 1).wait_recv()
            return carry
        lax.fori_loop(0, n_basin, arrived, 0)
        both = jnp.concatenate(split2(recv[...]), axis=1)
        stacked = lax.dot_general(both, table_ref[...], (((0,), (0,)), ((), ())),
                                  preferred_element_type=jnp.float32)
        half = stacked.shape[0] // 2
        wide = stacked[:half] + stacked[half:]
        arrive = wide[0:days, 0:reaches]
        for k in range(1, groups):
            arrive = arrive + wide[k * days : (k + 1) * days, k * reaches : (k + 1) * reaches]
        discharge = route_days(runoff_ref[...] + arrive, coef)
        out_ref[...] = discharge

        @pl.when(o < n_order - 1)
        def _():
            pack(discharge)

    @pl.when(o < n_order - 1)
    def _():
        def start(j, carry):
            data_copy(j, b, o + 1).start()
            return carry
        lax.fori_loop(0, n_basin, start, 0)

        def finish(j, carry):
            data_copy(j, b, o + 1).wait_send()
            target_copy(j, b, o + 1).wait_send()
            return carry
        lax.fori_loop(0, n_basin, finish, 0)


def river_kernel(block, n_order, n_basin, cap, forc_ref, w_in_ref, w_rec_ref, bias_ref, w_ro_ref,
                 tt_ref, wx_ref, db_ref, dr_ref, out_ref, h_scr, c_scr, run_scr, runoff_ref, *rest):
    def lstm():
        lstm_kernel(block, forc_ref, w_in_ref, w_rec_ref, bias_ref, w_ro_ref, runoff_ref,
                    h_scr, c_scr, run_scr)

    chain_kernel(n_order, n_basin, cap, runoff_ref, tt_ref, wx_ref, db_ref, dr_ref, out_ref, *rest,
                 before=lstm)


def river(forcings, w_input, w_recur, gate_bias, w_runoff, travel_time, weight_x, drain_basin,
          drain_reach, n_order, n_basin, cap, block=128):
    days, _, reaches = forcings.shape
    units = w_recur.shape[1]
    groups = cap // 8
    vmem = pl.BlockSpec(memory_space=pltpu.VMEM)
    return pl.pallas_call(
        functools.partial(river_kernel, block, n_order, n_basin, cap),
        out_shape=jax.ShapeDtypeStruct((days, reaches), jnp.float32),
        in_specs=[vmem] * 9,
        out_specs=vmem,
        scratch_shapes=[
            pltpu.VMEM((units, reaches), jnp.bfloat16),
            pltpu.VMEM((units, reaches), jnp.float32),
            pltpu.VMEM((days, 1, reaches), jnp.float32),
            pltpu.VMEM((days, reaches), jnp.float32),
            pltpu.VMEM((n_basin * 8, groups * days), jnp.float32),
            pltpu.VMEM((n_basin * 8, groups * days), jnp.float32),
            pltpu.VMEM((n_basin * 8, groups * reaches), jnp.bfloat16),
            pltpu.VMEM((n_basin * 8, groups), jnp.int32),
            pltpu.VMEM((2 * groups * days, groups * reaches), jnp.bfloat16),
            pltpu.VMEM((n_basin * 8, groups * reaches), jnp.bfloat16),
            pltpu.VMEM((n_basin * 8, groups), jnp.int32),
            pltpu.SemaphoreType.DMA((n_basin,)),
            pltpu.SemaphoreType.DMA((n_basin,)),
            pltpu.SemaphoreType.DMA((n_basin,)),
            pltpu.SemaphoreType.DMA((n_basin,)),
        ],
        compiler_params=pltpu.CompilerParams(collective_id=0, has_side_effects=True),
    )(forcings, w_input.T, w_recur, gate_bias.reshape(1, -1), w_runoff.reshape(1, -1),
      travel_time.reshape(1, reaches), weight_x.reshape(1, reaches),
      drain_basin.reshape(1, reaches), drain_reach.reshape(1, reaches))


def per_device(
    forcings, w_input, w_recur, gate_bias, w_runoff, travel_time, weight_x, drain_basin, drain_reach
):
    basins = lax.axis_size("basin")
    groups = lax.axis_size("order")
    reach_count = forcings.shape[2]
    capacity = 2 * reach_count // basins
    return river(forcings, w_input, w_recur, gate_bias, w_runoff, travel_time, weight_x,
                 drain_basin, drain_reach, groups, basins, capacity)


def solution(mesh):
    return jax.shard_map(
        per_device,
        mesh=mesh,
        in_specs=(
            P(None, None, ("order", "basin")),
            P(),
            P(),
            P(),
            P(),
            P(("order", "basin")),
            P(("order", "basin")),
            P(("order", "basin"), None),
            P(("order", "basin"), None),
        ),
        out_specs=P(None, ("order", "basin")),
        check_vma=False,
    )
```

```python
import functools

import jax
import jax.numpy as jnp
from jax import lax
from jax.experimental import pallas as pl
from jax.experimental.pallas import tpu as pltpu
from jax.sharding import PartitionSpec as P

MESH = pl.DeviceIdType.MESH


def lstm_days(lstm_state, day_block, w_input, w_recur, gate_bias, w_runoff):
    units = w_recur.shape[1]

    def one_day(recurrent, inputs):
        hidden, memory = recurrent
        gate_sums = (
            jnp.dot(w_input, inputs, preferred_element_type=jnp.float32)
            + jnp.dot(w_recur, hidden, preferred_element_type=jnp.float32)
            + gate_bias[:, None]
        )
        ingate = jax.nn.sigmoid(gate_sums[:units])
        forget = jax.nn.sigmoid(gate_sums[units : 2 * units])
        candidate = jnp.tanh(gate_sums[2 * units : 3 * units])
        outgate = jax.nn.sigmoid(gate_sums[3 * units :])
        memory = forget * memory + ingate * candidate
        hidden = (outgate * jnp.tanh(memory)).astype(jnp.bfloat16)
        runoff = jax.nn.softplus(
            jnp.dot(w_runoff, hidden.astype(jnp.float32), precision=lax.Precision.HIGHEST)
        )
        return ((hidden, memory), runoff)

    return lax.scan(one_day, lstm_state, day_block)


def half_tanh_sigmoid(x):
    return 0.5 + 0.5 * jnp.tanh(0.5 * x)


def as_columns(row, width):
    hi = row.astype(jnp.bfloat16).astype(jnp.float32)
    mid = (row - hi).astype(jnp.bfloat16).astype(jnp.float32)
    lo = (row - hi - mid).astype(jnp.bfloat16).astype(jnp.float32)
    parts = jnp.concatenate([hi, mid, lo, jnp.zeros((5, row.shape[1]), jnp.float32)], axis=0)
    ones = (lax.broadcasted_iota(jnp.int32, (8, width), 0) < 3).astype(jnp.bfloat16)
    return lax.dot_general(parts.astype(jnp.bfloat16), ones, (((0,), (0,)), ((), ())),
                           preferred_element_type=jnp.float32)


def lstm_kernel(block, forc_ref, w_in_ref, w_rec_ref, bias_ref, w_ro_ref, out_ref, h_scr, c_scr, run_scr):
    days = forc_ref.shape[0]
    units = w_rec_ref.shape[1]
    reaches = out_ref.shape[1]
    h_scr[...] = jnp.zeros_like(h_scr)
    c_scr[...] = jnp.zeros_like(c_scr)
    bias = as_columns(bias_ref[...], block)
    w_ro = as_columns(w_ro_ref[...], block)

    def step(t, cols):
        gates = (
            lax.dot_general(w_in_ref[...], forc_ref[t, :, cols], (((0,), (0,)), ((), ())),
                            preferred_element_type=jnp.float32)
            + jnp.dot(w_rec_ref[...], h_scr[:, cols], preferred_element_type=jnp.float32)
            + bias
        )
        ingate = half_tanh_sigmoid(gates[:units])
        forget = half_tanh_sigmoid(gates[units : 2 * units])
        candidate = jnp.tanh(gates[2 * units : 3 * units])
        outgate = half_tanh_sigmoid(gates[3 * units :])
        memory = forget * c_scr[:, cols] + ingate * candidate
        hidden = (outgate * jnp.tanh(memory)).astype(jnp.bfloat16)
        c_scr[:, cols] = memory
        h_scr[:, cols] = hidden
        z = jnp.sum(w_ro * hidden.astype(jnp.float32), axis=0, keepdims=True)
        return jnp.maximum(z, 0.0) + jnp.log1p(jnp.exp(-jnp.abs(z)))

    def day(t, carry):
        for j in range(reaches // block):
            cols = pl.ds(j * block, block)
            run_scr[t, :, cols] = step(t, cols)
        return carry

    lax.fori_loop(0, days, day, 0)
    for t in range(days):
        out_ref[t : t + 1, :] = run_scr[t]


def split2(x):
    hi = x.astype(jnp.bfloat16)
    lo = (x - hi.astype(jnp.float32)).astype(jnp.bfloat16)
    return hi, lo


def route_days(inflow, coef):
    days = inflow.shape[0]
    c0, gain, c2 = coef
    day = lax.broadcasted_iota(jnp.int32, inflow.shape, 0)
    lagged = jnp.where(day >= 1, pltpu.roll(inflow, shift=1, axis=0), 0.0)
    power = c2
    step = 1
    while step < days:
        moved = jnp.where(day >= step, pltpu.roll(lagged, shift=step, axis=0), 0.0)
        lagged = lagged + power * moved
        power = power * power
        step *= 2
    return c0 * inflow + gain * lagged


def chain_kernel(n_order, n_basin, cap, runoff_ref, tt_ref, wx_ref, db_ref, dr_ref, out_ref,
                 packed, recv, table_ref, tgt_recv, spread, send_ref, tgt_ref,
                 send_sem, recv_sem, tsend_sem, trecv_sem, before=None):
    o = lax.axis_index("order")
    b = lax.axis_index("basin")
    days, reaches = runoff_ref.shape
    groups = cap // 8
    rows = 8

    barrier = pltpu.get_barrier_semaphore()

    def greet(row):
        def body(j, carry):
            pl.semaphore_signal(barrier, inc=1, device_id=(row, j), device_id_type=MESH)
            return carry
        lax.fori_loop(0, n_basin, body, 0)

    @pl.when(o > 0)
    def _():
        greet(o - 1)

    @pl.when(o < n_order - 1)
    def _():
        greet(o + 1)

    if before is not None:
        before()
    drain_to = db_ref[...]
    drain_at = dr_ref[...]
    onehot = (lax.broadcasted_iota(jnp.int32, (n_basin, reaches), 0) == drain_to).astype(jnp.bfloat16)
    earlier = (
        lax.broadcasted_iota(jnp.int32, (reaches, reaches), 0)
        < lax.broadcasted_iota(jnp.int32, (reaches, reaches), 1)
    ).astype(jnp.bfloat16)
    counts = jnp.dot(onehot, earlier, preferred_element_type=jnp.float32)
    slot_index = jnp.sum(counts * onehot.astype(jnp.float32), axis=0, keepdims=True)
    flat_slot = drain_to * cap + slot_index.astype(jnp.int32)
    row = lax.broadcasted_iota(jnp.int32, (n_basin * rows, 1), 0)
    row_base = lax.shift_right_logical(row, 3) * cap + jnp.bitwise_and(row, rows - 1)
    named = (drain_at + 1).astype(jnp.float32)
    for k in range(groups):
        chosen = (row_base + k * rows) == flat_slot
        send_ref[:, k * reaches : (k + 1) * reaches] = chosen.astype(jnp.bfloat16)
        found = jnp.sum(jnp.where(chosen, named, 0.0), axis=1, keepdims=True)
        tgt_ref[:, k : k + 1] = found.astype(jnp.int32) - 1

    travel = tt_ref[...]
    weight = wx_ref[...]
    denominator = travel * (1.0 - weight) + 0.5
    coeff_first = (0.5 - travel * weight) / denominator
    coeff_second = (0.5 + travel * weight) / denominator
    recession = (travel * (1.0 - weight) - 0.5) / denominator
    coef = (coeff_first, coeff_first * recession + coeff_second, recession)

    def pack(discharge):
        for p, part in enumerate(split2(discharge)):
            for k in range(groups):
                top = (p * groups + k) * days
                spread[top : top + days, k * reaches : (k + 1) * reaches] = part
        stacked = lax.dot_general(send_ref[...], spread[...], (((1,), (1,)), ((), ())),
                                  preferred_element_type=jnp.float32)
        half = stacked.shape[1] // 2
        packed[...] = stacked[:, :half] + stacked[:, half:]

    spread[...] = jnp.zeros_like(spread)

    at_end = jnp.logical_or(o == 0, o == n_order - 1)

    @pl.when(at_end)
    def _():
        pl.semaphore_wait(barrier, n_basin)

    @pl.when(jnp.logical_not(at_end))
    def _():
        pl.semaphore_wait(barrier, 2 * n_basin)

    def target_copy(j, row, peer):
        return pltpu.make_async_remote_copy(
            src_ref=tgt_ref.at[pl.ds(j * rows, rows)],
            dst_ref=tgt_recv.at[pl.ds(row * rows, rows)],
            send_sem=tsend_sem.at[j],
            recv_sem=trecv_sem.at[row],
            device_id=(peer, j),
            device_id_type=MESH,
        )

    def data_copy(j, row, peer):
        return pltpu.make_async_remote_copy(
            src_ref=packed.at[pl.ds(j * rows, rows)],
            dst_ref=recv.at[pl.ds(row * rows, rows)],
            send_sem=send_sem.at[j],
            recv_sem=recv_sem.at[row],
            device_id=(peer, j),
            device_id_type=MESH,
        )

    @pl.when(o < n_order - 1)
    def _():
        def start(j, carry):
            target_copy(j, b, o + 1).start()
            return carry
        lax.fori_loop(0, n_basin, start, 0)

    @pl.when(o == 0)
    def _():
        discharge = route_days(runoff_ref[...], coef)
        out_ref[...] = discharge
        pack(discharge)

    @pl.when(o > 0)
    def _():
        def got(j, carry):
            target_copy(j, j, o - 1).wait_recv()
            return carry
        lax.fori_loop(0, n_basin, got, 0)
        reach = lax.broadcasted_iota(jnp.int32, (1, reaches), 1)
        for k in range(groups):
            table_ref[:, k * reaches : (k + 1) * reaches] = (
                tgt_recv[:, k : k + 1] == reach
            ).astype(jnp.bfloat16)

        def arrived(j, carry):
            data_copy(j, j, o - 1).wait_recv()
            return carry
        lax.fori_loop(0, n_basin, arrived, 0)
        both = jnp.concatenate(split2(recv[...]), axis=1)
        stacked = lax.dot_general(both, table_ref[...], (((0,), (0,)), ((), ())),
                                  preferred_element_type=jnp.float32)
        half = stacked.shape[0] // 2
        wide = stacked[:half] + stacked[half:]
        arrive = wide[0:days, 0:reaches]
        for k in range(1, groups):
            arrive = arrive + wide[k * days : (k + 1) * days, k * reaches : (k + 1) * reaches]
        discharge = route_days(runoff_ref[...] + arrive, coef)
        out_ref[...] = discharge

        @pl.when(o < n_order - 1)
        def _():
            pack(discharge)

    @pl.when(o < n_order - 1)
    def _():
        def start(j, carry):
            data_copy(j, b, o + 1).start()
            return carry
        lax.fori_loop(0, n_basin, start, 0)

        def finish(j, carry):
            data_copy(j, b, o + 1).wait_send()
            target_copy(j, b, o + 1).wait_send()
            return carry
        lax.fori_loop(0, n_basin, finish, 0)


def river_kernel(block, n_order, n_basin, cap, forc_ref, w_in_ref, w_rec_ref, bias_ref, w_ro_ref,
                 tt_ref, wx_ref, db_ref, dr_ref, out_ref, h_scr, c_scr, run_scr, runoff_ref, *rest):
    def lstm():
        lstm_kernel(block, forc_ref, w_in_ref, w_rec_ref, bias_ref, w_ro_ref, runoff_ref,
                    h_scr, c_scr, run_scr)

    chain_kernel(n_order, n_basin, cap, runoff_ref, tt_ref, wx_ref, db_ref, dr_ref, out_ref, *rest,
                 before=lstm)


def river(forcings, w_input, w_recur, gate_bias, w_runoff, travel_time, weight_x, drain_basin,
          drain_reach, n_order, n_basin, cap, block=128):
    days, _, reaches = forcings.shape
    units = w_recur.shape[1]
    groups = cap // 8
    vmem = pl.BlockSpec(memory_space=pltpu.VMEM)
    return pl.pallas_call(
        functools.partial(river_kernel, block, n_order, n_basin, cap),
        out_shape=jax.ShapeDtypeStruct((days, reaches), jnp.float32),
        in_specs=[vmem] * 9,
        out_specs=vmem,
        scratch_shapes=[
            pltpu.VMEM((units, reaches), jnp.bfloat16),
            pltpu.VMEM((units, reaches), jnp.float32),
            pltpu.VMEM((days, 1, reaches), jnp.float32),
            pltpu.VMEM((days, reaches), jnp.float32),
            pltpu.VMEM((n_basin * 8, groups * days), jnp.float32),
            pltpu.VMEM((n_basin * 8, groups * days), jnp.float32),
            pltpu.VMEM((n_basin * 8, groups * reaches), jnp.bfloat16),
            pltpu.VMEM((n_basin * 8, groups), jnp.int32),
            pltpu.VMEM((2 * groups * days, groups * reaches), jnp.bfloat16),
            pltpu.VMEM((n_basin * 8, groups * reaches), jnp.bfloat16),
            pltpu.VMEM((n_basin * 8, groups), jnp.int32),
            pltpu.SemaphoreType.DMA((n_basin,)),
            pltpu.SemaphoreType.DMA((n_basin,)),
            pltpu.SemaphoreType.DMA((n_basin,)),
            pltpu.SemaphoreType.DMA((n_basin,)),
        ],
        compiler_params=pltpu.CompilerParams(collective_id=0, has_side_effects=True),
    )(forcings, w_input.T, w_recur, gate_bias.reshape(1, -1), w_runoff.reshape(1, -1),
      travel_time.reshape(1, reaches), weight_x.reshape(1, reaches),
      drain_basin.reshape(1, reaches), drain_reach.reshape(1, reaches))


def per_device(
    forcings, w_input, w_recur, gate_bias, w_runoff, travel_time, weight_x, drain_basin, drain_reach
):
    basins = lax.axis_size("basin")
    groups = lax.axis_size("order")
    reach_count = forcings.shape[2]
    capacity = 2 * reach_count // basins
    return river(forcings, w_input, w_recur, gate_bias, w_runoff, travel_time, weight_x,
                 drain_basin, drain_reach, groups, basins, capacity)


def solution(mesh):
    return jax.shard_map(
        per_device,
        mesh=mesh,
        in_specs=(
            P(None, None, ("order", "basin")),
            P(),
            P(),
            P(),
            P(),
            P(("order", "basin")),
            P(("order", "basin")),
            P(("order", "basin"), None),
            P(("order", "basin"), None),
        ),
        out_specs=P(None, ("order", "basin")),
        check_vma=False,
    )
```

```python
import functools

import jax
import jax.numpy as jnp
from jax import lax
from jax.experimental import pallas as pl
from jax.experimental.pallas import tpu as pltpu
from jax.sharding import PartitionSpec as P

MESH = pl.DeviceIdType.MESH


def lstm_days(lstm_state, day_block, w_input, w_recur, gate_bias, w_runoff):
    units = w_recur.shape[1]

    def one_day(recurrent, inputs):
        hidden, memory = recurrent
        gate_sums = (
            jnp.dot(w_input, inputs, preferred_element_type=jnp.float32)
            + jnp.dot(w_recur, hidden, preferred_element_type=jnp.float32)
            + gate_bias[:, None]
        )
        ingate = jax.nn.sigmoid(gate_sums[:units])
        forget = jax.nn.sigmoid(gate_sums[units : 2 * units])
        candidate = jnp.tanh(gate_sums[2 * units : 3 * units])
        outgate = jax.nn.sigmoid(gate_sums[3 * units :])
        memory = forget * memory + ingate * candidate
        hidden = (outgate * jnp.tanh(memory)).astype(jnp.bfloat16)
        runoff = jax.nn.softplus(
            jnp.dot(w_runoff, hidden.astype(jnp.float32), precision=lax.Precision.HIGHEST)
        )
        return ((hidden, memory), runoff)

    return lax.scan(one_day, lstm_state, day_block)


def half_tanh_sigmoid(x):
    return 0.5 + 0.5 * jnp.tanh(0.5 * x)


def as_columns(row, width):
    hi = row.astype(jnp.bfloat16).astype(jnp.float32)
    mid = (row - hi).astype(jnp.bfloat16).astype(jnp.float32)
    lo = (row - hi - mid).astype(jnp.bfloat16).astype(jnp.float32)
    parts = jnp.concatenate([hi, mid, lo, jnp.zeros((5, row.shape[1]), jnp.float32)], axis=0)
    ones = (lax.broadcasted_iota(jnp.int32, (8, width), 0) < 3).astype(jnp.bfloat16)
    return lax.dot_general(parts.astype(jnp.bfloat16), ones, (((0,), (0,)), ((), ())),
                           preferred_element_type=jnp.float32)


def lstm_kernel(block, forc_ref, w_in_ref, w_rec_ref, bias_ref, w_ro_ref, out_ref, h_scr, c_scr, run_scr):
    days = forc_ref.shape[0]
    units = w_rec_ref.shape[1]
    reaches = out_ref.shape[1]
    h_scr[...] = jnp.zeros_like(h_scr)
    c_scr[...] = jnp.zeros_like(c_scr)
    bias = as_columns(bias_ref[...], block)
    w_ro = as_columns(w_ro_ref[...], block)

    def step(t, cols):
        gates = (
            lax.dot_general(w_in_ref[...], forc_ref[t, :, cols], (((0,), (0,)), ((), ())),
                            preferred_element_type=jnp.float32)
            + jnp.dot(w_rec_ref[...], h_scr[:, cols], preferred_element_type=jnp.float32)
            + bias
        )
        ingate = half_tanh_sigmoid(gates[:units])
        forget = half_tanh_sigmoid(gates[units : 2 * units])
        candidate = jnp.tanh(gates[2 * units : 3 * units])
        outgate = half_tanh_sigmoid(gates[3 * units :])
        memory = forget * c_scr[:, cols] + ingate * candidate
        hidden = (outgate * jnp.tanh(memory)).astype(jnp.bfloat16)
        c_scr[:, cols] = memory
        h_scr[:, cols] = hidden
        z = jnp.sum(w_ro * hidden.astype(jnp.float32), axis=0, keepdims=True)
        return jnp.maximum(z, 0.0) + jnp.log1p(jnp.exp(-jnp.abs(z)))

    def day(t, carry):
        for j in range(reaches // block):
            cols = pl.ds(j * block, block)
            run_scr[t, :, cols] = step(t, cols)
        return carry

    lax.fori_loop(0, days, day, 0)
    for t in range(days):
        out_ref[t : t + 1, :] = run_scr[t]


def split2(x):
    hi = x.astype(jnp.bfloat16)
    lo = (x - hi.astype(jnp.float32)).astype(jnp.bfloat16)
    return hi, lo


def route_days(inflow, coef):
    days = inflow.shape[0]
    c0, gain, c2 = coef
    day = lax.broadcasted_iota(jnp.int32, inflow.shape, 0)
    lagged = jnp.where(day >= 1, pltpu.roll(inflow, shift=1, axis=0), 0.0)
    power = c2
    step = 1
    while step < days:
        moved = jnp.where(day >= step, pltpu.roll(lagged, shift=step, axis=0), 0.0)
        lagged = lagged + power * moved
        power = power * power
        step *= 2
    return c0 * inflow + gain * lagged


def chain_kernel(n_order, n_basin, cap, runoff_ref, tt_ref, wx_ref, db_ref, dr_ref, out_ref,
                 packed, recv, table_ref, tgt_recv, spread, send_ref, tgt_ref,
                 send_sem, recv_sem, tsend_sem, trecv_sem, before=None):
    o = lax.axis_index("order")
    b = lax.axis_index("basin")
    days, reaches = runoff_ref.shape
    groups = cap // 8
    rows = 8

    barrier = pltpu.get_barrier_semaphore()

    def greet(row):
        def body(j, carry):
            pl.semaphore_signal(barrier, inc=1, device_id=(row, j), device_id_type=MESH)
            return carry
        lax.fori_loop(0, n_basin, body, 0)

    @pl.when(o > 0)
    def _():
        greet(o - 1)

    @pl.when(o < n_order - 1)
    def _():
        greet(o + 1)

    if before is not None:
        before()
    drain_to = db_ref[...]
    drain_at = dr_ref[...]
    onehot = (lax.broadcasted_iota(jnp.int32, (n_basin, reaches), 0) == drain_to).astype(jnp.bfloat16)
    earlier = (
        lax.broadcasted_iota(jnp.int32, (reaches, reaches), 0)
        < lax.broadcasted_iota(jnp.int32, (reaches, reaches), 1)
    ).astype(jnp.bfloat16)
    counts = jnp.dot(onehot, earlier, preferred_element_type=jnp.float32)
    slot_index = jnp.sum(counts * onehot.astype(jnp.float32), axis=0, keepdims=True)
    flat_slot = drain_to * cap + slot_index.astype(jnp.int32)
    row = lax.broadcasted_iota(jnp.int32, (n_basin * rows, 1), 0)
    row_base = lax.shift_right_logical(row, 3) * cap + jnp.bitwise_and(row, rows - 1)
    named = (drain_at + 1).astype(jnp.float32)
    for k in range(groups):
        chosen = (row_base + k * rows) == flat_slot
        send_ref[:, k * reaches : (k + 1) * reaches] = chosen.astype(jnp.bfloat16)
        found = jnp.sum(jnp.where(chosen, named, 0.0), axis=1, keepdims=True)
        tgt_ref[:, k : k + 1] = found.astype(jnp.int32) - 1

    travel = tt_ref[...]
    weight = wx_ref[...]
    denominator = travel * (1.0 - weight) + 0.5
    coeff_first = (0.5 - travel * weight) / denominator
    coeff_second = (0.5 + travel * weight) / denominator
    recession = (travel * (1.0 - weight) - 0.5) / denominator
    coef = (coeff_first, coeff_first * recession + coeff_second, recession)

    def pack(discharge):
        for p, part in enumerate(split2(discharge)):
            for k in range(groups):
                top = (p * groups + k) * days
                spread[top : top + days, k * reaches : (k + 1) * reaches] = part
        stacked = lax.dot_general(send_ref[...], spread[...], (((1,), (1,)), ((), ())),
                                  preferred_element_type=jnp.float32)
        half = stacked.shape[1] // 2
        packed[...] = stacked[:, :half] + stacked[:, half:]

    spread[...] = jnp.zeros_like(spread)

    at_end = jnp.logical_or(o == 0, o == n_order - 1)

    @pl.when(at_end)
    def _():
        pl.semaphore_wait(barrier, n_basin)

    @pl.when(jnp.logical_not(at_end))
    def _():
        pl.semaphore_wait(barrier, 2 * n_basin)

    def target_copy(j, row, peer):
        return pltpu.make_async_remote_copy(
            src_ref=tgt_ref.at[pl.ds(j * rows, rows)],
            dst_ref=tgt_recv.at[pl.ds(row * rows, rows)],
            send_sem=tsend_sem.at[j],
            recv_sem=trecv_sem.at[row],
            device_id=(peer, j),
            device_id_type=MESH,
        )

    def data_copy(j, row, peer):
        return pltpu.make_async_remote_copy(
            src_ref=packed.at[pl.ds(j * rows, rows)],
            dst_ref=recv.at[pl.ds(row * rows, rows)],
            send_sem=send_sem.at[j],
            recv_sem=recv_sem.at[row],
            device_id=(peer, j),
            device_id_type=MESH,
        )

    @pl.when(o < n_order - 1)
    def _():
        def start(j, carry):
            target_copy(j, b, o + 1).start()
            return carry
        lax.fori_loop(0, n_basin, start, 0)

    @pl.when(o == 0)
    def _():
        discharge = route_days(runoff_ref[...], coef)
        out_ref[...] = discharge
        pack(discharge)

    @pl.when(o > 0)
    def _():
        def got(j, carry):
            target_copy(j, j, o - 1).wait_recv()
            return carry
        lax.fori_loop(0, n_basin, got, 0)
        reach = lax.broadcasted_iota(jnp.int32, (1, reaches), 1)
        for k in range(groups):
            table_ref[:, k * reaches : (k + 1) * reaches] = (
                tgt_recv[:, k : k + 1] == reach
            ).astype(jnp.bfloat16)

        def arrived(j, carry):
            data_copy(j, j, o - 1).wait_recv()
            return carry
        lax.fori_loop(0, n_basin, arrived, 0)
        both = jnp.concatenate(split2(recv[...]), axis=1)
        stacked = lax.dot_general(both, table_ref[...], (((0,), (0,)), ((), ())),
                                  preferred_element_type=jnp.float32)
        half = stacked.shape[0] // 2
        wide = stacked[:half] + stacked[half:]
        arrive = wide[0:days, 0:reaches]
        for k in range(1, groups):
            arrive = arrive + wide[k * days : (k + 1) * days, k * reaches : (k + 1) * reaches]
        discharge = route_days(runoff_ref[...] + arrive, coef)
        out_ref[...] = discharge

        @pl.when(o < n_order - 1)
        def _():
            pack(discharge)

    @pl.when(o < n_order - 1)
    def _():
        def start(j, carry):
            data_copy(j, b, o + 1).start()
            return carry
        lax.fori_loop(0, n_basin, start, 0)

        def finish(j, carry):
            data_copy(j, b, o + 1).wait_send()
            target_copy(j, b, o + 1).wait_send()
            return carry
        lax.fori_loop(0, n_basin, finish, 0)


def river_kernel(block, n_order, n_basin, cap, forc_ref, w_in_ref, w_rec_ref, bias_ref, w_ro_ref,
                 tt_ref, wx_ref, db_ref, dr_ref, out_ref, h_scr, c_scr, run_scr, runoff_ref, *rest):
    def lstm():
        lstm_kernel(block, forc_ref, w_in_ref, w_rec_ref, bias_ref, w_ro_ref, runoff_ref,
                    h_scr, c_scr, run_scr)

    chain_kernel(n_order, n_basin, cap, runoff_ref, tt_ref, wx_ref, db_ref, dr_ref, out_ref, *rest,
                 before=lstm)


def river(forcings, w_input, w_recur, gate_bias, w_runoff, travel_time, weight_x, drain_basin,
          drain_reach, n_order, n_basin, cap, block=64):
    days, _, reaches = forcings.shape
    units = w_recur.shape[1]
    groups = cap // 8
    vmem = pl.BlockSpec(memory_space=pltpu.VMEM)
    return pl.pallas_call(
        functools.partial(river_kernel, block, n_order, n_basin, cap),
        out_shape=jax.ShapeDtypeStruct((days, reaches), jnp.float32),
        in_specs=[vmem] * 9,
        out_specs=vmem,
        scratch_shapes=[
            pltpu.VMEM((units, reaches), jnp.bfloat16),
            pltpu.VMEM((units, reaches), jnp.float32),
            pltpu.VMEM((days, 1, reaches), jnp.float32),
            pltpu.VMEM((days, reaches), jnp.float32),
            pltpu.VMEM((n_basin * 8, groups * days), jnp.float32),
            pltpu.VMEM((n_basin * 8, groups * days), jnp.float32),
            pltpu.VMEM((n_basin * 8, groups * reaches), jnp.bfloat16),
            pltpu.VMEM((n_basin * 8, groups), jnp.int32),
            pltpu.VMEM((2 * groups * days, groups * reaches), jnp.bfloat16),
            pltpu.VMEM((n_basin * 8, groups * reaches), jnp.bfloat16),
            pltpu.VMEM((n_basin * 8, groups), jnp.int32),
            pltpu.SemaphoreType.DMA((n_basin,)),
            pltpu.SemaphoreType.DMA((n_basin,)),
            pltpu.SemaphoreType.DMA((n_basin,)),
            pltpu.SemaphoreType.DMA((n_basin,)),
        ],
        compiler_params=pltpu.CompilerParams(collective_id=0, has_side_effects=True),
    )(forcings, w_input.T, w_recur, gate_bias.reshape(1, -1), w_runoff.reshape(1, -1),
      travel_time.reshape(1, reaches), weight_x.reshape(1, reaches),
      drain_basin.reshape(1, reaches), drain_reach.reshape(1, reaches))


def per_device(
    forcings, w_input, w_recur, gate_bias, w_runoff, travel_time, weight_x, drain_basin, drain_reach
):
    basins = lax.axis_size("basin")
    groups = lax.axis_size("order")
    reach_count = forcings.shape[2]
    capacity = 2 * reach_count // basins
    return river(forcings, w_input, w_recur, gate_bias, w_runoff, travel_time, weight_x,
                 drain_basin, drain_reach, groups, basins, capacity)


def solution(mesh):
    return jax.shard_map(
        per_device,
        mesh=mesh,
        in_specs=(
            P(None, None, ("order", "basin")),
            P(),
            P(),
            P(),
            P(),
            P(("order", "basin")),
            P(("order", "basin")),
            P(("order", "basin"), None),
            P(("order", "basin"), None),
        ),
        out_specs=P(None, ("order", "basin")),
        check_vma=False,
    )
```

```python
import functools

import jax
import jax.numpy as jnp
from jax import lax
from jax.experimental import pallas as pl
from jax.experimental.pallas import tpu as pltpu
from jax.sharding import PartitionSpec as P

MESH = pl.DeviceIdType.MESH


def lstm_days(lstm_state, day_block, w_input, w_recur, gate_bias, w_runoff):
    units = w_recur.shape[1]

    def one_day(recurrent, inputs):
        hidden, memory = recurrent
        gate_sums = (
            jnp.dot(w_input, inputs, preferred_element_type=jnp.float32)
            + jnp.dot(w_recur, hidden, preferred_element_type=jnp.float32)
            + gate_bias[:, None]
        )
        ingate = jax.nn.sigmoid(gate_sums[:units])
        forget = jax.nn.sigmoid(gate_sums[units : 2 * units])
        candidate = jnp.tanh(gate_sums[2 * units : 3 * units])
        outgate = jax.nn.sigmoid(gate_sums[3 * units :])
        memory = forget * memory + ingate * candidate
        hidden = (outgate * jnp.tanh(memory)).astype(jnp.bfloat16)
        runoff = jax.nn.softplus(
            jnp.dot(w_runoff, hidden.astype(jnp.float32), precision=lax.Precision.HIGHEST)
        )
        return ((hidden, memory), runoff)

    return lax.scan(one_day, lstm_state, day_block)


def half_tanh_sigmoid(x):
    return 0.5 + 0.5 * jnp.tanh(0.5 * x)


def as_columns(row, width):
    hi = row.astype(jnp.bfloat16).astype(jnp.float32)
    mid = (row - hi).astype(jnp.bfloat16).astype(jnp.float32)
    lo = (row - hi - mid).astype(jnp.bfloat16).astype(jnp.float32)
    parts = jnp.concatenate([hi, mid, lo, jnp.zeros((5, row.shape[1]), jnp.float32)], axis=0)
    ones = (lax.broadcasted_iota(jnp.int32, (8, width), 0) < 3).astype(jnp.bfloat16)
    return lax.dot_general(parts.astype(jnp.bfloat16), ones, (((0,), (0,)), ((), ())),
                           preferred_element_type=jnp.float32)


def lstm_kernel(block, forc_ref, w_in_ref, w_rec_ref, bias_ref, w_ro_ref, out_ref, h_scr, c_scr, run_scr):
    days = forc_ref.shape[0]
    units = w_rec_ref.shape[1]
    reaches = out_ref.shape[1]
    h_scr[...] = jnp.zeros_like(h_scr)
    c_scr[...] = jnp.zeros_like(c_scr)
    bias = as_columns(bias_ref[...], block)
    w_ro = as_columns(w_ro_ref[...], block)

    def step(t, cols):
        gates = (
            lax.dot_general(w_in_ref[...], forc_ref[t, :, cols], (((0,), (0,)), ((), ())),
                            preferred_element_type=jnp.float32)
            + jnp.dot(w_rec_ref[...], h_scr[:, cols], preferred_element_type=jnp.float32)
            + bias
        )
        ingate = half_tanh_sigmoid(gates[:units])
        forget = half_tanh_sigmoid(gates[units : 2 * units])
        candidate = jnp.tanh(gates[2 * units : 3 * units])
        outgate = half_tanh_sigmoid(gates[3 * units :])
        memory = forget * c_scr[:, cols] + ingate * candidate
        hidden = (outgate * jnp.tanh(memory)).astype(jnp.bfloat16)
        c_scr[:, cols] = memory
        h_scr[:, cols] = hidden
        z = jnp.sum(w_ro * hidden.astype(jnp.float32), axis=0, keepdims=True)
        return jnp.maximum(z, 0.0) + jnp.log1p(jnp.exp(-jnp.abs(z)))

    def day(t, carry):
        for j in range(reaches // block):
            cols = pl.ds(j * block, block)
            run_scr[t, :, cols] = step(t, cols)
        return carry

    lax.fori_loop(0, days, day, 0)
    for t in range(days):
        out_ref[t : t + 1, :] = run_scr[t]


def split2(x):
    hi = x.astype(jnp.bfloat16)
    lo = (x - hi.astype(jnp.float32)).astype(jnp.bfloat16)
    return hi, lo


def route_days(inflow, coef):
    days = inflow.shape[0]
    c0, gain, c2 = coef
    day = lax.broadcasted_iota(jnp.int32, inflow.shape, 0)
    lagged = jnp.where(day >= 1, pltpu.roll(inflow, shift=1, axis=0), 0.0)
    power = c2
    step = 1
    while step < days:
        moved = jnp.where(day >= step, pltpu.roll(lagged, shift=step, axis=0), 0.0)
        lagged = lagged + power * moved
        power = power * power
        step *= 2
    return c0 * inflow + gain * lagged


def chain_kernel(n_order, n_basin, cap, runoff_ref, tt_ref, wx_ref, db_ref, dr_ref, out_ref,
                 packed, recv, table_ref, tgt_recv, spread, send_ref, tgt_ref,
                 send_sem, recv_sem, tsend_sem, trecv_sem, before=None):
    o = lax.axis_index("order")
    b = lax.axis_index("basin")
    days, reaches = runoff_ref.shape
    groups = cap // 8
    rows = 8

    barrier = pltpu.get_barrier_semaphore()

    def greet(row):
        def body(j, carry):
            pl.semaphore_signal(barrier, inc=1, device_id=(row, j), device_id_type=MESH)
            return carry
        lax.fori_loop(0, n_basin, body, 0)

    @pl.when(o > 0)
    def _():
        greet(o - 1)

    @pl.when(o < n_order - 1)
    def _():
        greet(o + 1)

    if before is not None:
        before()
    drain_to = db_ref[...]
    drain_at = dr_ref[...]
    onehot = (lax.broadcasted_iota(jnp.int32, (n_basin, reaches), 0) == drain_to).astype(jnp.bfloat16)
    earlier = (
        lax.broadcasted_iota(jnp.int32, (reaches, reaches), 0)
        < lax.broadcasted_iota(jnp.int32, (reaches, reaches), 1)
    ).astype(jnp.bfloat16)
    counts = jnp.dot(onehot, earlier, preferred_element_type=jnp.float32)
    slot_index = jnp.sum(counts * onehot.astype(jnp.float32), axis=0, keepdims=True)
    flat_slot = drain_to * cap + slot_index.astype(jnp.int32)
    row = lax.broadcasted_iota(jnp.int32, (n_basin * rows, 1), 0)
    row_base = lax.shift_right_logical(row, 3) * cap + jnp.bitwise_and(row, rows - 1)
    named = (drain_at + 1).astype(jnp.float32)
    for k in range(groups):
        chosen = (row_base + k * rows) == flat_slot
        send_ref[:, k * reaches : (k + 1) * reaches] = chosen.astype(jnp.bfloat16)
        found = jnp.sum(jnp.where(chosen, named, 0.0), axis=1, keepdims=True)
        tgt_ref[:, k : k + 1] = found.astype(jnp.int32) - 1

    travel = tt_ref[...]
    weight = wx_ref[...]
    denominator = travel * (1.0 - weight) + 0.5
    coeff_first = (0.5 - travel * weight) / denominator
    coeff_second = (0.5 + travel * weight) / denominator
    recession = (travel * (1.0 - weight) - 0.5) / denominator
    coef = (coeff_first, coeff_first * recession + coeff_second, recession)

    def pack(discharge):
        for p, part in enumerate(split2(discharge)):
            for k in range(groups):
                top = (p * groups + k) * days
                spread[top : top + days, k * reaches : (k + 1) * reaches] = part
        stacked = lax.dot_general(send_ref[...], spread[...], (((1,), (1,)), ((), ())),
                                  preferred_element_type=jnp.float32)
        half = stacked.shape[1] // 2
        packed[...] = stacked[:, :half] + stacked[:, half:]

    spread[...] = jnp.zeros_like(spread)

    at_end = jnp.logical_or(o == 0, o == n_order - 1)

    @pl.when(at_end)
    def _():
        pl.semaphore_wait(barrier, n_basin)

    @pl.when(jnp.logical_not(at_end))
    def _():
        pl.semaphore_wait(barrier, 2 * n_basin)

    def target_copy(j, row, peer):
        return pltpu.make_async_remote_copy(
            src_ref=tgt_ref.at[pl.ds(j * rows, rows)],
            dst_ref=tgt_recv.at[pl.ds(row * rows, rows)],
            send_sem=tsend_sem.at[j],
            recv_sem=trecv_sem.at[row],
            device_id=(peer, j),
            device_id_type=MESH,
        )

    def data_copy(j, row, peer):
        return pltpu.make_async_remote_copy(
            src_ref=packed.at[pl.ds(j * rows, rows)],
            dst_ref=recv.at[pl.ds(row * rows, rows)],
            send_sem=send_sem.at[j],
            recv_sem=recv_sem.at[row],
            device_id=(peer, j),
            device_id_type=MESH,
        )

    @pl.when(o < n_order - 1)
    def _():
        def start(j, carry):
            target_copy(j, b, o + 1).start()
            return carry
        lax.fori_loop(0, n_basin, start, 0)

    @pl.when(o == 0)
    def _():
        discharge = route_days(runoff_ref[...], coef)
        out_ref[...] = discharge
        pack(discharge)

    @pl.when(o > 0)
    def _():
        def got(j, carry):
            target_copy(j, j, o - 1).wait_recv()
            return carry
        lax.fori_loop(0, n_basin, got, 0)
        reach = lax.broadcasted_iota(jnp.int32, (1, reaches), 1)
        for k in range(groups):
            table_ref[:, k * reaches : (k + 1) * reaches] = (
                tgt_recv[:, k : k + 1] == reach
            ).astype(jnp.bfloat16)

        def arrived(j, carry):
            data_copy(j, j, o - 1).wait_recv()
            return carry
        lax.fori_loop(0, n_basin, arrived, 0)
        arrive = None
        for k in range(groups):
            block = jnp.concatenate(split2(recv[:, k * days : (k + 1) * days]), axis=1)
            term = lax.dot_general(block, table_ref[:, k * reaches : (k + 1) * reaches],
                                   (((0,), (0,)), ((), ())), preferred_element_type=jnp.float32)
            term = term[:days] + term[days:]
            arrive = term if arrive is None else arrive + term
        discharge = route_days(runoff_ref[...] + arrive, coef)
        out_ref[...] = discharge

        @pl.when(o < n_order - 1)
        def _():
            pack(discharge)

    @pl.when(o < n_order - 1)
    def _():
        def start(j, carry):
            data_copy(j, b, o + 1).start()
            return carry
        lax.fori_loop(0, n_basin, start, 0)

        def finish(j, carry):
            data_copy(j, b, o + 1).wait_send()
            target_copy(j, b, o + 1).wait_send()
            return carry
        lax.fori_loop(0, n_basin, finish, 0)


def river_kernel(block, n_order, n_basin, cap, forc_ref, w_in_ref, w_rec_ref, bias_ref, w_ro_ref,
                 tt_ref, wx_ref, db_ref, dr_ref, out_ref, h_scr, c_scr, run_scr, runoff_ref, *rest):
    def lstm():
        lstm_kernel(block, forc_ref, w_in_ref, w_rec_ref, bias_ref, w_ro_ref, runoff_ref,
                    h_scr, c_scr, run_scr)

    chain_kernel(n_order, n_basin, cap, runoff_ref, tt_ref, wx_ref, db_ref, dr_ref, out_ref, *rest,
                 before=lstm)


def river(forcings, w_input, w_recur, gate_bias, w_runoff, travel_time, weight_x, drain_basin,
          drain_reach, n_order, n_basin, cap, block=128):
    days, _, reaches = forcings.shape
    units = w_recur.shape[1]
    groups = cap // 8
    vmem = pl.BlockSpec(memory_space=pltpu.VMEM)
    return pl.pallas_call(
        functools.partial(river_kernel, block, n_order, n_basin, cap),
        out_shape=jax.ShapeDtypeStruct((days, reaches), jnp.float32),
        in_specs=[vmem] * 9,
        out_specs=vmem,
        scratch_shapes=[
            pltpu.VMEM((units, reaches), jnp.bfloat16),
            pltpu.VMEM((units, reaches), jnp.float32),
            pltpu.VMEM((days, 1, reaches), jnp.float32),
            pltpu.VMEM((days, reaches), jnp.float32),
            pltpu.VMEM((n_basin * 8, groups * days), jnp.float32),
            pltpu.VMEM((n_basin * 8, groups * days), jnp.float32),
            pltpu.VMEM((n_basin * 8, groups * reaches), jnp.bfloat16),
            pltpu.VMEM((n_basin * 8, groups), jnp.int32),
            pltpu.VMEM((2 * groups * days, groups * reaches), jnp.bfloat16),
            pltpu.VMEM((n_basin * 8, groups * reaches), jnp.bfloat16),
            pltpu.VMEM((n_basin * 8, groups), jnp.int32),
            pltpu.SemaphoreType.DMA((n_basin,)),
            pltpu.SemaphoreType.DMA((n_basin,)),
            pltpu.SemaphoreType.DMA((n_basin,)),
            pltpu.SemaphoreType.DMA((n_basin,)),
        ],
        compiler_params=pltpu.CompilerParams(collective_id=0, has_side_effects=True),
    )(forcings, w_input.T, w_recur, gate_bias.reshape(1, -1), w_runoff.reshape(1, -1),
      travel_time.reshape(1, reaches), weight_x.reshape(1, reaches),
      drain_basin.reshape(1, reaches), drain_reach.reshape(1, reaches))


def per_device(
    forcings, w_input, w_recur, gate_bias, w_runoff, travel_time, weight_x, drain_basin, drain_reach
):
    basins = lax.axis_size("basin")
    groups = lax.axis_size("order")
    reach_count = forcings.shape[2]
    capacity = 2 * reach_count // basins
    return river(forcings, w_input, w_recur, gate_bias, w_runoff, travel_time, weight_x,
                 drain_basin, drain_reach, groups, basins, capacity)


def solution(mesh):
    return jax.shard_map(
        per_device,
        mesh=mesh,
        in_specs=(
            P(None, None, ("order", "basin")),
            P(),
            P(),
            P(),
            P(),
            P(("order", "basin")),
            P(("order", "basin")),
            P(("order", "basin"), None),
            P(("order", "basin"), None),
        ),
        out_specs=P(None, ("order", "basin")),
        check_vma=False,
    )
```

```python
import functools

import jax
import jax.numpy as jnp
from jax import lax
from jax.experimental import pallas as pl
from jax.experimental.pallas import tpu as pltpu
from jax.sharding import PartitionSpec as P

MESH = pl.DeviceIdType.MESH


def lstm_days(lstm_state, day_block, w_input, w_recur, gate_bias, w_runoff):
    units = w_recur.shape[1]

    def one_day(recurrent, inputs):
        hidden, memory = recurrent
        gate_sums = (
            jnp.dot(w_input, inputs, preferred_element_type=jnp.float32)
            + jnp.dot(w_recur, hidden, preferred_element_type=jnp.float32)
            + gate_bias[:, None]
        )
        ingate = jax.nn.sigmoid(gate_sums[:units])
        forget = jax.nn.sigmoid(gate_sums[units : 2 * units])
        candidate = jnp.tanh(gate_sums[2 * units : 3 * units])
        outgate = jax.nn.sigmoid(gate_sums[3 * units :])
        memory = forget * memory + ingate * candidate
        hidden = (outgate * jnp.tanh(memory)).astype(jnp.bfloat16)
        runoff = jax.nn.softplus(
            jnp.dot(w_runoff, hidden.astype(jnp.float32), precision=lax.Precision.HIGHEST)
        )
        return ((hidden, memory), runoff)

    return lax.scan(one_day, lstm_state, day_block)


def half_tanh_sigmoid(x):
    return 0.5 + 0.5 * jnp.tanh(0.5 * x)


def as_columns(row, width):
    hi = row.astype(jnp.bfloat16).astype(jnp.float32)
    mid = (row - hi).astype(jnp.bfloat16).astype(jnp.float32)
    lo = (row - hi - mid).astype(jnp.bfloat16).astype(jnp.float32)
    parts = jnp.concatenate([hi, mid, lo, jnp.zeros((5, row.shape[1]), jnp.float32)], axis=0)
    ones = (lax.broadcasted_iota(jnp.int32, (8, width), 0) < 3).astype(jnp.bfloat16)
    return lax.dot_general(parts.astype(jnp.bfloat16), ones, (((0,), (0,)), ((), ())),
                           preferred_element_type=jnp.float32)


def lstm_kernel(block, forc_ref, w_in_ref, w_rec_ref, bias_ref, w_ro_ref, out_ref, h_scr, c_scr, run_scr):
    days = forc_ref.shape[0]
    units = w_rec_ref.shape[1]
    reaches = out_ref.shape[1]
    h_scr[...] = jnp.zeros_like(h_scr)
    c_scr[...] = jnp.zeros_like(c_scr)
    bias = as_columns(bias_ref[...], block)
    w_ro = as_columns(w_ro_ref[...], block)

    def step(t, cols):
        gates = (
            lax.dot_general(w_in_ref[...], forc_ref[t, :, cols], (((0,), (0,)), ((), ())),
                            preferred_element_type=jnp.float32)
            + jnp.dot(w_rec_ref[...], h_scr[:, cols], preferred_element_type=jnp.float32)
            + bias
        )
        ingate = half_tanh_sigmoid(gates[:units])
        forget = half_tanh_sigmoid(gates[units : 2 * units])
        candidate = jnp.tanh(gates[2 * units : 3 * units])
        outgate = half_tanh_sigmoid(gates[3 * units :])
        memory = forget * c_scr[:, cols] + ingate * candidate
        hidden = (outgate * jnp.tanh(memory)).astype(jnp.bfloat16)
        c_scr[:, cols] = memory
        h_scr[:, cols] = hidden
        z = jnp.sum(w_ro * hidden.astype(jnp.float32), axis=0, keepdims=True)
        return jnp.maximum(z, 0.0) + jnp.log1p(jnp.exp(-jnp.abs(z)))

    def day(t, carry):
        for j in range(reaches // block):
            cols = pl.ds(j * block, block)
            run_scr[t, :, cols] = step(t, cols)
        return carry

    lax.fori_loop(0, days, day, 0)
    for t in range(days):
        out_ref[t : t + 1, :] = run_scr[t]


def split2(x):
    hi = x.astype(jnp.bfloat16)
    lo = (x - hi.astype(jnp.float32)).astype(jnp.bfloat16)
    return hi, lo


def route_days(inflow, coef):
    days = inflow.shape[0]
    c0, gain, c2 = coef
    day = lax.broadcasted_iota(jnp.int32, inflow.shape, 0)
    lagged = jnp.where(day >= 1, pltpu.roll(inflow, shift=1, axis=0), 0.0)
    power = c2
    step = 1
    while step < days:
        moved = jnp.where(day >= step, pltpu.roll(lagged, shift=step, axis=0), 0.0)
        lagged = lagged + power * moved
        power = power * power
        step *= 2
    return c0 * inflow + gain * lagged


def chain_kernel(n_order, n_basin, cap, runoff_ref, tt_ref, wx_ref, db_ref, dr_ref, out_ref,
                 packed, recv, table_ref, tgt_recv, spread, send_ref, tgt_ref,
                 send_sem, recv_sem, tsend_sem, trecv_sem, before=None):
    o = lax.axis_index("order")
    b = lax.axis_index("basin")
    days, reaches = runoff_ref.shape
    groups = cap // 8
    rows = 8

    barrier = pltpu.get_barrier_semaphore()

    def greet(row):
        def body(j, carry):
            pl.semaphore_signal(barrier, inc=1, device_id=(row, j), device_id_type=MESH)
            return carry
        lax.fori_loop(0, n_basin, body, 0)

    @pl.when(o > 0)
    def _():
        greet(o - 1)

    @pl.when(o < n_order - 1)
    def _():
        greet(o + 1)

    if before is not None:
        before()
    drain_to = db_ref[...]
    drain_at = dr_ref[...]
    onehot = (lax.broadcasted_iota(jnp.int32, (n_basin, reaches), 0) == drain_to).astype(jnp.bfloat16)
    earlier = (
        lax.broadcasted_iota(jnp.int32, (reaches, reaches), 0)
        < lax.broadcasted_iota(jnp.int32, (reaches, reaches), 1)
    ).astype(jnp.bfloat16)
    counts = jnp.dot(onehot, earlier, preferred_element_type=jnp.float32)
    slot_index = jnp.sum(counts * onehot.astype(jnp.float32), axis=0, keepdims=True)
    flat_slot = drain_to * cap + slot_index.astype(jnp.int32)
    row = lax.broadcasted_iota(jnp.int32, (n_basin * rows, 1), 0)
    row_base = lax.shift_right_logical(row, 3) * cap + jnp.bitwise_and(row, rows - 1)
    named = (drain_at + 1).astype(jnp.float32)
    for k in range(groups):
        chosen = (row_base + k * rows) == flat_slot
        send_ref[:, k * reaches : (k + 1) * reaches] = chosen.astype(jnp.bfloat16)
        found = jnp.sum(jnp.where(chosen, named, 0.0), axis=1, keepdims=True)
        tgt_ref[:, k : k + 1] = found.astype(jnp.int32) - 1

    travel = tt_ref[...]
    weight = wx_ref[...]
    denominator = travel * (1.0 - weight) + 0.5
    coeff_first = (0.5 - travel * weight) / denominator
    coeff_second = (0.5 + travel * weight) / denominator
    recession = (travel * (1.0 - weight) - 0.5) / denominator
    coef = (coeff_first, coeff_first * recession + coeff_second, recession)

    def pack(discharge):
        for p, part in enumerate(split2(discharge)):
            for k in range(groups):
                top = (p * groups + k) * days
                spread[top : top + days, k * reaches : (k + 1) * reaches] = part
        stacked = lax.dot_general(send_ref[...], spread[...], (((1,), (1,)), ((), ())),
                                  preferred_element_type=jnp.float32)
        half = stacked.shape[1] // 2
        packed[...] = stacked[:, :half] + stacked[:, half:]

    spread[...] = jnp.zeros_like(spread)

    at_end = jnp.logical_or(o == 0, o == n_order - 1)

    @pl.when(at_end)
    def _():
        pl.semaphore_wait(barrier, n_basin)

    @pl.when(jnp.logical_not(at_end))
    def _():
        pl.semaphore_wait(barrier, 2 * n_basin)

    def target_copy(j, row, peer):
        return pltpu.make_async_remote_copy(
            src_ref=tgt_ref.at[pl.ds(j * rows, rows)],
            dst_ref=tgt_recv.at[pl.ds(row * rows, rows)],
            send_sem=tsend_sem.at[j],
            recv_sem=trecv_sem.at[row],
            device_id=(peer, j),
            device_id_type=MESH,
        )

    def data_copy(j, row, peer):
        return pltpu.make_async_remote_copy(
            src_ref=packed.at[pl.ds(j * rows, rows)],
            dst_ref=recv.at[pl.ds(row * rows, rows)],
            send_sem=send_sem.at[j],
            recv_sem=recv_sem.at[row],
            device_id=(peer, j),
            device_id_type=MESH,
        )

    @pl.when(o < n_order - 1)
    def _():
        def start(j, carry):
            target_copy(lax.rem(b + j, n_basin), b, o + 1).start()
            return carry
        lax.fori_loop(0, n_basin, start, 0)

    @pl.when(o == 0)
    def _():
        discharge = route_days(runoff_ref[...], coef)
        out_ref[...] = discharge
        pack(discharge)

    @pl.when(o > 0)
    def _():
        def got(j, carry):
            target_copy(j, j, o - 1).wait_recv()
            return carry
        lax.fori_loop(0, n_basin, got, 0)
        reach = lax.broadcasted_iota(jnp.int32, (1, reaches), 1)
        for k in range(groups):
            table_ref[:, k * reaches : (k + 1) * reaches] = (
                tgt_recv[:, k : k + 1] == reach
            ).astype(jnp.bfloat16)

        def arrived(j, carry):
            data_copy(j, j, o - 1).wait_recv()
            return carry
        lax.fori_loop(0, n_basin, arrived, 0)
        arrive = None
        for k in range(groups):
            block = jnp.concatenate(split2(recv[:, k * days : (k + 1) * days]), axis=1)
            term = lax.dot_general(block, table_ref[:, k * reaches : (k + 1) * reaches],
                                   (((0,), (0,)), ((), ())), preferred_element_type=jnp.float32)
            term = term[:days] + term[days:]
            arrive = term if arrive is None else arrive + term
        discharge = route_days(runoff_ref[...] + arrive, coef)
        out_ref[...] = discharge

        @pl.when(o < n_order - 1)
        def _():
            pack(discharge)

    @pl.when(o < n_order - 1)
    def _():
        def start(j, carry):
            data_copy(lax.rem(b + j, n_basin), b, o + 1).start()
            return carry
        lax.fori_loop(0, n_basin, start, 0)

        def finish(j, carry):
            data_copy(j, b, o + 1).wait_send()
            target_copy(j, b, o + 1).wait_send()
            return carry
        lax.fori_loop(0, n_basin, finish, 0)


def river_kernel(block, n_order, n_basin, cap, forc_ref, w_in_ref, w_rec_ref, bias_ref, w_ro_ref,
                 tt_ref, wx_ref, db_ref, dr_ref, out_ref, h_scr, c_scr, run_scr, runoff_ref, *rest):
    def lstm():
        lstm_kernel(block, forc_ref, w_in_ref, w_rec_ref, bias_ref, w_ro_ref, runoff_ref,
                    h_scr, c_scr, run_scr)

    chain_kernel(n_order, n_basin, cap, runoff_ref, tt_ref, wx_ref, db_ref, dr_ref, out_ref, *rest,
                 before=lstm)


def river(forcings, w_input, w_recur, gate_bias, w_runoff, travel_time, weight_x, drain_basin,
          drain_reach, n_order, n_basin, cap, block=128):
    days, _, reaches = forcings.shape
    units = w_recur.shape[1]
    groups = cap // 8
    vmem = pl.BlockSpec(memory_space=pltpu.VMEM)
    return pl.pallas_call(
        functools.partial(river_kernel, block, n_order, n_basin, cap),
        out_shape=jax.ShapeDtypeStruct((days, reaches), jnp.float32),
        in_specs=[vmem] * 9,
        out_specs=vmem,
        scratch_shapes=[
            pltpu.VMEM((units, reaches), jnp.bfloat16),
            pltpu.VMEM((units, reaches), jnp.float32),
            pltpu.VMEM((days, 1, reaches), jnp.float32),
            pltpu.VMEM((days, reaches), jnp.float32),
            pltpu.VMEM((n_basin * 8, groups * days), jnp.float32),
            pltpu.VMEM((n_basin * 8, groups * days), jnp.float32),
            pltpu.VMEM((n_basin * 8, groups * reaches), jnp.bfloat16),
            pltpu.VMEM((n_basin * 8, groups), jnp.int32),
            pltpu.VMEM((2 * groups * days, groups * reaches), jnp.bfloat16),
            pltpu.VMEM((n_basin * 8, groups * reaches), jnp.bfloat16),
            pltpu.VMEM((n_basin * 8, groups), jnp.int32),
            pltpu.SemaphoreType.DMA((n_basin,)),
            pltpu.SemaphoreType.DMA((n_basin,)),
            pltpu.SemaphoreType.DMA((n_basin,)),
            pltpu.SemaphoreType.DMA((n_basin,)),
        ],
        compiler_params=pltpu.CompilerParams(collective_id=0, has_side_effects=True),
    )(forcings, w_input.T, w_recur, gate_bias.reshape(1, -1), w_runoff.reshape(1, -1),
      travel_time.reshape(1, reaches), weight_x.reshape(1, reaches),
      drain_basin.reshape(1, reaches), drain_reach.reshape(1, reaches))


def per_device(
    forcings, w_input, w_recur, gate_bias, w_runoff, travel_time, weight_x, drain_basin, drain_reach
):
    basins = lax.axis_size("basin")
    groups = lax.axis_size("order")
    reach_count = forcings.shape[2]
    capacity = 2 * reach_count // basins
    return river(forcings, w_input, w_recur, gate_bias, w_runoff, travel_time, weight_x,
                 drain_basin, drain_reach, groups, basins, capacity)


def solution(mesh):
    return jax.shard_map(
        per_device,
        mesh=mesh,
        in_specs=(
            P(None, None, ("order", "basin")),
            P(),
            P(),
            P(),
            P(),
            P(("order", "basin")),
            P(("order", "basin")),
            P(("order", "basin"), None),
            P(("order", "basin"), None),
        ),
        out_specs=P(None, ("order", "basin")),
        check_vma=False,
    )
```

```python
import functools

import jax
import jax.numpy as jnp
from jax import lax
from jax.experimental import pallas as pl
from jax.experimental.pallas import tpu as pltpu
from jax.sharding import PartitionSpec as P

MESH = pl.DeviceIdType.MESH


def lstm_days(lstm_state, day_block, w_input, w_recur, gate_bias, w_runoff):
    units = w_recur.shape[1]

    def one_day(recurrent, inputs):
        hidden, memory = recurrent
        gate_sums = (
            jnp.dot(w_input, inputs, preferred_element_type=jnp.float32)
            + jnp.dot(w_recur, hidden, preferred_element_type=jnp.float32)
            + gate_bias[:, None]
        )
        ingate = jax.nn.sigmoid(gate_sums[:units])
        forget = jax.nn.sigmoid(gate_sums[units : 2 * units])
        candidate = jnp.tanh(gate_sums[2 * units : 3 * units])
        outgate = jax.nn.sigmoid(gate_sums[3 * units :])
        memory = forget * memory + ingate * candidate
        hidden = (outgate * jnp.tanh(memory)).astype(jnp.bfloat16)
        runoff = jax.nn.softplus(
            jnp.dot(w_runoff, hidden.astype(jnp.float32), precision=lax.Precision.HIGHEST)
        )
        return ((hidden, memory), runoff)

    return lax.scan(one_day, lstm_state, day_block)


def half_tanh_sigmoid(x):
    return 0.5 + 0.5 * jnp.tanh(0.5 * x)


def as_columns(row, width):
    hi = row.astype(jnp.bfloat16).astype(jnp.float32)
    mid = (row - hi).astype(jnp.bfloat16).astype(jnp.float32)
    lo = (row - hi - mid).astype(jnp.bfloat16).astype(jnp.float32)
    parts = jnp.concatenate([hi, mid, lo, jnp.zeros((5, row.shape[1]), jnp.float32)], axis=0)
    ones = (lax.broadcasted_iota(jnp.int32, (8, width), 0) < 3).astype(jnp.bfloat16)
    return lax.dot_general(parts.astype(jnp.bfloat16), ones, (((0,), (0,)), ((), ())),
                           preferred_element_type=jnp.float32)


def lstm_kernel(block, forc_ref, w_in_ref, w_rec_ref, bias_ref, w_ro_ref, out_ref, h_scr, c_scr, run_scr):
    days = forc_ref.shape[0]
    units = w_rec_ref.shape[1]
    reaches = out_ref.shape[1]
    h_scr[...] = jnp.zeros_like(h_scr)
    c_scr[...] = jnp.zeros_like(c_scr)
    bias = as_columns(bias_ref[...], block)
    w_ro = as_columns(w_ro_ref[...], block)

    def step(t, cols):
        gates = (
            lax.dot_general(w_in_ref[...], forc_ref[t, :, cols], (((0,), (0,)), ((), ())),
                            preferred_element_type=jnp.float32)
            + jnp.dot(w_rec_ref[...], h_scr[:, cols], preferred_element_type=jnp.float32)
            + bias
        )
        ingate = half_tanh_sigmoid(gates[:units])
        forget = half_tanh_sigmoid(gates[units : 2 * units])
        candidate = jnp.tanh(gates[2 * units : 3 * units])
        outgate = half_tanh_sigmoid(gates[3 * units :])
        memory = forget * c_scr[:, cols] + ingate * candidate
        hidden = (outgate * jnp.tanh(memory)).astype(jnp.bfloat16)
        c_scr[:, cols] = memory
        h_scr[:, cols] = hidden
        z = jnp.sum(w_ro * hidden.astype(jnp.float32), axis=0, keepdims=True)
        return jnp.maximum(z, 0.0) + jnp.log1p(jnp.exp(-jnp.abs(z)))

    def day(t, carry):
        for j in range(reaches // block):
            cols = pl.ds(j * block, block)
            run_scr[t, :, cols] = step(t, cols)
        return carry

    lax.fori_loop(0, days, day, 0)
    for t in range(days):
        out_ref[t : t + 1, :] = run_scr[t]


def split2(x):
    hi = x.astype(jnp.bfloat16)
    lo = (x - hi.astype(jnp.float32)).astype(jnp.bfloat16)
    return hi, lo


def route_days(inflow, coef):
    days = inflow.shape[0]
    c0, gain, c2 = coef
    day = lax.broadcasted_iota(jnp.int32, inflow.shape, 0)
    lagged = jnp.where(day >= 1, pltpu.roll(inflow, shift=1, axis=0), 0.0)
    power = c2
    step = 1
    while step < days:
        moved = jnp.where(day >= step, pltpu.roll(lagged, shift=step, axis=0), 0.0)
        lagged = lagged + power * moved
        power = power * power
        step *= 2
    return c0 * inflow + gain * lagged


def chain_kernel(n_order, n_basin, cap, runoff_ref, tt_ref, wx_ref, db_ref, dr_ref, out_ref,
                 packed, recv, table_ref, tgt_recv, spread, send_ref, tgt_ref,
                 send_sem, recv_sem, tsend_sem, trecv_sem, before=None):
    o = lax.axis_index("order")
    b = lax.axis_index("basin")
    days, reaches = runoff_ref.shape
    groups = cap // 8
    rows = 8

    barrier = pltpu.get_barrier_semaphore()

    def greet(row):
        def body(j, carry):
            pl.semaphore_signal(barrier, inc=1, device_id=(row, j), device_id_type=MESH)
            return carry
        lax.fori_loop(0, n_basin, body, 0)

    @pl.when(o > 0)
    def _():
        greet(o - 1)

    @pl.when(o < n_order - 1)
    def _():
        greet(o + 1)

    if before is not None:
        before()
    drain_to = db_ref[...]
    drain_at = dr_ref[...]
    onehot = (lax.broadcasted_iota(jnp.int32, (n_basin, reaches), 0) == drain_to).astype(jnp.bfloat16)
    earlier = (
        lax.broadcasted_iota(jnp.int32, (reaches, reaches), 0)
        < lax.broadcasted_iota(jnp.int32, (reaches, reaches), 1)
    ).astype(jnp.bfloat16)
    counts = jnp.dot(onehot, earlier, preferred_element_type=jnp.float32)
    slot_index = jnp.sum(counts * onehot.astype(jnp.float32), axis=0, keepdims=True)
    flat_slot = drain_to * cap + slot_index.astype(jnp.int32)
    row = lax.broadcasted_iota(jnp.int32, (n_basin * rows, 1), 0)
    row_base = lax.shift_right_logical(row, 3) * cap + jnp.bitwise_and(row, rows - 1)
    named = (drain_at + 1).astype(jnp.float32)
    for k in range(groups):
        chosen = (row_base + k * rows) == flat_slot
        send_ref[:, k * reaches : (k + 1) * reaches] = chosen.astype(jnp.bfloat16)
        found = jnp.sum(jnp.where(chosen, named, 0.0), axis=1, keepdims=True)
        tgt_ref[:, k : k + 1] = found.astype(jnp.int32) - 1

    travel = tt_ref[...]
    weight = wx_ref[...]
    denominator = travel * (1.0 - weight) + 0.5
    coeff_first = (0.5 - travel * weight) / denominator
    coeff_second = (0.5 + travel * weight) / denominator
    recession = (travel * (1.0 - weight) - 0.5) / denominator
    coef = (coeff_first, coeff_first * recession + coeff_second, recession)

    def pack(discharge):
        for p, part in enumerate(split2(discharge)):
            for k in range(groups):
                top = (p * groups + k) * days
                spread[top : top + days, k * reaches : (k + 1) * reaches] = part
        stacked = lax.dot_general(send_ref[...], spread[...], (((1,), (1,)), ((), ())),
                                  preferred_element_type=jnp.float32)
        half = stacked.shape[1] // 2
        packed[...] = stacked[:, :half] + stacked[:, half:]

    spread[...] = jnp.zeros_like(spread)

    at_end = jnp.logical_or(o == 0, o == n_order - 1)

    @pl.when(at_end)
    def _():
        pl.semaphore_wait(barrier, n_basin)

    @pl.when(jnp.logical_not(at_end))
    def _():
        pl.semaphore_wait(barrier, 2 * n_basin)

    def target_copy(j, row, peer):
        return pltpu.make_async_remote_copy(
            src_ref=tgt_ref.at[pl.ds(j * rows, rows)],
            dst_ref=tgt_recv.at[pl.ds(row * rows, rows)],
            send_sem=tsend_sem.at[j],
            recv_sem=trecv_sem.at[row],
            device_id=(peer, j),
            device_id_type=MESH,
        )

    def data_copy(j, row, peer):
        return pltpu.make_async_remote_copy(
            src_ref=packed.at[pl.ds(j * rows, rows)],
            dst_ref=recv.at[pl.ds(row * rows, rows)],
            send_sem=send_sem.at[j],
            recv_sem=recv_sem.at[row],
            device_id=(peer, j),
            device_id_type=MESH,
        )

    @pl.when(o < n_order - 1)
    def _():
        def start(j, carry):
            target_copy(lax.rem(b + n_basin // 2 + j, n_basin), b, o + 1).start()
            return carry
        lax.fori_loop(0, n_basin, start, 0)

    @pl.when(o == 0)
    def _():
        discharge = route_days(runoff_ref[...], coef)
        out_ref[...] = discharge
        pack(discharge)

    @pl.when(o > 0)
    def _():
        def got(j, carry):
            target_copy(j, j, o - 1).wait_recv()
            return carry
        lax.fori_loop(0, n_basin, got, 0)
        reach = lax.broadcasted_iota(jnp.int32, (1, reaches), 1)
        for k in range(groups):
            table_ref[:, k * reaches : (k + 1) * reaches] = (
                tgt_recv[:, k : k + 1] == reach
            ).astype(jnp.bfloat16)

        def arrived(j, carry):
            data_copy(j, j, o - 1).wait_recv()
            return carry
        lax.fori_loop(0, n_basin, arrived, 0)
        arrive = None
        for k in range(groups):
            block = jnp.concatenate(split2(recv[:, k * days : (k + 1) * days]), axis=1)
            term = lax.dot_general(block, table_ref[:, k * reaches : (k + 1) * reaches],
                                   (((0,), (0,)), ((), ())), preferred_element_type=jnp.float32)
            term = term[:days] + term[days:]
            arrive = term if arrive is None else arrive + term
        discharge = route_days(runoff_ref[...] + arrive, coef)
        out_ref[...] = discharge

        @pl.when(o < n_order - 1)
        def _():
            pack(discharge)

    @pl.when(o < n_order - 1)
    def _():
        def start(j, carry):
            data_copy(lax.rem(b + n_basin // 2 + j, n_basin), b, o + 1).start()
            return carry
        lax.fori_loop(0, n_basin, start, 0)

        def finish(j, carry):
            data_copy(j, b, o + 1).wait_send()
            target_copy(j, b, o + 1).wait_send()
            return carry
        lax.fori_loop(0, n_basin, finish, 0)


def river_kernel(block, n_order, n_basin, cap, forc_ref, w_in_ref, w_rec_ref, bias_ref, w_ro_ref,
                 tt_ref, wx_ref, db_ref, dr_ref, out_ref, h_scr, c_scr, run_scr, runoff_ref, *rest):
    def lstm():
        lstm_kernel(block, forc_ref, w_in_ref, w_rec_ref, bias_ref, w_ro_ref, runoff_ref,
                    h_scr, c_scr, run_scr)

    chain_kernel(n_order, n_basin, cap, runoff_ref, tt_ref, wx_ref, db_ref, dr_ref, out_ref, *rest,
                 before=lstm)


def river(forcings, w_input, w_recur, gate_bias, w_runoff, travel_time, weight_x, drain_basin,
          drain_reach, n_order, n_basin, cap, block=128):
    days, _, reaches = forcings.shape
    units = w_recur.shape[1]
    groups = cap // 8
    vmem = pl.BlockSpec(memory_space=pltpu.VMEM)
    return pl.pallas_call(
        functools.partial(river_kernel, block, n_order, n_basin, cap),
        out_shape=jax.ShapeDtypeStruct((days, reaches), jnp.float32),
        in_specs=[vmem] * 9,
        out_specs=vmem,
        scratch_shapes=[
            pltpu.VMEM((units, reaches), jnp.bfloat16),
            pltpu.VMEM((units, reaches), jnp.float32),
            pltpu.VMEM((days, 1, reaches), jnp.float32),
            pltpu.VMEM((days, reaches), jnp.float32),
            pltpu.VMEM((n_basin * 8, groups * days), jnp.float32),
            pltpu.VMEM((n_basin * 8, groups * days), jnp.float32),
            pltpu.VMEM((n_basin * 8, groups * reaches), jnp.bfloat16),
            pltpu.VMEM((n_basin * 8, groups), jnp.int32),
            pltpu.VMEM((2 * groups * days, groups * reaches), jnp.bfloat16),
            pltpu.VMEM((n_basin * 8, groups * reaches), jnp.bfloat16),
            pltpu.VMEM((n_basin * 8, groups), jnp.int32),
            pltpu.SemaphoreType.DMA((n_basin,)),
            pltpu.SemaphoreType.DMA((n_basin,)),
            pltpu.SemaphoreType.DMA((n_basin,)),
            pltpu.SemaphoreType.DMA((n_basin,)),
        ],
        compiler_params=pltpu.CompilerParams(collective_id=0, has_side_effects=True),
    )(forcings, w_input.T, w_recur, gate_bias.reshape(1, -1), w_runoff.reshape(1, -1),
      travel_time.reshape(1, reaches), weight_x.reshape(1, reaches),
      drain_basin.reshape(1, reaches), drain_reach.reshape(1, reaches))


def per_device(
    forcings, w_input, w_recur, gate_bias, w_runoff, travel_time, weight_x, drain_basin, drain_reach
):
    basins = lax.axis_size("basin")
    groups = lax.axis_size("order")
    reach_count = forcings.shape[2]
    capacity = 2 * reach_count // basins
    return river(forcings, w_input, w_recur, gate_bias, w_runoff, travel_time, weight_x,
                 drain_basin, drain_reach, groups, basins, capacity)


def solution(mesh):
    return jax.shard_map(
        per_device,
        mesh=mesh,
        in_specs=(
            P(None, None, ("order", "basin")),
            P(),
            P(),
            P(),
            P(),
            P(("order", "basin")),
            P(("order", "basin")),
            P(("order", "basin"), None),
            P(("order", "basin"), None),
        ),
        out_specs=P(None, ("order", "basin")),
        check_vma=False,
    )
```

```python
import functools

import jax
import jax.numpy as jnp
from jax import lax
from jax.experimental import pallas as pl
from jax.experimental.pallas import tpu as pltpu
from jax.sharding import PartitionSpec as P

MESH = pl.DeviceIdType.MESH


def lstm_days(lstm_state, day_block, w_input, w_recur, gate_bias, w_runoff):
    units = w_recur.shape[1]

    def one_day(recurrent, inputs):
        hidden, memory = recurrent
        gate_sums = (
            jnp.dot(w_input, inputs, preferred_element_type=jnp.float32)
            + jnp.dot(w_recur, hidden, preferred_element_type=jnp.float32)
            + gate_bias[:, None]
        )
        ingate = jax.nn.sigmoid(gate_sums[:units])
        forget = jax.nn.sigmoid(gate_sums[units : 2 * units])
        candidate = jnp.tanh(gate_sums[2 * units : 3 * units])
        outgate = jax.nn.sigmoid(gate_sums[3 * units :])
        memory = forget * memory + ingate * candidate
        hidden = (outgate * jnp.tanh(memory)).astype(jnp.bfloat16)
        runoff = jax.nn.softplus(
            jnp.dot(w_runoff, hidden.astype(jnp.float32), precision=lax.Precision.HIGHEST)
        )
        return ((hidden, memory), runoff)

    return lax.scan(one_day, lstm_state, day_block)


def half_tanh_sigmoid(x):
    return 0.5 + 0.5 * jnp.tanh(0.5 * x)


def as_columns(row, width):
    hi = row.astype(jnp.bfloat16).astype(jnp.float32)
    mid = (row - hi).astype(jnp.bfloat16).astype(jnp.float32)
    lo = (row - hi - mid).astype(jnp.bfloat16).astype(jnp.float32)
    parts = jnp.concatenate([hi, mid, lo, jnp.zeros((5, row.shape[1]), jnp.float32)], axis=0)
    ones = (lax.broadcasted_iota(jnp.int32, (8, width), 0) < 3).astype(jnp.bfloat16)
    return lax.dot_general(parts.astype(jnp.bfloat16), ones, (((0,), (0,)), ((), ())),
                           preferred_element_type=jnp.float32)


def lstm_kernel(block, forc_ref, w_in_ref, w_rec_ref, bias_ref, w_ro_ref, out_ref, h_scr, c_scr, run_scr):
    days = forc_ref.shape[0]
    units = w_rec_ref.shape[1]
    reaches = out_ref.shape[1]
    h_scr[...] = jnp.zeros_like(h_scr)
    c_scr[...] = jnp.zeros_like(c_scr)
    bias = as_columns(bias_ref[...], block)
    w_ro = as_columns(w_ro_ref[...], block)

    def step(t, cols):
        gates = (
            lax.dot_general(w_in_ref[...], forc_ref[t, :, cols], (((0,), (0,)), ((), ())),
                            preferred_element_type=jnp.float32)
            + jnp.dot(w_rec_ref[...], h_scr[:, cols], preferred_element_type=jnp.float32)
            + bias
        )
        ingate = half_tanh_sigmoid(gates[:units])
        forget = half_tanh_sigmoid(gates[units : 2 * units])
        candidate = jnp.tanh(gates[2 * units : 3 * units])
        outgate = half_tanh_sigmoid(gates[3 * units :])
        memory = forget * c_scr[:, cols] + ingate * candidate
        hidden = (outgate * jnp.tanh(memory)).astype(jnp.bfloat16)
        c_scr[:, cols] = memory
        h_scr[:, cols] = hidden
        z = jnp.sum(w_ro * hidden.astype(jnp.float32), axis=0, keepdims=True)
        return jnp.maximum(z, 0.0) + jnp.log1p(jnp.exp(-jnp.abs(z)))

    def day(t, carry):
        for j in range(reaches // block):
            cols = pl.ds(j * block, block)
            run_scr[t, :, cols] = step(t, cols)
        return carry

    lax.fori_loop(0, days, day, 0)
    for t in range(days):
        out_ref[t : t + 1, :] = run_scr[t]


def split2(x):
    hi = x.astype(jnp.bfloat16)
    lo = (x - hi.astype(jnp.float32)).astype(jnp.bfloat16)
    return hi, lo


def route_days(inflow, coef):
    days = inflow.shape[0]
    c0, gain, c2 = coef
    day = lax.broadcasted_iota(jnp.int32, inflow.shape, 0)
    lagged = jnp.where(day >= 1, pltpu.roll(inflow, shift=1, axis=0), 0.0)
    power = c2
    step = 1
    while step < days:
        moved = jnp.where(day >= step, pltpu.roll(lagged, shift=step, axis=0), 0.0)
        lagged = lagged + power * moved
        power = power * power
        step *= 2
    return c0 * inflow + gain * lagged


def chain_kernel(n_order, n_basin, cap, runoff_ref, tt_ref, wx_ref, db_ref, dr_ref, out_ref,
                 packed, recv, table_ref, tgt_recv, spread, send_ref, tgt_ref,
                 send_sem, recv_sem, tsend_sem, trecv_sem, before=None):
    o = lax.axis_index("order")
    b = lax.axis_index("basin")
    days, reaches = runoff_ref.shape
    groups = cap // 8
    rows = 8

    barrier = pltpu.get_barrier_semaphore()

    def greet(row):
        def body(j, carry):
            pl.semaphore_signal(barrier, inc=1, device_id=(row, j), device_id_type=MESH)
            return carry
        lax.fori_loop(0, n_basin, body, 0)

    @pl.when(o > 0)
    def _():
        greet(o - 1)

    @pl.when(o < n_order - 1)
    def _():
        greet(o + 1)

    if before is not None:
        before()
    drain_to = db_ref[...]
    drain_at = dr_ref[...]
    onehot = (lax.broadcasted_iota(jnp.int32, (n_basin, reaches), 0) == drain_to).astype(jnp.bfloat16)
    earlier = (
        lax.broadcasted_iota(jnp.int32, (reaches, reaches), 0)
        < lax.broadcasted_iota(jnp.int32, (reaches, reaches), 1)
    ).astype(jnp.bfloat16)
    counts = jnp.dot(onehot, earlier, preferred_element_type=jnp.float32)
    slot_index = jnp.sum(counts * onehot.astype(jnp.float32), axis=0, keepdims=True)
    flat_slot = drain_to * cap + slot_index.astype(jnp.int32)
    row = lax.broadcasted_iota(jnp.int32, (n_basin * rows, 1), 0)
    row_base = lax.shift_right_logical(row, 3) * cap + jnp.bitwise_and(row, rows - 1)
    named = (drain_at + 1).astype(jnp.float32)
    named_hi, named_lo = split2(named)
    named_parts = jnp.concatenate(
        [named_hi.astype(jnp.float32), named_lo.astype(jnp.float32),
         jnp.zeros((6, reaches), jnp.float32)], axis=0).astype(jnp.bfloat16)
    for k in range(groups):
        chosen = ((row_base + k * rows) == flat_slot).astype(jnp.bfloat16)
        send_ref[:, k * reaches : (k + 1) * reaches] = chosen
        picked = lax.dot_general(chosen, named_parts, (((1,), (1,)), ((), ())),
                                 preferred_element_type=jnp.float32)
        found = picked[:, 0:1] + picked[:, 1:2]
        tgt_ref[:, k : k + 1] = found.astype(jnp.int32) - 1

    travel = tt_ref[...]
    weight = wx_ref[...]
    denominator = travel * (1.0 - weight) + 0.5
    coeff_first = (0.5 - travel * weight) / denominator
    coeff_second = (0.5 + travel * weight) / denominator
    recession = (travel * (1.0 - weight) - 0.5) / denominator
    coef = (coeff_first, coeff_first * recession + coeff_second, recession)

    def pack(discharge):
        for p, part in enumerate(split2(discharge)):
            for k in range(groups):
                top = (p * groups + k) * days
                spread[top : top + days, k * reaches : (k + 1) * reaches] = part
        stacked = lax.dot_general(send_ref[...], spread[...], (((1,), (1,)), ((), ())),
                                  preferred_element_type=jnp.float32)
        half = stacked.shape[1] // 2
        packed[...] = stacked[:, :half] + stacked[:, half:]

    spread[...] = jnp.zeros_like(spread)

    at_end = jnp.logical_or(o == 0, o == n_order - 1)

    @pl.when(at_end)
    def _():
        pl.semaphore_wait(barrier, n_basin)

    @pl.when(jnp.logical_not(at_end))
    def _():
        pl.semaphore_wait(barrier, 2 * n_basin)

    def target_copy(j, row, peer):
        return pltpu.make_async_remote_copy(
            src_ref=tgt_ref.at[pl.ds(j * rows, rows)],
            dst_ref=tgt_recv.at[pl.ds(row * rows, rows)],
            send_sem=tsend_sem.at[j],
            recv_sem=trecv_sem.at[row],
            device_id=(peer, j),
            device_id_type=MESH,
        )

    def data_copy(j, row, peer):
        return pltpu.make_async_remote_copy(
            src_ref=packed.at[pl.ds(j * rows, rows)],
            dst_ref=recv.at[pl.ds(row * rows, rows)],
            send_sem=send_sem.at[j],
            recv_sem=recv_sem.at[row],
            device_id=(peer, j),
            device_id_type=MESH,
        )

    @pl.when(o < n_order - 1)
    def _():
        def start(j, carry):
            target_copy(j, b, o + 1).start()
            return carry
        lax.fori_loop(0, n_basin, start, 0)

    @pl.when(o == 0)
    def _():
        discharge = route_days(runoff_ref[...], coef)
        out_ref[...] = discharge
        pack(discharge)

    @pl.when(o > 0)
    def _():
        def got(j, carry):
            target_copy(j, j, o - 1).wait_recv()
            return carry
        lax.fori_loop(0, n_basin, got, 0)
        reach = lax.broadcasted_iota(jnp.int32, (1, reaches), 1)
        for k in range(groups):
            table_ref[:, k * reaches : (k + 1) * reaches] = (
                tgt_recv[:, k : k + 1] == reach
            ).astype(jnp.bfloat16)

        def arrived(j, carry):
            data_copy(j, j, o - 1).wait_recv()
            return carry
        lax.fori_loop(0, n_basin, arrived, 0)
        arrive = None
        for k in range(groups):
            block = jnp.concatenate(split2(recv[:, k * days : (k + 1) * days]), axis=1)
            term = lax.dot_general(block, table_ref[:, k * reaches : (k + 1) * reaches],
                                   (((0,), (0,)), ((), ())), preferred_element_type=jnp.float32)
            term = term[:days] + term[days:]
            arrive = term if arrive is None else arrive + term
        discharge = route_days(runoff_ref[...] + arrive, coef)
        out_ref[...] = discharge

        @pl.when(o < n_order - 1)
        def _():
            pack(discharge)

    @pl.when(o < n_order - 1)
    def _():
        def start(j, carry):
            data_copy(j, b, o + 1).start()
            return carry
        lax.fori_loop(0, n_basin, start, 0)

        def finish(j, carry):
            data_copy(j, b, o + 1).wait_send()
            target_copy(j, b, o + 1).wait_send()
            return carry
        lax.fori_loop(0, n_basin, finish, 0)


def river_kernel(block, n_order, n_basin, cap, forc_ref, w_in_ref, w_rec_ref, bias_ref, w_ro_ref,
                 tt_ref, wx_ref, db_ref, dr_ref, out_ref, h_scr, c_scr, run_scr, runoff_ref, *rest):
    def lstm():
        lstm_kernel(block, forc_ref, w_in_ref, w_rec_ref, bias_ref, w_ro_ref, runoff_ref,
                    h_scr, c_scr, run_scr)

    chain_kernel(n_order, n_basin, cap, runoff_ref, tt_ref, wx_ref, db_ref, dr_ref, out_ref, *rest,
                 before=lstm)


def river(forcings, w_input, w_recur, gate_bias, w_runoff, travel_time, weight_x, drain_basin,
          drain_reach, n_order, n_basin, cap, block=128):
    days, _, reaches = forcings.shape
    units = w_recur.shape[1]
    groups = cap // 8
    vmem = pl.BlockSpec(memory_space=pltpu.VMEM)
    return pl.pallas_call(
        functools.partial(river_kernel, block, n_order, n_basin, cap),
        out_shape=jax.ShapeDtypeStruct((days, reaches), jnp.float32),
        in_specs=[vmem] * 9,
        out_specs=vmem,
        scratch_shapes=[
            pltpu.VMEM((units, reaches), jnp.bfloat16),
            pltpu.VMEM((units, reaches), jnp.float32),
            pltpu.VMEM((days, 1, reaches), jnp.float32),
            pltpu.VMEM((days, reaches), jnp.float32),
            pltpu.VMEM((n_basin * 8, groups * days), jnp.float32),
            pltpu.VMEM((n_basin * 8, groups * days), jnp.float32),
            pltpu.VMEM((n_basin * 8, groups * reaches), jnp.bfloat16),
            pltpu.VMEM((n_basin * 8, groups), jnp.int32),
            pltpu.VMEM((2 * groups * days, groups * reaches), jnp.bfloat16),
            pltpu.VMEM((n_basin * 8, groups * reaches), jnp.bfloat16),
            pltpu.VMEM((n_basin * 8, groups), jnp.int32),
            pltpu.SemaphoreType.DMA((n_basin,)),
            pltpu.SemaphoreType.DMA((n_basin,)),
            pltpu.SemaphoreType.DMA((n_basin,)),
            pltpu.SemaphoreType.DMA((n_basin,)),
        ],
        compiler_params=pltpu.CompilerParams(collective_id=0, has_side_effects=True),
    )(forcings, w_input.T, w_recur, gate_bias.reshape(1, -1), w_runoff.reshape(1, -1),
      travel_time.reshape(1, reaches), weight_x.reshape(1, reaches),
      drain_basin.reshape(1, reaches), drain_reach.reshape(1, reaches))


def per_device(
    forcings, w_input, w_recur, gate_bias, w_runoff, travel_time, weight_x, drain_basin, drain_reach
):
    basins = lax.axis_size("basin")
    groups = lax.axis_size("order")
    reach_count = forcings.shape[2]
    capacity = 2 * reach_count // basins
    return river(forcings, w_input, w_recur, gate_bias, w_runoff, travel_time, weight_x,
                 drain_basin, drain_reach, groups, basins, capacity)


def solution(mesh):
    return jax.shard_map(
        per_device,
        mesh=mesh,
        in_specs=(
            P(None, None, ("order", "basin")),
            P(),
            P(),
            P(),
            P(),
            P(("order", "basin")),
            P(("order", "basin")),
            P(("order", "basin"), None),
            P(("order", "basin"), None),
        ),
        out_specs=P(None, ("order", "basin")),
        check_vma=False,
    )
```
